32 devices in a mesh: px: 4 (over z), py: 8 (over y, x, core).
Axes of the slice: x: 2, y: 2, z: 4, core: 2. Of those that a mesh axis runs over, the one named last changes fastest.
Arguments:
- wind_east: bfloat16 [64, 128, 256], P('px', 'py'), may hold values from -4 to 4
- wind_north: bfloat16 [64, 128, 256], P('px', 'py'), may hold values from -4 to 4
- wind_up: bfloat16 [64, 128, 256], P('px', 'py'), may hold values from -4 to 4
Outputs:
- pressure: float32 [64, 128, 256], P('px', 'py')
The draws below stay inside these ranges and needn't reach their ends.
All inputs are finite; a program needn't handle non-finite values.
Results may differ from the reference program's by a relative error of at most 0.0003.
Values may be sent and summed in bfloat16 or wider, within the bound.
No kernel may reach another device: no remote copies, remote signals or barrier semaphores. Data moves between devices by JAX's collectives and lax.ppermute only.
A program may use at most 64 MiB of HBM per device.

```python
import math
import jax
import jax.numpy as jnp
from jax import lax

NZ = 256
NX = 64
NY = 128
N_PX = 4


def wind_field(key, component):
    stream = jax.random.fold_in(key, component)
    values = jax.random.normal(stream, (NX, NY, NZ), jnp.float32)
    return jnp.clip(values, -4.0, 4.0).astype(jnp.bfloat16)


def draw_wind_east(key, part):
    return wind_field(key, 1)


def draw_wind_north(key, part):
    return wind_field(key, 2)


def draw_wind_up(key, part):
    return wind_field(key, 3)


def setup_inputs(seed: int = 0) -> dict:
    key_list = jax.random.split(jax.random.key(seed), 4)
    return {
        "wind_east": draw_wind_east(jax.random.fold_in(key_list[3], 71), 0),
        "wind_north": draw_wind_north(jax.random.fold_in(key_list[3], 71), 0),
        "wind_up": draw_wind_up(jax.random.fold_in(key_list[3], 71), 0),
    }


NU_BASE = 0.01
SMAGORINSKY = 0.16
STRAIN_FLOOR = 1.0
TIME_STEP = 0.25

def neighbour(values, dimension, offset):
    starts = [1, 1, 1]
    limits = [values.shape[0] - 1, values.shape[1] - 1, values.shape[2] - 1]
    starts[dimension] = starts[dimension] + offset
    limits[dimension] = limits[dimension] + offset
    return lax.slice(values, tuple(starts), tuple(limits))

def derivative(values, dimension):
    return 0.5 * (neighbour(values, dimension, 1) - neighbour(values, dimension, -1))

def divergence_source(wind_fields):
    centre = [neighbour(values, 0, 0) for values in wind_fields]
    gradient = [[derivative(wind_fields[component], dimension) for dimension in range(3)] for component in range(3)]
    strain = jnp.zeros_like(centre[0])
    for first_dim in range(3):
        for second_dim in range(3):
            paired = 0.5 * (gradient[second_dim][first_dim] + gradient[first_dim][second_dim])
            strain = strain + paired * paired
    viscosity = NU_BASE + SMAGORINSKY * jnp.sqrt(2.0 * strain + STRAIN_FLOOR)
    middle = neighbour(viscosity, 0, 0)
    provisional = []
    for component in range(3):
        current = neighbour(centre[component], 0, 0)
        advection = jnp.zeros_like(current)
        diffusion = jnp.zeros_like(current)
        for dimension in range(3):
            advection = advection - neighbour(centre[dimension], 0, 0) * neighbour(gradient[component][dimension], 0, 0)
            upper_flux = 0.5 * (neighbour(viscosity, dimension, 1) + middle) * (neighbour(centre[component], dimension, 1) - current)
            lower_flux = 0.5 * (middle + neighbour(viscosity, dimension, -1)) * (current - neighbour(centre[component], dimension, -1))
            diffusion = diffusion + upper_flux - lower_flux
        provisional.append(current + TIME_STEP * (advection + diffusion))
    return derivative(provisional[0], 0) + derivative(provisional[1], 1) + derivative(provisional[2], 2)

def cosine_basis(levels):
    level_index = lax.broadcasted_iota(jnp.int32, (levels, levels), 0)
    mode_index = lax.broadcasted_iota(jnp.int32, (levels, levels), 1)
    phase_count = (2 * level_index + 1) * mode_index % (4 * levels)
    radians = math.pi / (2.0 * levels) * phase_count.astype(jnp.float32)
    weight = jnp.where(mode_index == 0, math.sqrt(1.0 / levels), math.sqrt(2.0 / levels))
    return weight * jnp.cos(radians)

def reference(wind_east, wind_north, wind_up):

    def extend(values):
        rimmed = jnp.pad(values, ((3, 3), (3, 3), (0, 0)), mode='wrap')
        return jnp.pad(rimmed, ((0, 0), (0, 0), (3, 3)))
    extended = [extend(values) for values in (wind_east, wind_north, wind_up)]
    block_rows = NX // N_PX
    basis = cosine_basis(NZ)

    def one_block(block):
        start = (block * block_rows).astype(jnp.int32)
        zero_index = jnp.zeros((), jnp.int32)
        pieces = [lax.dynamic_slice(values, (start, zero_index, zero_index), (block_rows + 6, NY + 6, NZ + 6)).astype(jnp.float32) for values in extended]
        source = divergence_source(pieces)
        flat = jnp.dot(source.reshape(block_rows * NY, NZ), basis, precision=lax.Precision.HIGHEST, preferred_element_type=jnp.float32)
        return flat.reshape(block_rows, NY, NZ)
    modes = lax.map(one_block, jnp.arange(N_PX, dtype=jnp.int32)).reshape(NX, NY, NZ)
    wave_east = jnp.arange(NX, dtype=jnp.int32)
    wave_north = jnp.arange(NY, dtype=jnp.int32)
    eigen_east = 4.0 * jnp.sin(math.pi / NX * wave_east.astype(jnp.float32)) ** 2
    eigen_north = 4.0 * jnp.sin(math.pi / NY * wave_north.astype(jnp.float32)) ** 2

    def one_level(level):
        plane = lax.dynamic_index_in_dim(modes, level, axis=2, keepdims=False)
        spectrum = jnp.fft.fft2(plane)
        eigen_up = 4.0 * jnp.sin(math.pi / (2.0 * NZ) * level.astype(jnp.float32)) ** 2
        eigen = eigen_east[:, None] + eigen_north[None, :] + eigen_up
        empty = (wave_east[:, None] == 0) & (wave_north[None, :] == 0) & (level == 0)
        factor = jnp.where(empty, 0.0, -1.0 / jnp.where(empty, 1.0, eigen))
        return jnp.real(jnp.fft.ifft2(spectrum * factor)).astype(jnp.float32)
    solved = lax.map(one_level, jnp.arange(NZ, dtype=jnp.int32))
    return jnp.einsum('mxy,zm->xyz', solved, basis, precision=lax.Precision.HIGHEST, preferred_element_type=jnp.float32)
```

```python
import functools
import math

import jax
import jax.numpy as jnp
import numpy as np
from jax import lax
from jax.experimental import pallas as pl
from jax.experimental.pallas import tpu as pltpu
from jax.sharding import PartitionSpec as P

NU_BASE = 0.01
SMAGORINSKY = 0.16
STRAIN_FLOOR = 1.0
TIME_STEP = 0.25
HALO = 3
F32 = jnp.float32


def cosine_basis(levels):
    level = np.arange(levels, dtype=np.int64)[:, None]
    mode = np.arange(levels, dtype=np.int64)[None, :]
    radians = math.pi / (2.0 * levels) * ((2 * level + 1) * mode % (4 * levels))
    weight = np.where(mode == 0, math.sqrt(1.0 / levels), math.sqrt(2.0 / levels))
    return (weight * np.cos(radians)).astype(np.float32)


def fourier_basis(length):
    cell = np.arange(length)
    half = length // 2
    columns = [np.full(length, math.sqrt(1.0 / length))]
    waves = [0]
    for wave in range(1, half):
        angle = 2.0 * math.pi * (cell * wave % length) / length
        columns += [math.sqrt(2.0 / length) * np.cos(angle), math.sqrt(2.0 / length) * np.sin(angle)]
        waves += [wave, wave]
    columns.append(math.sqrt(1.0 / length) * (1.0 - 2.0 * (cell % 2)))
    waves.append(half)
    eigen = 4.0 * np.sin(math.pi / length * np.array(waves)) ** 2
    return np.stack(columns, axis=1).astype(np.float32), eigen.astype(np.float32)


def mode_eigen(levels):
    return (4.0 * np.sin(math.pi / (2.0 * levels) * np.arange(levels)) ** 2).astype(np.float32)


def high_dot(left, right, contract):
    return lax.dot_general(
        left, right, (contract, ((), ())), precision=lax.Precision.HIGHEST, preferred_element_type=F32
    )


def with_halo(stacked):
    width = HALO
    pad = -(stacked.shape[2] + 2 * width) % 8
    for axis, dim in (("py", 2), ("px", 1)):
        size, length = lax.axis_size(axis), stacked.shape[dim]
        up = [(i, (i + 1) % size) for i in range(size)]
        down = [(j, i) for i, j in up]
        last = lax.slice_in_dim(stacked, length - width, length, axis=dim)
        leading = lax.slice_in_dim(stacked, 0, width, axis=dim)
        before = lax.ppermute(last, axis, up)
        after = lax.ppermute(leading, axis, down)
        if dim == 2:
            shape = list(stacked.shape)
            shape[2] = pad
            pieces = [stacked, after, jnp.zeros(shape, stacked.dtype), before]
        else:
            pieces = [before, stacked, after]
        stacked = jnp.concatenate(pieces, axis=dim)
    return stacked


def source_kernel(cells_x, cells_y, rim_ref, basis_ref, out_ref, wind, visc, east, part, source):
    rows = wind.shape[2]
    levels = wind.shape[3]
    planes = cells_x + 2 * HALO
    lane = lax.broadcasted_iota(jnp.int32, (rows, levels), 1)
    bottom = lane == 0
    top = lane == levels - 1

    def y_next(values):
        return pltpu.roll(values, rows - 1, 0)

    def y_prev(values):
        return pltpu.roll(values, 1, 0)

    def z_next(values, edge=0.0):
        return jnp.where(top, edge, pltpu.roll(values, levels - 1, 1))

    def z_prev(values, edge=0.0):
        return jnp.where(bottom, edge, pltpu.roll(values, 1, 1))

    def eddy(total):
        return NU_BASE + SMAGORINSKY * jnp.sqrt(total + STRAIN_FLOOR)

    def load(x, carry):
        for c in range(3):
            wind[c, x] = rim_ref[c, x].astype(F32)
        return carry

    lax.fori_loop(0, planes, load, 0)

    def viscosity(x, carry):
        centre = [wind[c, x] for c in range(3)]
        along_x = [wind[c, x + 1] - wind[c, x - 1] for c in range(3)]
        along_y = [y_next(u) - y_prev(u) for u in centre]
        along_z = [z_next(u) - z_prev(u) for u in centre]
        normal = along_x[0] * along_x[0] + along_y[1] * along_y[1] + along_z[2] * along_z[2]
        xy = along_x[1] + along_y[0]
        xz = along_x[2] + along_z[0]
        yz = along_y[2] + along_z[1]
        visc[x] = eddy(0.5 * normal + 0.25 * (xy * xy + xz * xz + yz * yz))
        return carry

    lax.fori_loop(1, planes - 1, viscosity, 0)

    def provisional(x, carry):
        centre = [wind[c, x] for c in range(3)]
        nu = visc[x]
        beyond = eddy(
            0.5 * centre[2] * centre[2] + 0.25 * (centre[0] * centre[0] + centre[1] * centre[1])
        )
        sum_xn = nu + visc[x + 1]
        sum_xp = nu + visc[x - 1]
        sum_yn = nu + y_next(nu)
        sum_yp = nu + y_prev(nu)
        sum_zn = nu + z_next(nu, beyond)
        sum_zp = nu + z_prev(nu, beyond)
        whole = (sum_xn + sum_xp) + (sum_yn + sum_yp) + (sum_zn + sum_zp)
        coef = (
            sum_xn - centre[0],
            sum_xp + centre[0],
            sum_yn - centre[1],
            sum_yp + centre[1],
            sum_zn - centre[2],
            sum_zp + centre[2],
        )

        def one(c):
            u = centre[c]
            total = coef[0] * wind[c, x + 1] + coef[1] * wind[c, x - 1]
            total = total + coef[2] * y_next(u) + coef[3] * y_prev(u)
            total = total + coef[4] * z_next(u) + coef[5] * z_prev(u)
            return u + (0.5 * TIME_STEP) * (total - whole * u)

        east[x] = one(0)
        north = one(1)
        up = one(2)
        up_edge_top = (0.5 * TIME_STEP) * (sum_zn * centre[2])
        up_edge_bottom = (0.5 * TIME_STEP) * (sum_zp * centre[2])
        part[x] = (y_next(north) - y_prev(north)) + (
            z_next(up, up_edge_top) - z_prev(up, up_edge_bottom)
        )
        return carry

    lax.fori_loop(2, planes - 2, provisional, 0)

    def collect(x, carry):
        value = 0.5 * (part[x] + (east[x + 1] - east[x - 1]))
        source[x - HALO] = value[:cells_y]
        return carry

    lax.fori_loop(HALO, planes - HALO, collect, 0)
    flat = source[...].reshape(cells_x * cells_y, levels)
    out_ref[...] = high_dot(basis_ref[...], flat, ((1,), (1,)))


def source_modes(rim, basis_rows, cells_x, cells_y):
    planes, rows, levels = rim.shape[1:]
    return pl.pallas_call(
        functools.partial(source_kernel, cells_x, cells_y),
        out_shape=jax.ShapeDtypeStruct((levels, cells_x * cells_y), F32),
        in_specs=[pl.BlockSpec(memory_space=pltpu.VMEM)] * 2,
        out_specs=pl.BlockSpec(memory_space=pltpu.VMEM),
        scratch_shapes=[
            pltpu.VMEM((3, planes, rows, levels), F32),
            pltpu.VMEM((planes, rows, levels), F32),
            pltpu.VMEM((planes, rows, levels), F32),
            pltpu.VMEM((planes, rows, levels), F32),
            pltpu.VMEM((cells_x, cells_y, levels), F32),
        ],
        name="source_modes",
    )(rim, basis_rows)


def block_transpose(values, width):
    count = len(values)
    values = list(values)
    lane = lax.broadcasted_iota(jnp.int32, values[0].shape, 1) // width
    step = 1
    while step < count:
        odd = (lane & step) != 0
        for i in range(count):
            if i & step:
                continue
            low, high = values[i], values[i + step]
            shift = width * step
            values[i] = jnp.where(odd, pltpu.roll(high, shift, 1), low)
            values[i + step] = jnp.where(odd, high, pltpu.roll(low, low.shape[1] - shift, 1))
        step *= 2
    return values


def solve_kernel(
    east_count, north_count, cells_x, cells_y,
    in_ref, qx_ref, qxt_ref, qy_ref, qyt_ref, ex_ref, ey_ref, em_ref, rank_ref, out_ref, work,
):
    total_x = east_count * cells_x
    total_y = north_count * cells_y
    block = in_ref.shape[1]
    groups = cells_x // north_count
    for a in range(east_count):
        for g in range(groups):
            lanes = slice(g * total_y, (g + 1) * total_y)
            pieces = [in_ref[a * north_count + b, :, lanes] for b in range(north_count)]
            for i, piece in enumerate(block_transpose(pieces, cells_y)):
                row = (a * cells_x + g * north_count + i) * block
                work[row : row + block, :] = piece
    work[...] = high_dot(work[...], qy_ref[...], ((1,), (0,)))
    planes = [work[pl.ds(i, total_x, stride=block), :] for i in range(block)]
    waves = high_dot(qxt_ref[...], jnp.concatenate(planes, axis=1), ((1,), (0,)))
    eigen = ex_ref[...] + ey_ref[0:1, :]
    first = rank_ref[0] * block
    solved = []
    for i in range(block):
        value = eigen + em_ref[first + i]
        empty = value == 0.0
        factor = jnp.where(empty, 0.0, -1.0 / jnp.where(empty, 1.0, value))
        solved.append(waves[:, i * total_y : (i + 1) * total_y] * factor)
    back = high_dot(qx_ref[...], jnp.concatenate(solved, axis=1), ((1,), (0,)))
    for i in range(block):
        work[pl.ds(i, total_x, stride=block), :] = back[:, i * total_y : (i + 1) * total_y]
    work[...] = high_dot(work[...], qyt_ref[...], ((1,), (0,)))
    for a in range(east_count):
        for g in range(groups):
            lanes = slice(g * total_y, (g + 1) * total_y)
            rows = [(a * cells_x + g * north_count + i) * block for i in range(north_count)]
            pieces = [work[row : row + block, :] for row in rows]
            for b, piece in enumerate(block_transpose(pieces, cells_y)):
                out_ref[a * north_count + b, :, lanes] = piece


def solve_planes(blocks, rank, east_count, north_count, cells_x, cells_y, levels):
    total_x = east_count * cells_x
    total_y = north_count * cells_y
    qx, ex = fourier_basis(total_x)
    qy, ey = fourier_basis(total_y)
    vmem = pl.BlockSpec(memory_space=pltpu.VMEM)
    smem = pl.BlockSpec(memory_space=pltpu.SMEM)
    return pl.pallas_call(
        functools.partial(solve_kernel, east_count, north_count, cells_x, cells_y),
        out_shape=jax.ShapeDtypeStruct(blocks.shape, F32),
        in_specs=[vmem] * 7 + [smem] * 2,
        out_specs=vmem,
        scratch_shapes=[pltpu.VMEM((total_x * blocks.shape[1], total_y), F32)],
        name="solve_planes",
    )(
        blocks, qx, np.ascontiguousarray(qx.T), qy, np.ascontiguousarray(qy.T),
        np.ascontiguousarray(np.broadcast_to(ex[:, None], (total_x, total_y))),
        np.ascontiguousarray(np.broadcast_to(ey[None, :], (8, total_y))),
        mode_eigen(levels), rank,
    )


def pressure_kernel(modes_ref, basis_ref, out_ref):
    out_ref[...] = high_dot(modes_ref[...], basis_ref[...], ((0,), (0,)))


def pressure_cells(modes, basis_rows):
    return pl.pallas_call(
        pressure_kernel,
        out_shape=jax.ShapeDtypeStruct((modes.shape[1], basis_rows.shape[1]), F32),
        in_specs=[pl.BlockSpec(memory_space=pltpu.VMEM)] * 2,
        out_specs=pl.BlockSpec(memory_space=pltpu.VMEM),
        name="pressure_cells",
    )(modes, basis_rows)


def rotation(row_count, col_count, length, direction):
    product = (
        lax.broadcasted_iota(jnp.int32, (row_count, col_count), 0)
        * lax.broadcasted_iota(jnp.int32, (row_count, col_count), 1)
        % length
    )
    radians = 2.0 * math.pi / length * product.astype(jnp.float32)
    return (jnp.cos(radians), direction * jnp.sin(radians))


def matmul(table, operand):
    return jnp.dot(
        table, operand, precision=lax.Precision.HIGHEST, preferred_element_type=jnp.float32
    )


def contract(formula, table, operand):
    return jnp.einsum(
        formula, table, operand, precision=lax.Precision.HIGHEST, preferred_element_type=jnp.float32
    )


def transform_rows(real_part, imag_part, direction):
    length = real_part.shape[0]
    width = real_part.shape[1]
    factor_low = 1
    for candidate in range(1, math.isqrt(length) + 1):
        if length % candidate == 0:
            factor_low = candidate
    factor_high = length // factor_low
    cos_high, sin_high = rotation(factor_high, factor_high, factor_high, direction)
    grid_real = real_part.reshape(factor_high, factor_low * width)
    grid_imag = imag_part.reshape(factor_high, factor_low * width)
    section_real = (matmul(cos_high, grid_real) - matmul(sin_high, grid_imag)).reshape(
        factor_high, factor_low, width
    )
    section_imag = (matmul(cos_high, grid_imag) + matmul(sin_high, grid_real)).reshape(
        factor_high, factor_low, width
    )
    turn_cos, turn_sin = rotation(factor_high, factor_low, length, direction)
    turn_cos = turn_cos[:, :, None]
    turn_sin = turn_sin[:, :, None]
    turned_real = section_real * turn_cos - section_imag * turn_sin
    turned_imag = section_real * turn_sin + section_imag * turn_cos
    cos_low, sin_low = rotation(factor_low, factor_low, factor_low, direction)
    out_real = contract("ca,kar->ckr", cos_low, turned_real) - contract(
        "ca,kar->ckr", sin_low, turned_imag
    )
    out_imag = contract("ca,kar->ckr", cos_low, turned_imag) + contract(
        "ca,kar->ckr", sin_low, turned_real
    )
    return (out_real.reshape(length, width), out_imag.reshape(length, width))


def first_forward(flat, high_count, second_cells, level_count):
    total = flat.shape[0]
    width = flat.shape[1]
    low_length = total // high_count
    grid = flat.reshape(low_length, high_count * width)
    cos_low, sin_low = rotation(low_length, low_length, low_length, -1.0)
    section_real = matmul(cos_low, grid).reshape(low_length, high_count, second_cells, level_count)
    section_imag = matmul(sin_low, grid).reshape(low_length, high_count, second_cells, level_count)
    turn_cos, turn_sin = rotation(low_length, high_count, total, -1.0)
    turn_cos = turn_cos[:, :, None, None]
    turn_sin = turn_sin[:, :, None, None]
    turned_real = section_real * turn_cos - section_imag * turn_sin
    turned_imag = section_real * turn_sin + section_imag * turn_cos
    cos_high, sin_high = rotation(high_count, high_count, high_count, -1.0)
    out_real = contract("ca,kaym->cykm", cos_high, turned_real) - contract(
        "ca,kaym->cykm", sin_high, turned_imag
    )
    out_imag = contract("ca,kaym->cykm", cos_high, turned_imag) + contract(
        "ca,kaym->cykm", sin_high, turned_real
    )
    merged = low_length * level_count
    return (
        out_real.reshape(high_count, second_cells, merged),
        out_imag.reshape(high_count, second_cells, merged),
    )


def first_inverse(real_part, imag_part, level_count):
    high_count = real_part.shape[0]
    second_cells = real_part.shape[1]
    low_length = real_part.shape[2] // level_count
    total = high_count * low_length
    data_real = real_part.reshape(high_count, second_cells, low_length, level_count)
    data_imag = imag_part.reshape(high_count, second_cells, low_length, level_count)
    cos_high, sin_high = rotation(high_count, high_count, high_count, 1.0)
    section_real = contract("ac,cykm->kaym", cos_high, data_real) - contract(
        "ac,cykm->kaym", sin_high, data_imag
    )
    section_imag = contract("ac,cykm->kaym", cos_high, data_imag) + contract(
        "ac,cykm->kaym", sin_high, data_real
    )
    turn_cos, turn_sin = rotation(low_length, high_count, total, 1.0)
    turn_cos = turn_cos[:, :, None, None]
    turn_sin = turn_sin[:, :, None, None]
    turned_real = section_real * turn_cos - section_imag * turn_sin
    turned_imag = section_real * turn_sin + section_imag * turn_cos
    cos_low, sin_low = rotation(low_length, low_length, low_length, 1.0)
    flat = matmul(cos_low, turned_real.reshape(low_length, -1)) - matmul(
        sin_low, turned_imag.reshape(low_length, -1)
    )
    return flat.reshape(total, second_cells * level_count)


def solve_modes(
    real_part, imag_part, first_rank, second_rank, first_total, second_total, levels, level_count
):
    low_length = real_part.shape[1] // level_count
    shape_full = (second_total, low_length, level_count)
    wave_second = lax.broadcasted_iota(jnp.int32, shape_full, 0)
    wave_first = second_rank * low_length + lax.broadcasted_iota(jnp.int32, shape_full, 1)
    mode_index = first_rank * level_count + lax.broadcasted_iota(jnp.int32, shape_full, 2)
    eigen = 4.0 * jnp.sin(math.pi / first_total * wave_first.astype(jnp.float32)) ** 2
    eigen = eigen + 4.0 * jnp.sin(math.pi / second_total * wave_second.astype(jnp.float32)) ** 2
    eigen = eigen + 4.0 * jnp.sin(math.pi / (2.0 * levels) * mode_index.astype(jnp.float32)) ** 2
    empty = (wave_first == 0) & (wave_second == 0) & (mode_index == 0)
    factor = jnp.where(empty, 0.0, -1.0 / jnp.where(empty, 1.0, eigen)) / (
        first_total * second_total
    )
    factor = factor.reshape(second_total, low_length * level_count)
    return (real_part * factor, imag_part * factor)


def fold_half(real_part, imag_part, level_count):
    high_count = real_part.shape[0]
    second_cells = real_part.shape[1]
    low_length = real_part.shape[2] // level_count
    half_high = high_count // 2
    half_low = low_length // 2
    nyquist = real_part[half_high, :, :level_count]

    def halve(values):
        kept = values[:half_high].reshape(half_high, second_cells, 2, half_low * level_count)
        return kept.transpose(0, 2, 1, 3).reshape(high_count, second_cells, half_low * level_count)

    kept_real = halve(real_part)
    kept_imag = halve(imag_part).at[0, :, :level_count].set(nyquist)
    return (kept_real, kept_imag)


def solve_half(
    real_part, imag_part, first_rank, second_rank, first_total, second_total, levels, level_count
):
    packed_real = real_part[:, :level_count]
    packed_imag = imag_part[:, :level_count]
    mirror_real = jnp.roll(packed_real[::-1], 1, axis=0)
    mirror_imag = jnp.roll(packed_imag[::-1], 1, axis=0)
    zero_real = 0.5 * (packed_real + mirror_real)
    zero_imag = 0.5 * (packed_imag - mirror_imag)
    nyquist_real = 0.5 * (packed_imag + mirror_imag)
    nyquist_imag = -0.5 * (packed_real - mirror_real)
    first_block = second_rank == 0
    real_part = jnp.where(first_block, real_part.at[:, :level_count].set(zero_real), real_part)
    imag_part = jnp.where(first_block, imag_part.at[:, :level_count].set(zero_imag), imag_part)
    solved_real, solved_imag = solve_modes(
        real_part,
        imag_part,
        first_rank,
        second_rank,
        first_total,
        second_total,
        levels,
        level_count,
    )
    wave_second = lax.broadcasted_iota(jnp.int32, (second_total, level_count), 0)
    mode_index = first_rank * level_count + lax.broadcasted_iota(
        jnp.int32, (second_total, level_count), 1
    )
    eigen = 4.0 + 4.0 * jnp.sin(math.pi / second_total * wave_second.astype(jnp.float32)) ** 2
    eigen = eigen + 4.0 * jnp.sin(math.pi / (2.0 * levels) * mode_index.astype(jnp.float32)) ** 2
    nyquist_factor = -1.0 / eigen / (first_total * second_total)
    solved_nyquist_real = nyquist_real * nyquist_factor
    solved_nyquist_imag = nyquist_imag * nyquist_factor
    joined_real = solved_real[:, :level_count] - solved_nyquist_imag
    joined_imag = solved_imag[:, :level_count] + solved_nyquist_real
    solved_real = jnp.where(
        first_block, solved_real.at[:, :level_count].set(joined_real), solved_real
    )
    solved_imag = jnp.where(
        first_block, solved_imag.at[:, :level_count].set(joined_imag), solved_imag
    )
    return (solved_real, solved_imag)


def unfold_half(real_part, imag_part, level_count):
    high_count = real_part.shape[0]
    second_cells = real_part.shape[1]
    half_low = real_part.shape[2] // level_count
    half_high = high_count // 2
    low_length = 2 * half_low

    def unhalve(values):
        shaped = values.reshape(half_high, 2, second_cells, half_low * level_count)
        return shaped.transpose(0, 2, 1, 3).reshape(
            half_high, second_cells, low_length * level_count
        )

    lower_real = unhalve(real_part)
    lower_imag = unhalve(imag_part)
    zero_line = lower_real[0, :, :level_count]
    nyquist_line = lower_imag[0, :, :level_count]
    upper = jnp.zeros((high_count - half_high, second_cells, low_length * level_count), jnp.float32)
    full_real = jnp.concatenate([2.0 * lower_real, upper], axis=0)
    full_imag = jnp.concatenate([2.0 * lower_imag, upper], axis=0)
    full_real = (
        full_real.at[0, :, :level_count]
        .set(zero_line)
        .at[half_high, :, :level_count]
        .set(nyquist_line)
    )
    full_imag = full_imag.at[0, :, :level_count].set(0.0)
    return (full_real, full_imag)


def spectral(
    modes,
    first_rank,
    second_rank,
    second_count,
    levels,
    send_out,
    send_across,
    bring_back,
    bring_home,
):
    first_count = modes.shape[0]
    first_cells = modes.shape[1]
    merged = modes.shape[2]
    level_count = levels // first_count
    second_cells = merged // level_count
    first_total = first_count * first_cells
    second_total = second_count * second_cells
    pencil = send_out(modes).reshape(first_total, merged)
    line_real, line_imag = first_forward(pencil, second_count, second_cells, level_count)
    line_real, line_imag = fold_half(line_real, line_imag, level_count)
    across_real, across_imag = send_across(line_real, line_imag)
    across_real = across_real.reshape(second_total, -1)
    across_imag = across_imag.reshape(second_total, -1)
    wave_real, wave_imag = transform_rows(across_real, across_imag, -1.0)
    wave_real, wave_imag = solve_half(
        wave_real,
        wave_imag,
        first_rank,
        second_rank,
        first_total,
        second_total,
        levels,
        level_count,
    )
    back_real, back_imag = transform_rows(wave_real, wave_imag, 1.0)
    home_real, home_imag = bring_back(
        back_real.reshape(1, second_total, -1), back_imag.reshape(1, second_total, -1)
    )
    home_real, home_imag = unfold_half(home_real, home_imag, level_count)
    flat = first_inverse(home_real, home_imag, level_count)
    return bring_home(flat.reshape(1, first_total, merged))


def staged(modes, east_count, north_count, cells_x, cells_y):
    levels = modes.shape[0]
    level_count = levels // east_count

    def send_out(values):
        return lax.all_to_all(values, "px", split_axis=0, concat_axis=1, tiled=True)

    def send_across(real_part, imag_part):
        return (
            lax.all_to_all(real_part, "py", split_axis=0, concat_axis=1, tiled=True),
            lax.all_to_all(imag_part, "py", split_axis=0, concat_axis=1, tiled=True),
        )

    def bring_back(real_part, imag_part):
        return (
            lax.all_to_all(real_part, "py", split_axis=1, concat_axis=0, tiled=True),
            lax.all_to_all(imag_part, "py", split_axis=1, concat_axis=0, tiled=True),
        )

    def bring_home(values):
        return lax.all_to_all(values, "px", split_axis=1, concat_axis=0, tiled=True)

    shaped = modes.reshape(east_count, level_count, cells_x, cells_y).transpose(0, 2, 3, 1)
    result = spectral(
        shaped.reshape(east_count, cells_x, cells_y * level_count),
        lax.axis_index("px"),
        lax.axis_index("py"),
        north_count,
        levels,
        send_out,
        send_across,
        bring_back,
        bring_home,
    )
    result = result.reshape(east_count, cells_x, cells_y, level_count).transpose(0, 3, 1, 2)
    return result.reshape(levels, cells_x * cells_y)


def shards(wind_east, wind_north, wind_up):
    cells_x, cells_y, levels = wind_east.shape
    east_count = lax.axis_size("px")
    north_count = lax.axis_size("py")
    devices = east_count * north_count
    basis_rows = np.ascontiguousarray(cosine_basis(levels).T)
    rim = with_halo(jnp.stack((wind_east, wind_north, wind_up)))
    modes = source_modes(rim, basis_rows, cells_x, cells_y)
    if levels == 8 * devices and north_count * cells_y == 128 and cells_x % north_count == 0:
        blocks = modes.reshape(devices, levels // devices, cells_x * cells_y)
        blocks = lax.all_to_all(blocks, ("px", "py"), split_axis=0, concat_axis=0, tiled=True)
        rank = (lax.axis_index("px") * north_count + lax.axis_index("py")).reshape(1)
        blocks = solve_planes(blocks, rank, east_count, north_count, cells_x, cells_y, levels)
        blocks = lax.all_to_all(blocks, ("px", "py"), split_axis=0, concat_axis=0, tiled=True)
        modes = blocks.reshape(levels, cells_x * cells_y)
    else:
        modes = staged(modes, east_count, north_count, cells_x, cells_y)
    return pressure_cells(modes, basis_rows).reshape(cells_x, cells_y, levels)


def solution(mesh):
    return jax.shard_map(
        shards,
        mesh=mesh,
        in_specs=(P("px", "py", None), P("px", "py", None), P("px", "py", None)),
        out_specs=P("px", "py", None),
        check_vma=False,
    )
```

```python
import functools
import math

import jax
import jax.numpy as jnp
import ml_dtypes
import numpy as np
from jax import lax
from jax.experimental import pallas as pl
from jax.experimental.pallas import tpu as pltpu
from jax.sharding import PartitionSpec as P

NU_BASE = 0.01
SMAGORINSKY = 0.16
STRAIN_FLOOR = 1.0
TIME_STEP = 0.25
HALO = 3
LANES = 128
F32 = jnp.float32
BF16 = jnp.bfloat16
FORWARD = 3
INVERSE = 2
KERNEL_VMEM = pltpu.CompilerParams(vmem_limit_bytes=24 * 2**20)


def cosine_basis(levels):
    level = np.arange(levels, dtype=np.int64)[:, None]
    mode = np.arange(levels, dtype=np.int64)[None, :]
    radians = math.pi / (2.0 * levels) * ((2 * level + 1) * mode % (4 * levels))
    weight = np.where(mode == 0, math.sqrt(1.0 / levels), math.sqrt(2.0 / levels))
    return (weight * np.cos(radians)).astype(np.float32)


def fourier_basis(length):
    cell = np.arange(length)
    half = length // 2
    columns = [np.full(length, math.sqrt(1.0 / length))]
    waves = [0]
    for wave in range(1, half):
        angle = 2.0 * math.pi * (cell * wave % length) / length
        columns += [math.sqrt(2.0 / length) * np.cos(angle), math.sqrt(2.0 / length) * np.sin(angle)]
        waves += [wave, wave]
    columns.append(math.sqrt(1.0 / length) * (1.0 - 2.0 * (cell % 2)))
    waves.append(half)
    eigen = 4.0 * np.sin(math.pi / length * np.array(waves)) ** 2
    return np.stack(columns, axis=1).astype(np.float32), eigen.astype(np.float32)


def mode_eigen(levels):
    return (4.0 * np.sin(math.pi / (2.0 * levels) * np.arange(levels)) ** 2).astype(np.float32)


PAIRS = {2: ((0, 0), (0, 1), (1, 0)), 3: ((0, 0), (0, 1), (1, 0), (1, 1), (0, 2), (2, 0))}


def parts_of(values, count, narrow):
    parts = []
    for _ in range(count):
        parts.append(values.astype(narrow))
        values = values - parts[-1].astype(values.dtype)
    return parts


def table_parts(table, axis, count):
    parts = parts_of(table, count, ml_dtypes.bfloat16)
    return np.ascontiguousarray(np.concatenate([parts[t] for t, _ in PAIRS[count]], axis=axis))


def value_parts(values, axis, count):
    parts = parts_of(values, count, BF16)
    return jnp.concatenate([parts[v] for _, v in PAIRS[count]], axis=axis)


def dot(left, right, contract):
    return lax.dot_general(left, right, (contract, ((), ())), preferred_element_type=F32)


def on_chip(values):
    return pltpu.with_memory_space_constraint(values, pltpu.VMEM)


def ring(axis):
    size = lax.axis_size(axis)
    up = [(i, (i + 1) % size) for i in range(size)]
    return up, [(j, i) for i, j in up]


def lane_blocks(values):
    return [values[:, i : i + LANES] for i in range(0, values.shape[1], LANES)]


def z_next(values, edge):
    lane = lax.broadcasted_iota(jnp.int32, (values.shape[0], LANES), 1)
    turned = [pltpu.roll(block, LANES - 1, 1) for block in lane_blocks(values)] + [edge]
    last = lane == LANES - 1
    pairs = zip(turned[1:], turned[:-1])
    return jnp.concatenate([jnp.where(last, after, here) for after, here in pairs], axis=1)


def z_prev(values, edge):
    lane = lax.broadcasted_iota(jnp.int32, (values.shape[0], LANES), 1)
    turned = [edge] + [pltpu.roll(block, 1, 1) for block in lane_blocks(values)]
    pairs = zip(turned[:-1], turned[1:])
    return jnp.concatenate([jnp.where(lane == 0, before, here) for before, here in pairs], axis=1)


def y_next(values):
    return pltpu.roll(values, values.shape[0] - 1, 0)


def y_prev(values):
    return pltpu.roll(values, 1, 0)


def eddy(total):
    root = total + 4.0 * STRAIN_FLOOR
    return NU_BASE + (0.5 * SMAGORINSKY) * (root * lax.rsqrt(root))


def visc_plane(x, wind, above, below, visc):
    along_x = [wind[c, x + 1] - wind[c, x - 1] for c in range(3)]
    along_y = [y_next(wind[c, x]) - y_prev(wind[c, x]) for c in range(3)]
    along_z = [above[c, x] - below[c, x] for c in range(3)]
    normal = along_x[0] * along_x[0] + along_y[1] * along_y[1] + along_z[2] * along_z[2]
    xy = along_x[1] + along_y[0]
    xz = along_x[2] + along_z[0]
    yz = along_y[2] + along_z[1]
    visc[x] = eddy((normal + normal) + (xy * xy + xz * xz + yz * yz))


def wind_plane(x, wind, above, below, visc, east, part):
    cells = east.shape[1]
    centre = [wind[c, x] for c in range(3)]
    nu = visc[x]
    lane = lax.broadcasted_iota(jnp.int32, (nu.shape[0], LANES), 1)
    ends = [jnp.where(lane < LANES // 2, u[:, :LANES], u[:, -LANES:]) for u in centre]
    beyond = eddy(2.0 * (ends[2] * ends[2]) + (ends[0] * ends[0] + ends[1] * ends[1]))
    sum_xn = nu + visc[x + 1]
    sum_xp = nu + visc[x - 1]
    sum_yn = nu + y_next(nu)
    sum_yp = nu + y_prev(nu)
    sum_zn = nu + z_next(nu, beyond)
    sum_zp = nu + z_prev(nu, beyond)
    whole = ((sum_xn + sum_xp) + (sum_yn + sum_yp)) + ((sum_zn + sum_zp) - 2.0 / TIME_STEP)
    coef = (
        sum_xn - centre[0],
        sum_xp + centre[0],
        sum_yn - centre[1],
        sum_yp + centre[1],
        sum_zn - centre[2],
        sum_zp + centre[2],
    )

    def one(c, rows):
        u = centre[c]
        total = coef[0][:rows] * wind[c, x + 1, :rows] + coef[1][:rows] * wind[c, x - 1, :rows]
        total += coef[2][:rows] * y_next(u)[:rows] + coef[3][:rows] * y_prev(u)[:rows]
        total += coef[4][:rows] * above[c, x, :rows] + coef[5][:rows] * below[c, x, :rows]
        return total - whole[:rows] * u[:rows]

    east[x] = one(0, cells)
    north = one(1, nu.shape[0])
    up = one(2, cells)
    edge = centre[2][:cells]
    top = sum_zn[:cells, -LANES:] * edge[:, -LANES:]
    bottom = sum_zp[:cells, :LANES] * edge[:, :LANES]
    part[x] = (y_next(north) - y_prev(north))[:cells] + (z_next(up, top) - z_prev(up, bottom))


def store_plane(c, x, plane, wind, above, below):
    none = jnp.zeros((plane.shape[0], LANES), F32)
    wind[c, x] = plane
    above[c, x] = z_next(plane, none)
    below[c, x] = z_prev(plane, none)


def each(first, last, body, jump=0, skip=0):
    def step(i, carry):
        body(i + jnp.where(i >= first + jump, skip, 0) if skip else i)
        return carry

    lax.fori_loop(first, last, step, 0)


def inner_kernel(winds_ref, before_ref, after_ref, wind, above, below, visc, east, part):
    cells_x, cells_y, levels = winds_ref.shape[1:]
    rows = wind.shape[2]
    gap = jnp.zeros((rows - cells_y - 2 * HALO, levels), F32)

    def load(x):
        for c in range(3):
            pieces = [winds_ref[c, x], after_ref[c, x], before_ref[c, x]]
            own, after, before = [piece.astype(F32) for piece in pieces]
            plane = jnp.concatenate([own, after, gap, before], axis=0)
            store_plane(c, x + HALO, plane, wind, above, below)

    each(0, cells_x, load)
    first, last = HALO, HALO + cells_x
    each(first + 1, last - 1, lambda x: visc_plane(x, wind, above, below, visc))
    each(first + 2, last - 2, lambda x: wind_plane(x, wind, above, below, visc, east, part))


def outer_kernel(low_ref, high_ref, basis_ref, *refs):
    wind, above, below, visc, east, part = refs[6:12]
    out_ref, source = refs[12:]
    cells_x, cells_y, levels = source.shape
    skip = cells_x

    def load(x):
        for c in range(3):
            for ref, start in ((low_ref, 0), (high_ref, HALO + cells_x)):
                store_plane(c, x + start, ref[c, x].astype(F32), wind, above, below)

    each(0, HALO, load)
    each(1, 7, lambda x: visc_plane(x, wind, above, below, visc), 3, skip - 2)
    each(2, 8, lambda x: wind_plane(x, wind, above, below, visc, east, part), 3, skip - 4)

    def collect(x):
        source[x] = part[x + HALO] + (east[x + HALO + 1] - east[x + HALO - 1])

    each(0, cells_x, collect)
    flat = source[...].reshape(cells_x * cells_y, levels)
    out_ref[...] = dot(basis_ref[...], value_parts(flat, 1, FORWARD), ((1,), (1,)))


def pack_kernel(east_ref, north_ref, up_ref, winds_ref, leading_ref, last_ref):
    cells_x, cells_y, levels = east_ref.shape

    def plane(x):
        for c, ref in enumerate((east_ref, north_ref, up_ref)):
            own = ref[x]
            winds_ref[c, x] = own
            wide = own.astype(F32)
            leading_ref[c, x] = wide[:HALO].astype(BF16)
            last_ref[c, x] = wide[cells_y - HALO :].astype(BF16)

    each(0, cells_x, plane)


def pack_winds(winds):
    cells_x, cells_y, levels = winds[0].shape
    vmem = pl.BlockSpec(memory_space=pltpu.VMEM)
    edge = pltpu.VMEM((3, cells_x, HALO, levels), BF16)
    return pl.pallas_call(
        pack_kernel,
        out_shape=[pltpu.VMEM((3, cells_x, cells_y, levels), BF16), edge, edge],
        in_specs=[vmem] * 3,
        out_specs=[vmem] * 3,
        compiler_params=KERNEL_VMEM,
        name="pack_winds",
    )(*[pltpu.with_memory_space_constraint(wind, pltpu.HBM) for wind in winds])


def source_modes(winds, basis_rows):
    cells_x, cells_y, levels = winds[0].shape
    planes = cells_x + 2 * HALO
    gap = -(cells_y + 2 * HALO) % 8
    rows = cells_y + 2 * HALO + gap
    up, down = ring("py")
    stacked, leading, last = pack_winds(winds)
    before = lax.ppermute(last, "py", up)
    after = lax.ppermute(leading, "py", down)
    none = jnp.zeros((3, HALO, gap, levels), BF16)

    def edge(first):
        own = stacked[:, first : first + HALO]
        span = slice(first, first + HALO)
        return jnp.concatenate([own, after[:, span], none, before[:, span]], axis=2)

    up, down = ring("px")
    low = lax.ppermute(edge(cells_x - HALO), "px", up)
    high = lax.ppermute(edge(0), "px", down)
    vmem = pl.BlockSpec(memory_space=pltpu.VMEM)
    shapes = [pltpu.VMEM((3, planes, rows, levels), F32)] * 3
    shapes += [pltpu.VMEM((planes, rows, levels), F32)]
    shapes += [pltpu.VMEM((planes, cells_y, levels), F32)] * 2
    state = pl.pallas_call(
        inner_kernel,
        out_shape=shapes,
        in_specs=[vmem] * 3,
        out_specs=[vmem] * 6,
        cost_estimate=pl.CostEstimate(flops=40_000_000, bytes_accessed=6_000_000, transcendentals=0),
        compiler_params=KERNEL_VMEM,
        name="inner_planes",
    )(on_chip(stacked), on_chip(before), on_chip(after))
    results = pl.pallas_call(
        outer_kernel,
        out_shape=shapes + [pltpu.VMEM((levels, cells_x * cells_y), F32)],
        in_specs=[vmem] * 9,
        out_specs=[vmem] * 7,
        input_output_aliases={3 + i: i for i in range(6)},
        scratch_shapes=[pltpu.VMEM((cells_x, cells_y, levels), F32)],
        compiler_params=KERNEL_VMEM,
        name="outer_planes",
    )(on_chip(low), on_chip(high), on_chip(table_parts(basis_rows * np.float32(0.0625), 1, FORWARD)), *[on_chip(part) for part in state])
    return results[6]


def block_transpose(values, width):
    count = len(values)
    values = list(values)
    lane = lax.broadcasted_iota(jnp.int32, values[0].shape, 1) // width
    step = 1
    while step < count:
        odd = (lane & step) != 0
        for i in range(count):
            if i & step:
                continue
            low, high = values[i], values[i + step]
            shift = width * step
            values[i] = jnp.where(odd, pltpu.roll(high, shift, 1), low)
            values[i + step] = jnp.where(odd, high, pltpu.roll(low, low.shape[1] - shift, 1))
        step *= 2
    return values


def solve_kernel(
    east_count, north_count, cells_x, cells_y,
    in_ref, qx_ref, qxt_ref, qy_ref, qyt_ref, ex_ref, ey_ref, em_ref, rank_ref, out_ref, work,
):
    total_x = east_count * cells_x
    total_y = north_count * cells_y
    block = in_ref.shape[1]
    groups = cells_x // north_count
    for a in range(east_count):
        for g in range(groups):
            lanes = slice(g * total_y, (g + 1) * total_y)
            pieces = [in_ref[a * north_count + b, :, lanes] for b in range(north_count)]
            for i, piece in enumerate(block_transpose(pieces, cells_y)):
                row = (a * cells_x + g * north_count + i) * block
                work[row : row + block, :] = piece
    work[...] = dot(value_parts(work[...], 1, FORWARD), qy_ref[...], ((1,), (0,)))
    planes = [work[pl.ds(i, total_x, stride=block), :] for i in range(block)]
    waves = dot(qxt_ref[...], value_parts(jnp.concatenate(planes, axis=1), 0, FORWARD), ((1,), (0,)))
    eigen = ex_ref[...] + ey_ref[0:1, :]
    first = rank_ref[0] * block
    solved = []
    for i in range(block):
        value = eigen + em_ref[first + i]
        empty = value == 0.0
        factor = jnp.where(empty, 0.0, -1.0 / jnp.where(empty, 1.0, value))
        solved.append(waves[:, i * total_y : (i + 1) * total_y] * factor)
    back = dot(qx_ref[...], value_parts(jnp.concatenate(solved, axis=1), 0, INVERSE), ((1,), (0,)))
    for i in range(block):
        work[pl.ds(i, total_x, stride=block), :] = back[:, i * total_y : (i + 1) * total_y]
    work[...] = dot(value_parts(work[...], 1, INVERSE), qyt_ref[...], ((1,), (0,)))
    for a in range(east_count):
        for g in range(groups):
            lanes = slice(g * total_y, (g + 1) * total_y)
            rows = [(a * cells_x + g * north_count + i) * block for i in range(north_count)]
            pieces = [work[row : row + block, :] for row in rows]
            for b, piece in enumerate(block_transpose(pieces, cells_y)):
                out_ref[a * north_count + b, :, lanes] = piece


def solve_planes(blocks, rank, east_count, north_count, cells_x, cells_y, levels):
    total_x = east_count * cells_x
    total_y = north_count * cells_y
    qx, ex = fourier_basis(total_x)
    qy, ey = fourier_basis(total_y)
    tables = [
        table_parts(qx, 1, INVERSE),
        table_parts(qx.T, 1, FORWARD),
        table_parts(qy, 0, FORWARD),
        table_parts(qy.T, 0, INVERSE),
    ]
    tables += [
        np.ascontiguousarray(np.broadcast_to(ex[:, None], (total_x, total_y))),
        np.ascontiguousarray(np.broadcast_to(ey[None, :], (8, total_y))),
    ]
    vmem = pl.BlockSpec(memory_space=pltpu.VMEM)
    smem = pl.BlockSpec(memory_space=pltpu.SMEM)
    return pl.pallas_call(
        functools.partial(solve_kernel, east_count, north_count, cells_x, cells_y),
        out_shape=pltpu.VMEM(blocks.shape, F32),
        in_specs=[vmem] * 7 + [smem] * 2,
        out_specs=vmem,
        scratch_shapes=[pltpu.VMEM((total_x * blocks.shape[1], total_y), F32)],
        compiler_params=KERNEL_VMEM,
        name="solve_planes",
    )(on_chip(blocks), *[on_chip(table) for table in tables], mode_eigen(levels), rank)


def pressure_kernel(modes_ref, basis_ref, out_ref):
    out_ref[...] = dot(value_parts(modes_ref[...], 0, INVERSE), basis_ref[...], ((0,), (0,)))


def pressure_cells(modes, basis_rows):
    return pl.pallas_call(
        pressure_kernel,
        out_shape=jax.ShapeDtypeStruct((modes.shape[1], basis_rows.shape[1]), F32),
        in_specs=[pl.BlockSpec(memory_space=pltpu.VMEM)] * 2,
        out_specs=pl.BlockSpec(memory_space=pltpu.VMEM),
        compiler_params=KERNEL_VMEM,
        name="pressure_cells",
    )(on_chip(modes), on_chip(table_parts(basis_rows, 0, INVERSE)))


def rotation(row_count, col_count, length, direction):
    product = (
        lax.broadcasted_iota(jnp.int32, (row_count, col_count), 0)
        * lax.broadcasted_iota(jnp.int32, (row_count, col_count), 1)
        % length
    )
    radians = 2.0 * math.pi / length * product.astype(jnp.float32)
    return (jnp.cos(radians), direction * jnp.sin(radians))


def matmul(table, operand):
    return jnp.dot(
        table, operand, precision=lax.Precision.HIGHEST, preferred_element_type=jnp.float32
    )


def contract(formula, table, operand):
    return jnp.einsum(
        formula, table, operand, precision=lax.Precision.HIGHEST, preferred_element_type=jnp.float32
    )


def transform_rows(real_part, imag_part, direction):
    length = real_part.shape[0]
    width = real_part.shape[1]
    factor_low = 1
    for candidate in range(1, math.isqrt(length) + 1):
        if length % candidate == 0:
            factor_low = candidate
    factor_high = length // factor_low
    cos_high, sin_high = rotation(factor_high, factor_high, factor_high, direction)
    grid_real = real_part.reshape(factor_high, factor_low * width)
    grid_imag = imag_part.reshape(factor_high, factor_low * width)
    section_real = (matmul(cos_high, grid_real) - matmul(sin_high, grid_imag)).reshape(
        factor_high, factor_low, width
    )
    section_imag = (matmul(cos_high, grid_imag) + matmul(sin_high, grid_real)).reshape(
        factor_high, factor_low, width
    )
    turn_cos, turn_sin = rotation(factor_high, factor_low, length, direction)
    turn_cos = turn_cos[:, :, None]
    turn_sin = turn_sin[:, :, None]
    turned_real = section_real * turn_cos - section_imag * turn_sin
    turned_imag = section_real * turn_sin + section_imag * turn_cos
    cos_low, sin_low = rotation(factor_low, factor_low, factor_low, direction)
    out_real = contract("ca,kar->ckr", cos_low, turned_real) - contract(
        "ca,kar->ckr", sin_low, turned_imag
    )
    out_imag = contract("ca,kar->ckr", cos_low, turned_imag) + contract(
        "ca,kar->ckr", sin_low, turned_real
    )
    return (out_real.reshape(length, width), out_imag.reshape(length, width))


def first_forward(flat, high_count, second_cells, level_count):
    total = flat.shape[0]
    width = flat.shape[1]
    low_length = total // high_count
    grid = flat.reshape(low_length, high_count * width)
    cos_low, sin_low = rotation(low_length, low_length, low_length, -1.0)
    section_real = matmul(cos_low, grid).reshape(low_length, high_count, second_cells, level_count)
    section_imag = matmul(sin_low, grid).reshape(low_length, high_count, second_cells, level_count)
    turn_cos, turn_sin = rotation(low_length, high_count, total, -1.0)
    turn_cos = turn_cos[:, :, None, None]
    turn_sin = turn_sin[:, :, None, None]
    turned_real = section_real * turn_cos - section_imag * turn_sin
    turned_imag = section_real * turn_sin + section_imag * turn_cos
    cos_high, sin_high = rotation(high_count, high_count, high_count, -1.0)
    out_real = contract("ca,kaym->cykm", cos_high, turned_real) - contract(
        "ca,kaym->cykm", sin_high, turned_imag
    )
    out_imag = contract("ca,kaym->cykm", cos_high, turned_imag) + contract(
        "ca,kaym->cykm", sin_high, turned_real
    )
    merged = low_length * level_count
    return (
        out_real.reshape(high_count, second_cells, merged),
        out_imag.reshape(high_count, second_cells, merged),
    )


def first_inverse(real_part, imag_part, level_count):
    high_count = real_part.shape[0]
    second_cells = real_part.shape[1]
    low_length = real_part.shape[2] // level_count
    total = high_count * low_length
    data_real = real_part.reshape(high_count, second_cells, low_length, level_count)
    data_imag = imag_part.reshape(high_count, second_cells, low_length, level_count)
    cos_high, sin_high = rotation(high_count, high_count, high_count, 1.0)
    section_real = contract("ac,cykm->kaym", cos_high, data_real) - contract(
        "ac,cykm->kaym", sin_high, data_imag
    )
    section_imag = contract("ac,cykm->kaym", cos_high, data_imag) + contract(
        "ac,cykm->kaym", sin_high, data_real
    )
    turn_cos, turn_sin = rotation(low_length, high_count, total, 1.0)
    turn_cos = turn_cos[:, :, None, None]
    turn_sin = turn_sin[:, :, None, None]
    turned_real = section_real * turn_cos - section_imag * turn_sin
    turned_imag = section_real * turn_sin + section_imag * turn_cos
    cos_low, sin_low = rotation(low_length, low_length, low_length, 1.0)
    flat = matmul(cos_low, turned_real.reshape(low_length, -1)) - matmul(
        sin_low, turned_imag.reshape(low_length, -1)
    )
    return flat.reshape(total, second_cells * level_count)


def solve_modes(
    real_part, imag_part, first_rank, second_rank, first_total, second_total, levels, level_count
):
    low_length = real_part.shape[1] // level_count
    shape_full = (second_total, low_length, level_count)
    wave_second = lax.broadcasted_iota(jnp.int32, shape_full, 0)
    wave_first = second_rank * low_length + lax.broadcasted_iota(jnp.int32, shape_full, 1)
    mode_index = first_rank * level_count + lax.broadcasted_iota(jnp.int32, shape_full, 2)
    eigen = 4.0 * jnp.sin(math.pi / first_total * wave_first.astype(jnp.float32)) ** 2
    eigen = eigen + 4.0 * jnp.sin(math.pi / second_total * wave_second.astype(jnp.float32)) ** 2
    eigen = eigen + 4.0 * jnp.sin(math.pi / (2.0 * levels) * mode_index.astype(jnp.float32)) ** 2
    empty = (wave_first == 0) & (wave_second == 0) & (mode_index == 0)
    factor = jnp.where(empty, 0.0, -1.0 / jnp.where(empty, 1.0, eigen)) / (
        first_total * second_total
    )
    factor = factor.reshape(second_total, low_length * level_count)
    return (real_part * factor, imag_part * factor)


def fold_half(real_part, imag_part, level_count):
    high_count = real_part.shape[0]
    second_cells = real_part.shape[1]
    low_length = real_part.shape[2] // level_count
    half_high = high_count // 2
    half_low = low_length // 2
    nyquist = real_part[half_high, :, :level_count]

    def halve(values):
        kept = values[:half_high].reshape(half_high, second_cells, 2, half_low * level_count)
        return kept.transpose(0, 2, 1, 3).reshape(high_count, second_cells, half_low * level_count)

    kept_real = halve(real_part)
    kept_imag = halve(imag_part).at[0, :, :level_count].set(nyquist)
    return (kept_real, kept_imag)


def solve_half(
    real_part, imag_part, first_rank, second_rank, first_total, second_total, levels, level_count
):
    packed_real = real_part[:, :level_count]
    packed_imag = imag_part[:, :level_count]
    mirror_real = jnp.roll(packed_real[::-1], 1, axis=0)
    mirror_imag = jnp.roll(packed_imag[::-1], 1, axis=0)
    zero_real = 0.5 * (packed_real + mirror_real)
    zero_imag = 0.5 * (packed_imag - mirror_imag)
    nyquist_real = 0.5 * (packed_imag + mirror_imag)
    nyquist_imag = -0.5 * (packed_real - mirror_real)
    first_block = second_rank == 0
    real_part = jnp.where(first_block, real_part.at[:, :level_count].set(zero_real), real_part)
    imag_part = jnp.where(first_block, imag_part.at[:, :level_count].set(zero_imag), imag_part)
    solved_real, solved_imag = solve_modes(
        real_part,
        imag_part,
        first_rank,
        second_rank,
        first_total,
        second_total,
        levels,
        level_count,
    )
    wave_second = lax.broadcasted_iota(jnp.int32, (second_total, level_count), 0)
    mode_index = first_rank * level_count + lax.broadcasted_iota(
        jnp.int32, (second_total, level_count), 1
    )
    eigen = 4.0 + 4.0 * jnp.sin(math.pi / second_total * wave_second.astype(jnp.float32)) ** 2
    eigen = eigen + 4.0 * jnp.sin(math.pi / (2.0 * levels) * mode_index.astype(jnp.float32)) ** 2
    nyquist_factor = -1.0 / eigen / (first_total * second_total)
    solved_nyquist_real = nyquist_real * nyquist_factor
    solved_nyquist_imag = nyquist_imag * nyquist_factor
    joined_real = solved_real[:, :level_count] - solved_nyquist_imag
    joined_imag = solved_imag[:, :level_count] + solved_nyquist_real
    solved_real = jnp.where(
        first_block, solved_real.at[:, :level_count].set(joined_real), solved_real
    )
    solved_imag = jnp.where(
        first_block, solved_imag.at[:, :level_count].set(joined_imag), solved_imag
    )
    return (solved_real, solved_imag)


def unfold_half(real_part, imag_part, level_count):
    high_count = real_part.shape[0]
    second_cells = real_part.shape[1]
    half_low = real_part.shape[2] // level_count
    half_high = high_count // 2
    low_length = 2 * half_low

    def unhalve(values):
        shaped = values.reshape(half_high, 2, second_cells, half_low * level_count)
        return shaped.transpose(0, 2, 1, 3).reshape(
            half_high, second_cells, low_length * level_count
        )

    lower_real = unhalve(real_part)
    lower_imag = unhalve(imag_part)
    zero_line = lower_real[0, :, :level_count]
    nyquist_line = lower_imag[0, :, :level_count]
    upper = jnp.zeros((high_count - half_high, second_cells, low_length * level_count), jnp.float32)
    full_real = jnp.concatenate([2.0 * lower_real, upper], axis=0)
    full_imag = jnp.concatenate([2.0 * lower_imag, upper], axis=0)
    full_real = (
        full_real.at[0, :, :level_count]
        .set(zero_line)
        .at[half_high, :, :level_count]
        .set(nyquist_line)
    )
    full_imag = full_imag.at[0, :, :level_count].set(0.0)
    return (full_real, full_imag)


def spectral(
    modes,
    first_rank,
    second_rank,
    second_count,
    levels,
    send_out,
    send_across,
    bring_back,
    bring_home,
):
    first_count = modes.shape[0]
    first_cells = modes.shape[1]
    merged = modes.shape[2]
    level_count = levels // first_count
    second_cells = merged // level_count
    first_total = first_count * first_cells
    second_total = second_count * second_cells
    pencil = send_out(modes).reshape(first_total, merged)
    line_real, line_imag = first_forward(pencil, second_count, second_cells, level_count)
    line_real, line_imag = fold_half(line_real, line_imag, level_count)
    across_real, across_imag = send_across(line_real, line_imag)
    across_real = across_real.reshape(second_total, -1)
    across_imag = across_imag.reshape(second_total, -1)
    wave_real, wave_imag = transform_rows(across_real, across_imag, -1.0)
    wave_real, wave_imag = solve_half(
        wave_real,
        wave_imag,
        first_rank,
        second_rank,
        first_total,
        second_total,
        levels,
        level_count,
    )
    back_real, back_imag = transform_rows(wave_real, wave_imag, 1.0)
    home_real, home_imag = bring_back(
        back_real.reshape(1, second_total, -1), back_imag.reshape(1, second_total, -1)
    )
    home_real, home_imag = unfold_half(home_real, home_imag, level_count)
    flat = first_inverse(home_real, home_imag, level_count)
    return bring_home(flat.reshape(1, first_total, merged))


def staged(modes, east_count, north_count, cells_x, cells_y):
    levels = modes.shape[0]
    level_count = levels // east_count

    def send_out(values):
        return lax.all_to_all(values, "px", split_axis=0, concat_axis=1, tiled=True)

    def send_across(real_part, imag_part):
        return (
            lax.all_to_all(real_part, "py", split_axis=0, concat_axis=1, tiled=True),
            lax.all_to_all(imag_part, "py", split_axis=0, concat_axis=1, tiled=True),
        )

    def bring_back(real_part, imag_part):
        return (
            lax.all_to_all(real_part, "py", split_axis=1, concat_axis=0, tiled=True),
            lax.all_to_all(imag_part, "py", split_axis=1, concat_axis=0, tiled=True),
        )

    def bring_home(values):
        return lax.all_to_all(values, "px", split_axis=1, concat_axis=0, tiled=True)

    shaped = modes.reshape(east_count, level_count, cells_x, cells_y).transpose(0, 2, 3, 1)
    result = spectral(
        shaped.reshape(east_count, cells_x, cells_y * level_count),
        lax.axis_index("px"),
        lax.axis_index("py"),
        north_count,
        levels,
        send_out,
        send_across,
        bring_back,
        bring_home,
    )
    result = result.reshape(east_count, cells_x, cells_y, level_count).transpose(0, 3, 1, 2)
    return result.reshape(levels, cells_x * cells_y)


def shards(wind_east, wind_north, wind_up):
    cells_x, cells_y, levels = wind_east.shape
    east_count = lax.axis_size("px")
    north_count = lax.axis_size("py")
    devices = east_count * north_count
    basis_rows = np.ascontiguousarray(cosine_basis(levels).T)
    modes = source_modes((wind_east, wind_north, wind_up), basis_rows)
    if levels == 8 * devices and north_count * cells_y == 128 and cells_x % north_count == 0:
        blocks = modes.reshape(devices, levels // devices, cells_x * cells_y)
        blocks = lax.all_to_all(blocks, ("px", "py"), split_axis=0, concat_axis=0, tiled=True)
        rank = (lax.axis_index("px") * north_count + lax.axis_index("py")).reshape(1)
        blocks = solve_planes(blocks, rank, east_count, north_count, cells_x, cells_y, levels)
        blocks = lax.all_to_all(blocks, ("px", "py"), split_axis=0, concat_axis=0, tiled=True)
        modes = blocks.reshape(levels, cells_x * cells_y)
    else:
        modes = staged(modes, east_count, north_count, cells_x, cells_y)
    return pressure_cells(modes, basis_rows).reshape(cells_x, cells_y, levels)


def solution(mesh):
    return jax.shard_map(
        shards,
        mesh=mesh,
        in_specs=(P("px", "py", None), P("px", "py", None), P("px", "py", None)),
        out_specs=P("px", "py", None),
        check_vma=False,
    )
```

```python
import functools
import math

import jax
import jax.numpy as jnp
import ml_dtypes
import numpy as np
from jax import lax
from jax.experimental import pallas as pl
from jax.experimental.pallas import tpu as pltpu
from jax.sharding import PartitionSpec as P

NU_BASE = 0.01
SMAGORINSKY = 0.16
STRAIN_FLOOR = 1.0
TIME_STEP = 0.25
HALO = 3
ROWS = 4
LANES = 128
F32 = jnp.float32
BF16 = jnp.bfloat16
DCT_PARTS = 3
NORTH_PARTS = 3
EAST_PARTS = 3
INVERSE = 2
KERNEL_VMEM = pltpu.CompilerParams(vmem_limit_bytes=24 * 2**20)


def cosine_basis(levels):
    level = np.arange(levels, dtype=np.int64)[:, None]
    mode = np.arange(levels, dtype=np.int64)[None, :]
    radians = math.pi / (2.0 * levels) * ((2 * level + 1) * mode % (4 * levels))
    weight = np.where(mode == 0, math.sqrt(1.0 / levels), math.sqrt(2.0 / levels))
    return (weight * np.cos(radians)).astype(np.float32)


def fourier_basis(length):
    cell = np.arange(length)
    half = length // 2
    columns = [np.full(length, math.sqrt(1.0 / length))]
    waves = [0]
    for wave in range(1, half):
        angle = 2.0 * math.pi * (cell * wave % length) / length
        columns += [math.sqrt(2.0 / length) * np.cos(angle), math.sqrt(2.0 / length) * np.sin(angle)]
        waves += [wave, wave]
    columns.append(math.sqrt(1.0 / length) * (1.0 - 2.0 * (cell % 2)))
    waves.append(half)
    eigen = 4.0 * np.sin(math.pi / length * np.array(waves)) ** 2
    return np.stack(columns, axis=1).astype(np.float32), eigen.astype(np.float32)


def mode_eigen(levels):
    return (4.0 * np.sin(math.pi / (2.0 * levels) * np.arange(levels)) ** 2).astype(np.float32)


PAIRS = {2: ((0, 0), (0, 1), (1, 0)), 3: ((0, 0), (0, 1), (1, 0), (1, 1), (0, 2), (2, 0))}


def parts_of(values, count, narrow):
    parts = []
    for _ in range(count):
        parts.append(values.astype(narrow))
        values = values - parts[-1].astype(values.dtype)
    return parts


def table_parts(table, axis, count):
    parts = parts_of(table, count, ml_dtypes.bfloat16)
    return np.ascontiguousarray(np.concatenate([parts[t] for t, _ in PAIRS[count]], axis=axis))


def value_parts(values, axis, count):
    parts = parts_of(values, count, BF16)
    return jnp.concatenate([parts[v] for _, v in PAIRS[count]], axis=axis)


def dot(left, right, contract):
    return lax.dot_general(left, right, (contract, ((), ())), preferred_element_type=F32)


def on_chip(values):
    return pltpu.with_memory_space_constraint(values, pltpu.VMEM)


def swaps(axis):
    size = lax.axis_size(axis)
    inner = [(i, i ^ 1) for i in range(size)]
    outer = [(i, (i - 1 if i % 2 == 0 else i + 1) % size) for i in range(size)]
    return inner, outer


def ring(axis):
    size = lax.axis_size(axis)
    up = [(i, (i + 1) % size) for i in range(size)]
    return up, [(j, i) for i, j in up]


def lane_blocks(values):
    return [values[:, i : i + LANES] for i in range(0, values.shape[1], LANES)]


def z_next(values, edge):
    lane = lax.broadcasted_iota(jnp.int32, (values.shape[0], LANES), 1)
    turned = [pltpu.roll(block, LANES - 1, 1) for block in lane_blocks(values)] + [edge]
    last = lane == LANES - 1
    pairs = zip(turned[1:], turned[:-1])
    return jnp.concatenate([jnp.where(last, after, here) for after, here in pairs], axis=1)


def z_prev(values, edge):
    lane = lax.broadcasted_iota(jnp.int32, (values.shape[0], LANES), 1)
    turned = [edge] + [pltpu.roll(block, 1, 1) for block in lane_blocks(values)]
    pairs = zip(turned[:-1], turned[1:])
    return jnp.concatenate([jnp.where(lane == 0, before, here) for before, here in pairs], axis=1)


def y_next(values):
    return pltpu.roll(values, values.shape[0] - 1, 0)


def y_prev(values):
    return pltpu.roll(values, 1, 0)


def eddy(total):
    root = total + 4.0 * STRAIN_FLOOR
    return NU_BASE + (0.5 * SMAGORINSKY) * (root * lax.rsqrt(root))


def visc_plane(x, wind, above, below, visc):
    along_x = [wind[c, x + 1] - wind[c, x - 1] for c in range(3)]
    along_y = [y_next(wind[c, x]) - y_prev(wind[c, x]) for c in range(3)]
    along_z = [above[c, x] - below[c, x] for c in range(3)]
    normal = along_x[0] * along_x[0] + along_y[1] * along_y[1] + along_z[2] * along_z[2]
    xy = along_x[1] + along_y[0]
    xz = along_x[2] + along_z[0]
    yz = along_y[2] + along_z[1]
    visc[x] = eddy((normal + normal) + (xy * xy + xz * xz + yz * yz))


def wind_plane(x, wind, above, below, visc, east, part):
    cells = east.shape[1]
    centre = [wind[c, x] for c in range(3)]
    nu = visc[x]
    lane = lax.broadcasted_iota(jnp.int32, (nu.shape[0], LANES), 1)
    ends = [jnp.where(lane < LANES // 2, u[:, :LANES], u[:, -LANES:]) for u in centre]
    beyond = eddy(2.0 * (ends[2] * ends[2]) + (ends[0] * ends[0] + ends[1] * ends[1]))
    sum_xn = nu + visc[x + 1]
    sum_xp = nu + visc[x - 1]
    sum_yn = nu + y_next(nu)
    sum_yp = nu + y_prev(nu)
    sum_zn = nu + z_next(nu, beyond)
    sum_zp = nu + z_prev(nu, beyond)
    whole = ((sum_xn + sum_xp) + (sum_yn + sum_yp)) + ((sum_zn + sum_zp) - 2.0 / TIME_STEP)
    coef = (
        sum_xn - centre[0],
        sum_xp + centre[0],
        sum_yn - centre[1],
        sum_yp + centre[1],
        sum_zn - centre[2],
        sum_zp + centre[2],
    )

    def one(c, rows):
        u = centre[c]
        total = coef[0][:rows] * wind[c, x + 1, :rows] + coef[1][:rows] * wind[c, x - 1, :rows]
        total += coef[2][:rows] * y_next(u)[:rows] + coef[3][:rows] * y_prev(u)[:rows]
        total += coef[4][:rows] * above[c, x, :rows] + coef[5][:rows] * below[c, x, :rows]
        return total - whole[:rows] * u[:rows]

    east[x] = one(0, cells)
    north = one(1, nu.shape[0])
    up = one(2, cells)
    edge = centre[2][:cells]
    top = sum_zn[:cells, -LANES:] * edge[:, -LANES:]
    bottom = sum_zp[:cells, :LANES] * edge[:, :LANES]
    part[x] = (y_next(north) - y_prev(north))[:cells] + (z_next(up, top) - z_prev(up, bottom))


def store_plane(c, x, plane, wind, above, below):
    none = jnp.zeros((plane.shape[0], LANES), F32)
    wind[c, x] = plane
    above[c, x] = z_next(plane, none)
    below[c, x] = z_prev(plane, none)


def by_parity(odd, body):
    pl.when(odd == 1)(lambda: body(True))
    pl.when(odd == 0)(lambda: body(False))


def each(first, last, body, jump=0, skip=0, unroll=1):
    def step(i, carry):
        body(i + jnp.where(i >= first + jump, skip, 0) if skip else i)
        return carry

    lax.fori_loop(first, last, step, 0, unroll=unroll)


def inner_kernel(odd_ref, winds_ref, near_ref, far_ref, wind, above, below, visc, east, part):
    cells_x, cells_y, levels = winds_ref.shape[1:]

    def load(odd):
        after_ref, before_ref = (far_ref, near_ref) if odd else (near_ref, far_ref)

        def plane(x):
            for c in range(3):
                pieces = [winds_ref[c, x], after_ref[c, x], before_ref[c, x]]
                own, after, before = [piece.astype(F32) for piece in pieces]
                whole = jnp.concatenate([own, after, before], axis=0)
                store_plane(c, x + HALO, whole, wind, above, below)

        each(0, cells_x, plane, unroll=4)

    by_parity(odd_ref[0], load)
    first, last = HALO, HALO + cells_x
    each(first + 1, last - 1, lambda x: visc_plane(x, wind, above, below, visc), unroll=2)
    each(first + 2, last - 2, lambda x: wind_plane(x, wind, above, below, visc, east, part), unroll=2)


def outer_kernel(low_ref, high_ref, low_corner_ref, high_corner_ref, basis_ref, *refs):
    wind, above, below, visc, east, part = refs[6:12]
    out_ref, source = refs[12:]
    cells_x, cells_y, levels = source.shape
    skip = cells_x


    row = lax.broadcasted_iota(jnp.int32, (8, levels), 0)

    def load(c):
        for side, ref, corner_ref in ((0, low_ref, low_corner_ref), (1, high_ref, high_corner_ref)):
            nearest = corner_ref[c].astype(F32)
            second = jnp.where(row < 4, pltpu.roll(nearest, 6, 0), pltpu.roll(nearest, 2, 0))
            for i, rest in enumerate((nearest, second, jnp.zeros_like(nearest))):
                index = i if side else HALO - 1 - i
                plane = jnp.concatenate([ref[c, index].astype(F32), rest], axis=0)
                start = HALO + cells_x if side else 0
                store_plane(c, start + index, plane, wind, above, below)

    each(0, 3, load)
    each(1, 7, lambda x: visc_plane(x, wind, above, below, visc), 3, skip - 2, unroll=2)
    each(2, 8, lambda x: wind_plane(x, wind, above, below, visc, east, part), 3, skip - 4, unroll=2)

    def collect(x):
        source[x] = part[x + HALO] + (east[x + HALO + 1] - east[x + HALO - 1])

    each(0, cells_x, collect, unroll=4)
    flat = source[...].reshape(cells_x * cells_y, levels)
    out_ref[...] = dot(basis_ref[...], value_parts(flat, 1, DCT_PARTS), ((1,), (1,)))


def pack_kernel(odd_ref, *refs):
    winds = refs[:3]
    winds_ref, inner_ref, outer_ref, down_ref, up_ref, sems = refs[3:]
    cells_x, cells_y, levels = winds[0].shape

    def pack(odd):
        leading_ref, last_ref = (inner_ref, outer_ref) if odd else (outer_ref, inner_ref)
        copies = []
        for c, ref in enumerate(winds):
            pairs = (
                (ref.at[:, pl.ds(0, ROWS)], leading_ref.at[c]),
                (ref.at[:, pl.ds(cells_y - ROWS, ROWS)], last_ref.at[c]),
                (ref.at[pl.ds(0, HALO)], down_ref.at[c]),
                (ref.at[pl.ds(cells_x - HALO, HALO)], up_ref.at[c]),
                (ref, winds_ref.at[c]),
            )
            for i, (source, target) in enumerate(pairs):
                copies.append(pltpu.make_async_copy(source, target, sems.at[5 * c + i]))
        for copy in copies:
            copy.start()
        for copy in copies:
            copy.wait()

    by_parity(odd_ref[0], pack)


def pack_winds(winds, odd):
    cells_x, cells_y, levels = winds[0].shape
    vmem = pl.BlockSpec(memory_space=pltpu.VMEM)
    edge = pltpu.VMEM((3, cells_x, ROWS, levels), BF16)
    side = pltpu.VMEM((3, HALO, cells_y, levels), BF16)
    return pl.pallas_call(
        pack_kernel,
        out_shape=[pltpu.VMEM((3, cells_x, cells_y, levels), BF16), edge, edge, side, side],
        in_specs=[pl.BlockSpec(memory_space=pltpu.SMEM)] + [pl.BlockSpec(memory_space=pl.ANY)] * 3,
        out_specs=[vmem] * 5,
        scratch_shapes=[pltpu.SemaphoreType.DMA((15,))],
        compiler_params=KERNEL_VMEM,
        name="pack_winds",
    )(odd, *[pltpu.with_memory_space_constraint(wind, pltpu.HBM) for wind in winds])


def source_modes(winds, basis_rows):
    cells_x, cells_y, levels = winds[0].shape
    planes = cells_x + 2 * HALO
    rows = cells_y + 2 * ROWS
    odd_north = lax.axis_index("py") % 2
    odd = odd_north.reshape(1)
    stacked, inner_rows, outer_rows, leading, last = pack_winds(winds, odd)
    inner, outer = swaps("py")
    up, down = ring("px")
    outer_got = lax.ppermute(outer_rows, "py", outer)
    inner_got = lax.ppermute(inner_rows, "py", inner)
    low = lax.ppermute(last, "px", up)
    high = lax.ppermute(leading, "px", down)

    def corner(first, second):
        near, far = [[v[:, x] for x in (first, second)] for v in (inner_got, outer_got)]
        after = [jnp.where(odd_north == 1, f, n) for n, f in zip(near, far)]
        before = [jnp.where(odd_north == 1, n, f) for n, f in zip(near, far)]
        none = jnp.zeros((3, 2, levels), BF16)
        pieces = [after[0][:, :2], after[1][:, :1], none, before[1][:, 3:], before[0][:, 2:]]
        return jnp.concatenate(pieces, axis=1)

    low_corner = lax.ppermute(corner(cells_x - 1, cells_x - 2), "px", up)
    high_corner = lax.ppermute(corner(0, 1), "px", down)
    vmem = pl.BlockSpec(memory_space=pltpu.VMEM)
    smem = pl.BlockSpec(memory_space=pltpu.SMEM)
    shapes = [pltpu.VMEM((3, planes, rows, levels), F32)] * 3
    shapes += [pltpu.VMEM((planes, rows, levels), F32)]
    shapes += [pltpu.VMEM((planes, cells_y, levels), F32)] * 2
    state = pl.pallas_call(
        inner_kernel,
        out_shape=shapes,
        in_specs=[smem] + [vmem] * 3,
        out_specs=[vmem] * 6,
        cost_estimate=pl.CostEstimate(flops=40_000_000, bytes_accessed=6_000_000, transcendentals=0),
        compiler_params=KERNEL_VMEM,
        name="inner_planes",
    )(odd, on_chip(stacked), on_chip(inner_got), on_chip(outer_got))
    results = pl.pallas_call(
        outer_kernel,
        out_shape=shapes + [pltpu.VMEM((levels, cells_x * cells_y), F32)],
        in_specs=[vmem] * 11,
        out_specs=[vmem] * 7,
        input_output_aliases={5 + i: i for i in range(6)},
        scratch_shapes=[pltpu.VMEM((cells_x, cells_y, levels), F32)],
        compiler_params=KERNEL_VMEM,
        name="outer_planes",
    )(
        on_chip(low),
        on_chip(high),
        on_chip(low_corner),
        on_chip(high_corner),
        on_chip(table_parts(basis_rows * np.float32(0.0625), 1, DCT_PARTS)),
        *[on_chip(part) for part in state],
    )
    return results[6]


def block_transpose(values, width):
    count = len(values)
    values = list(values)
    lane = lax.broadcasted_iota(jnp.int32, values[0].shape, 1) // width
    step = 1
    while step < count:
        odd = (lane & step) != 0
        for i in range(count):
            if i & step:
                continue
            low, high = values[i], values[i + step]
            shift = width * step
            values[i] = jnp.where(odd, pltpu.roll(high, shift, 1), low)
            values[i + step] = jnp.where(odd, high, pltpu.roll(low, low.shape[1] - shift, 1))
        step *= 2
    return values


def solve_kernel(
    east_count, north_count, cells_x, cells_y,
    in_ref, qx_ref, qxt_ref, qy_ref, qyt_ref, ex_ref, ey_ref, em_ref, rank_ref, out_ref, work,
):
    total_x = east_count * cells_x
    total_y = north_count * cells_y
    block = in_ref.shape[1]
    groups = cells_x // north_count
    for a in range(east_count):
        for g in range(groups):
            lanes = slice(g * total_y, (g + 1) * total_y)
            pieces = [in_ref[a * north_count + b, :, lanes] for b in range(north_count)]
            for i, piece in enumerate(block_transpose(pieces, cells_y)):
                row = (a * cells_x + g * north_count + i) * block
                work[row : row + block, :] = piece
    work[...] = dot(value_parts(work[...], 1, NORTH_PARTS), qy_ref[...], ((1,), (0,)))
    planes = [work[pl.ds(i, total_x, stride=block), :] for i in range(block)]
    waves = dot(qxt_ref[...], value_parts(jnp.concatenate(planes, axis=1), 0, EAST_PARTS), ((1,), (0,)))
    eigen = ex_ref[...] + ey_ref[0:1, :]
    first = rank_ref[0] * block
    solved = []
    for i in range(block):
        value = eigen + em_ref[first + i]
        empty = value == 0.0
        factor = jnp.where(empty, 0.0, -1.0 / jnp.where(empty, 1.0, value))
        solved.append(waves[:, i * total_y : (i + 1) * total_y] * factor)
    back = dot(qx_ref[...], value_parts(jnp.concatenate(solved, axis=1), 0, INVERSE), ((1,), (0,)))
    for i in range(block):
        work[pl.ds(i, total_x, stride=block), :] = back[:, i * total_y : (i + 1) * total_y]
    work[...] = dot(value_parts(work[...], 1, INVERSE), qyt_ref[...], ((1,), (0,)))
    for a in range(east_count):
        for g in range(groups):
            lanes = slice(g * total_y, (g + 1) * total_y)
            rows = [(a * cells_x + g * north_count + i) * block for i in range(north_count)]
            pieces = [work[row : row + block, :] for row in rows]
            for b, piece in enumerate(block_transpose(pieces, cells_y)):
                out_ref[a * north_count + b, :, lanes] = piece


def solve_planes(blocks, rank, east_count, north_count, cells_x, cells_y, levels):
    total_x = east_count * cells_x
    total_y = north_count * cells_y
    qx, ex = fourier_basis(total_x)
    qy, ey = fourier_basis(total_y)
    tables = [
        table_parts(qx, 1, INVERSE),
        table_parts(qx.T, 1, EAST_PARTS),
        table_parts(qy, 0, NORTH_PARTS),
        table_parts(qy.T, 0, INVERSE),
    ]
    tables += [
        np.ascontiguousarray(np.broadcast_to(ex[:, None], (total_x, total_y))),
        np.ascontiguousarray(np.broadcast_to(ey[None, :], (8, total_y))),
    ]
    vmem = pl.BlockSpec(memory_space=pltpu.VMEM)
    smem = pl.BlockSpec(memory_space=pltpu.SMEM)
    return pl.pallas_call(
        functools.partial(solve_kernel, east_count, north_count, cells_x, cells_y),
        out_shape=pltpu.VMEM(blocks.shape, F32),
        in_specs=[vmem] * 7 + [smem] * 2,
        out_specs=vmem,
        scratch_shapes=[pltpu.VMEM((total_x * blocks.shape[1], total_y), F32)],
        compiler_params=KERNEL_VMEM,
        name="solve_planes",
    )(on_chip(blocks), *[on_chip(table) for table in tables], mode_eigen(levels), rank)


def pressure_kernel(modes_ref, basis_ref, out_ref):
    out_ref[...] = dot(value_parts(modes_ref[...], 0, INVERSE), basis_ref[...], ((0,), (0,)))


def pressure_cells(modes, basis_rows):
    return pl.pallas_call(
        pressure_kernel,
        out_shape=jax.ShapeDtypeStruct((modes.shape[1], basis_rows.shape[1]), F32),
        in_specs=[pl.BlockSpec(memory_space=pltpu.VMEM)] * 2,
        out_specs=pl.BlockSpec(memory_space=pltpu.VMEM),
        compiler_params=KERNEL_VMEM,
        name="pressure_cells",
    )(on_chip(modes), on_chip(table_parts(basis_rows, 0, INVERSE)))


def rotation(row_count, col_count, length, direction):
    product = (
        lax.broadcasted_iota(jnp.int32, (row_count, col_count), 0)
        * lax.broadcasted_iota(jnp.int32, (row_count, col_count), 1)
        % length
    )
    radians = 2.0 * math.pi / length * product.astype(jnp.float32)
    return (jnp.cos(radians), direction * jnp.sin(radians))


def matmul(table, operand):
    return jnp.dot(
        table, operand, precision=lax.Precision.HIGHEST, preferred_element_type=jnp.float32
    )


def contract(formula, table, operand):
    return jnp.einsum(
        formula, table, operand, precision=lax.Precision.HIGHEST, preferred_element_type=jnp.float32
    )


def transform_rows(real_part, imag_part, direction):
    length = real_part.shape[0]
    width = real_part.shape[1]
    factor_low = 1
    for candidate in range(1, math.isqrt(length) + 1):
        if length % candidate == 0:
            factor_low = candidate
    factor_high = length // factor_low
    cos_high, sin_high = rotation(factor_high, factor_high, factor_high, direction)
    grid_real = real_part.reshape(factor_high, factor_low * width)
    grid_imag = imag_part.reshape(factor_high, factor_low * width)
    section_real = (matmul(cos_high, grid_real) - matmul(sin_high, grid_imag)).reshape(
        factor_high, factor_low, width
    )
    section_imag = (matmul(cos_high, grid_imag) + matmul(sin_high, grid_real)).reshape(
        factor_high, factor_low, width
    )
    turn_cos, turn_sin = rotation(factor_high, factor_low, length, direction)
    turn_cos = turn_cos[:, :, None]
    turn_sin = turn_sin[:, :, None]
    turned_real = section_real * turn_cos - section_imag * turn_sin
    turned_imag = section_real * turn_sin + section_imag * turn_cos
    cos_low, sin_low = rotation(factor_low, factor_low, factor_low, direction)
    out_real = contract("ca,kar->ckr", cos_low, turned_real) - contract(
        "ca,kar->ckr", sin_low, turned_imag
    )
    out_imag = contract("ca,kar->ckr", cos_low, turned_imag) + contract(
        "ca,kar->ckr", sin_low, turned_real
    )
    return (out_real.reshape(length, width), out_imag.reshape(length, width))


def first_forward(flat, high_count, second_cells, level_count):
    total = flat.shape[0]
    width = flat.shape[1]
    low_length = total // high_count
    grid = flat.reshape(low_length, high_count * width)
    cos_low, sin_low = rotation(low_length, low_length, low_length, -1.0)
    section_real = matmul(cos_low, grid).reshape(low_length, high_count, second_cells, level_count)
    section_imag = matmul(sin_low, grid).reshape(low_length, high_count, second_cells, level_count)
    turn_cos, turn_sin = rotation(low_length, high_count, total, -1.0)
    turn_cos = turn_cos[:, :, None, None]
    turn_sin = turn_sin[:, :, None, None]
    turned_real = section_real * turn_cos - section_imag * turn_sin
    turned_imag = section_real * turn_sin + section_imag * turn_cos
    cos_high, sin_high = rotation(high_count, high_count, high_count, -1.0)
    out_real = contract("ca,kaym->cykm", cos_high, turned_real) - contract(
        "ca,kaym->cykm", sin_high, turned_imag
    )
    out_imag = contract("ca,kaym->cykm", cos_high, turned_imag) + contract(
        "ca,kaym->cykm", sin_high, turned_real
    )
    merged = low_length * level_count
    return (
        out_real.reshape(high_count, second_cells, merged),
        out_imag.reshape(high_count, second_cells, merged),
    )


def first_inverse(real_part, imag_part, level_count):
    high_count = real_part.shape[0]
    second_cells = real_part.shape[1]
    low_length = real_part.shape[2] // level_count
    total = high_count * low_length
    data_real = real_part.reshape(high_count, second_cells, low_length, level_count)
    data_imag = imag_part.reshape(high_count, second_cells, low_length, level_count)
    cos_high, sin_high = rotation(high_count, high_count, high_count, 1.0)
    section_real = contract("ac,cykm->kaym", cos_high, data_real) - contract(
        "ac,cykm->kaym", sin_high, data_imag
    )
    section_imag = contract("ac,cykm->kaym", cos_high, data_imag) + contract(
        "ac,cykm->kaym", sin_high, data_real
    )
    turn_cos, turn_sin = rotation(low_length, high_count, total, 1.0)
    turn_cos = turn_cos[:, :, None, None]
    turn_sin = turn_sin[:, :, None, None]
    turned_real = section_real * turn_cos - section_imag * turn_sin
    turned_imag = section_real * turn_sin + section_imag * turn_cos
    cos_low, sin_low = rotation(low_length, low_length, low_length, 1.0)
    flat = matmul(cos_low, turned_real.reshape(low_length, -1)) - matmul(
        sin_low, turned_imag.reshape(low_length, -1)
    )
    return flat.reshape(total, second_cells * level_count)


def solve_modes(
    real_part, imag_part, first_rank, second_rank, first_total, second_total, levels, level_count
):
    low_length = real_part.shape[1] // level_count
    shape_full = (second_total, low_length, level_count)
    wave_second = lax.broadcasted_iota(jnp.int32, shape_full, 0)
    wave_first = second_rank * low_length + lax.broadcasted_iota(jnp.int32, shape_full, 1)
    mode_index = first_rank * level_count + lax.broadcasted_iota(jnp.int32, shape_full, 2)
    eigen = 4.0 * jnp.sin(math.pi / first_total * wave_first.astype(jnp.float32)) ** 2
    eigen = eigen + 4.0 * jnp.sin(math.pi / second_total * wave_second.astype(jnp.float32)) ** 2
    eigen = eigen + 4.0 * jnp.sin(math.pi / (2.0 * levels) * mode_index.astype(jnp.float32)) ** 2
    empty = (wave_first == 0) & (wave_second == 0) & (mode_index == 0)
    factor = jnp.where(empty, 0.0, -1.0 / jnp.where(empty, 1.0, eigen)) / (
        first_total * second_total
    )
    factor = factor.reshape(second_total, low_length * level_count)
    return (real_part * factor, imag_part * factor)


def fold_half(real_part, imag_part, level_count):
    high_count = real_part.shape[0]
    second_cells = real_part.shape[1]
    low_length = real_part.shape[2] // level_count
    half_high = high_count // 2
    half_low = low_length // 2
    nyquist = real_part[half_high, :, :level_count]

    def halve(values):
        kept = values[:half_high].reshape(half_high, second_cells, 2, half_low * level_count)
        return kept.transpose(0, 2, 1, 3).reshape(high_count, second_cells, half_low * level_count)

    kept_real = halve(real_part)
    kept_imag = halve(imag_part).at[0, :, :level_count].set(nyquist)
    return (kept_real, kept_imag)


def solve_half(
    real_part, imag_part, first_rank, second_rank, first_total, second_total, levels, level_count
):
    packed_real = real_part[:, :level_count]
    packed_imag = imag_part[:, :level_count]
    mirror_real = jnp.roll(packed_real[::-1], 1, axis=0)
    mirror_imag = jnp.roll(packed_imag[::-1], 1, axis=0)
    zero_real = 0.5 * (packed_real + mirror_real)
    zero_imag = 0.5 * (packed_imag - mirror_imag)
    nyquist_real = 0.5 * (packed_imag + mirror_imag)
    nyquist_imag = -0.5 * (packed_real - mirror_real)
    first_block = second_rank == 0
    real_part = jnp.where(first_block, real_part.at[:, :level_count].set(zero_real), real_part)
    imag_part = jnp.where(first_block, imag_part.at[:, :level_count].set(zero_imag), imag_part)
    solved_real, solved_imag = solve_modes(
        real_part,
        imag_part,
        first_rank,
        second_rank,
        first_total,
        second_total,
        levels,
        level_count,
    )
    wave_second = lax.broadcasted_iota(jnp.int32, (second_total, level_count), 0)
    mode_index = first_rank * level_count + lax.broadcasted_iota(
        jnp.int32, (second_total, level_count), 1
    )
    eigen = 4.0 + 4.0 * jnp.sin(math.pi / second_total * wave_second.astype(jnp.float32)) ** 2
    eigen = eigen + 4.0 * jnp.sin(math.pi / (2.0 * levels) * mode_index.astype(jnp.float32)) ** 2
    nyquist_factor = -1.0 / eigen / (first_total * second_total)
    solved_nyquist_real = nyquist_real * nyquist_factor
    solved_nyquist_imag = nyquist_imag * nyquist_factor
    joined_real = solved_real[:, :level_count] - solved_nyquist_imag
    joined_imag = solved_imag[:, :level_count] + solved_nyquist_real
    solved_real = jnp.where(
        first_block, solved_real.at[:, :level_count].set(joined_real), solved_real
    )
    solved_imag = jnp.where(
        first_block, solved_imag.at[:, :level_count].set(joined_imag), solved_imag
    )
    return (solved_real, solved_imag)


def unfold_half(real_part, imag_part, level_count):
    high_count = real_part.shape[0]
    second_cells = real_part.shape[1]
    half_low = real_part.shape[2] // level_count
    half_high = high_count // 2
    low_length = 2 * half_low

    def unhalve(values):
        shaped = values.reshape(half_high, 2, second_cells, half_low * level_count)
        return shaped.transpose(0, 2, 1, 3).reshape(
            half_high, second_cells, low_length * level_count
        )

    lower_real = unhalve(real_part)
    lower_imag = unhalve(imag_part)
    zero_line = lower_real[0, :, :level_count]
    nyquist_line = lower_imag[0, :, :level_count]
    upper = jnp.zeros((high_count - half_high, second_cells, low_length * level_count), jnp.float32)
    full_real = jnp.concatenate([2.0 * lower_real, upper], axis=0)
    full_imag = jnp.concatenate([2.0 * lower_imag, upper], axis=0)
    full_real = (
        full_real.at[0, :, :level_count]
        .set(zero_line)
        .at[half_high, :, :level_count]
        .set(nyquist_line)
    )
    full_imag = full_imag.at[0, :, :level_count].set(0.0)
    return (full_real, full_imag)


def spectral(
    modes,
    first_rank,
    second_rank,
    second_count,
    levels,
    send_out,
    send_across,
    bring_back,
    bring_home,
):
    first_count = modes.shape[0]
    first_cells = modes.shape[1]
    merged = modes.shape[2]
    level_count = levels // first_count
    second_cells = merged // level_count
    first_total = first_count * first_cells
    second_total = second_count * second_cells
    pencil = send_out(modes).reshape(first_total, merged)
    line_real, line_imag = first_forward(pencil, second_count, second_cells, level_count)
    line_real, line_imag = fold_half(line_real, line_imag, level_count)
    across_real, across_imag = send_across(line_real, line_imag)
    across_real = across_real.reshape(second_total, -1)
    across_imag = across_imag.reshape(second_total, -1)
    wave_real, wave_imag = transform_rows(across_real, across_imag, -1.0)
    wave_real, wave_imag = solve_half(
        wave_real,
        wave_imag,
        first_rank,
        second_rank,
        first_total,
        second_total,
        levels,
        level_count,
    )
    back_real, back_imag = transform_rows(wave_real, wave_imag, 1.0)
    home_real, home_imag = bring_back(
        back_real.reshape(1, second_total, -1), back_imag.reshape(1, second_total, -1)
    )
    home_real, home_imag = unfold_half(home_real, home_imag, level_count)
    flat = first_inverse(home_real, home_imag, level_count)
    return bring_home(flat.reshape(1, first_total, merged))


def staged(modes, east_count, north_count, cells_x, cells_y):
    levels = modes.shape[0]
    level_count = levels // east_count

    def send_out(values):
        return lax.all_to_all(values, "px", split_axis=0, concat_axis=1, tiled=True)

    def send_across(real_part, imag_part):
        return (
            lax.all_to_all(real_part, "py", split_axis=0, concat_axis=1, tiled=True),
            lax.all_to_all(imag_part, "py", split_axis=0, concat_axis=1, tiled=True),
        )

    def bring_back(real_part, imag_part):
        return (
            lax.all_to_all(real_part, "py", split_axis=1, concat_axis=0, tiled=True),
            lax.all_to_all(imag_part, "py", split_axis=1, concat_axis=0, tiled=True),
        )

    def bring_home(values):
        return lax.all_to_all(values, "px", split_axis=1, concat_axis=0, tiled=True)

    shaped = modes.reshape(east_count, level_count, cells_x, cells_y).transpose(0, 2, 3, 1)
    result = spectral(
        shaped.reshape(east_count, cells_x, cells_y * level_count),
        lax.axis_index("px"),
        lax.axis_index("py"),
        north_count,
        levels,
        send_out,
        send_across,
        bring_back,
        bring_home,
    )
    result = result.reshape(east_count, cells_x, cells_y, level_count).transpose(0, 3, 1, 2)
    return result.reshape(levels, cells_x * cells_y)


def shards(wind_east, wind_north, wind_up):
    cells_x, cells_y, levels = wind_east.shape
    east_count = lax.axis_size("px")
    north_count = lax.axis_size("py")
    devices = east_count * north_count
    basis_rows = np.ascontiguousarray(cosine_basis(levels).T)
    modes = source_modes((wind_east, wind_north, wind_up), basis_rows)
    if levels == 8 * devices and north_count * cells_y == 128 and cells_x % north_count == 0:
        blocks = modes.reshape(devices, levels // devices, cells_x * cells_y)
        blocks = lax.all_to_all(blocks, ("px", "py"), split_axis=0, concat_axis=0, tiled=True)
        rank = (lax.axis_index("px") * north_count + lax.axis_index("py")).reshape(1)
        blocks = solve_planes(blocks, rank, east_count, north_count, cells_x, cells_y, levels)
        blocks = lax.all_to_all(blocks, ("px", "py"), split_axis=0, concat_axis=0, tiled=True)
        modes = blocks.reshape(levels, cells_x * cells_y)
    else:
        modes = staged(modes, east_count, north_count, cells_x, cells_y)
    return pressure_cells(modes, basis_rows).reshape(cells_x, cells_y, levels)


def solution(mesh):
    return jax.shard_map(
        shards,
        mesh=mesh,
        in_specs=(P("px", "py", None), P("px", "py", None), P("px", "py", None)),
        out_specs=P("px", "py", None),
        check_vma=False,
    )
```

```python
import functools
import math

import jax
import jax.numpy as jnp
import ml_dtypes
import numpy as np
from jax import lax
from jax.experimental import pallas as pl
from jax.experimental.pallas import tpu as pltpu
from jax.sharding import PartitionSpec as P

NU_BASE = 0.01
SMAGORINSKY = 0.16
STRAIN_FLOOR = 1.0
TIME_STEP = 0.25
HALO = 3
ROWS = 4
EARLY = 4
CHUNKS = 2
LANES = 128
F32 = jnp.float32
BF16 = jnp.bfloat16
DCT_PARTS = 3
NORTH_PARTS = 3
EAST_PARTS = 3
INVERSE = 2
KERNEL_VMEM = pltpu.CompilerParams(vmem_limit_bytes=24 * 2**20)


def cosine_basis(levels):
    level = np.arange(levels, dtype=np.int64)[:, None]
    mode = np.arange(levels, dtype=np.int64)[None, :]
    radians = math.pi / (2.0 * levels) * ((2 * level + 1) * mode % (4 * levels))
    weight = np.where(mode == 0, math.sqrt(1.0 / levels), math.sqrt(2.0 / levels))
    return (weight * np.cos(radians)).astype(np.float32)


def fourier_basis(length):
    cell = np.arange(length)
    half = length // 2
    columns = [np.full(length, math.sqrt(1.0 / length))]
    waves = [0]
    for wave in range(1, half):
        angle = 2.0 * math.pi * (cell * wave % length) / length
        columns += [math.sqrt(2.0 / length) * np.cos(angle), math.sqrt(2.0 / length) * np.sin(angle)]
        waves += [wave, wave]
    columns.append(math.sqrt(1.0 / length) * (1.0 - 2.0 * (cell % 2)))
    waves.append(half)
    eigen = 4.0 * np.sin(math.pi / length * np.array(waves)) ** 2
    return np.stack(columns, axis=1).astype(np.float32), eigen.astype(np.float32)


def mode_eigen(levels):
    return (4.0 * np.sin(math.pi / (2.0 * levels) * np.arange(levels)) ** 2).astype(np.float32)


PAIRS = {2: ((0, 0), (0, 1), (1, 0)), 3: ((0, 0), (0, 1), (1, 0), (1, 1), (0, 2), (2, 0))}


def parts_of(values, count, narrow):
    parts = []
    for _ in range(count):
        parts.append(values.astype(narrow))
        values = values - parts[-1].astype(values.dtype)
    return parts


def table_parts(table, axis, count):
    parts = parts_of(table, count, ml_dtypes.bfloat16)
    return np.ascontiguousarray(np.concatenate([parts[t] for t, _ in PAIRS[count]], axis=axis))


def value_parts(values, axis, count):
    parts = parts_of(values, count, BF16)
    return jnp.concatenate([parts[v] for _, v in PAIRS[count]], axis=axis)


def dot(left, right, contract):
    return lax.dot_general(left, right, (contract, ((), ())), preferred_element_type=F32)


def on_chip(values):
    return pltpu.with_memory_space_constraint(values, pltpu.VMEM)


def swaps(axis):
    size = lax.axis_size(axis)
    inner = [(i, i ^ 1) for i in range(size)]
    outer = [(i, (i - 1 if i % 2 == 0 else i + 1) % size) for i in range(size)]
    return inner, outer


def ring(axis):
    size = lax.axis_size(axis)
    up = [(i, (i + 1) % size) for i in range(size)]
    return up, [(j, i) for i, j in up]


def lane_blocks(values):
    return [values[:, i : i + LANES] for i in range(0, values.shape[1], LANES)]


def z_next(values, edge):
    lane = lax.broadcasted_iota(jnp.int32, (values.shape[0], LANES), 1)
    turned = [pltpu.roll(block, LANES - 1, 1) for block in lane_blocks(values)] + [edge]
    last = lane == LANES - 1
    pairs = zip(turned[1:], turned[:-1])
    return jnp.concatenate([jnp.where(last, after, here) for after, here in pairs], axis=1)


def z_prev(values, edge):
    lane = lax.broadcasted_iota(jnp.int32, (values.shape[0], LANES), 1)
    turned = [edge] + [pltpu.roll(block, 1, 1) for block in lane_blocks(values)]
    pairs = zip(turned[:-1], turned[1:])
    return jnp.concatenate([jnp.where(lane == 0, before, here) for before, here in pairs], axis=1)


def y_next(values):
    return pltpu.roll(values, values.shape[0] - 1, 0)


def y_prev(values):
    return pltpu.roll(values, 1, 0)


def eddy(total):
    root = total + 4.0 * STRAIN_FLOOR
    return NU_BASE + (0.5 * SMAGORINSKY) * (root * lax.rsqrt(root))


def visc_plane(x, wind, above, below, visc):
    along_x = [wind[c, x + 1] - wind[c, x - 1] for c in range(3)]
    along_y = [y_next(wind[c, x]) - y_prev(wind[c, x]) for c in range(3)]
    along_z = [above[c, x] - below[c, x] for c in range(3)]
    normal = along_x[0] * along_x[0] + along_y[1] * along_y[1] + along_z[2] * along_z[2]
    xy = along_x[1] + along_y[0]
    xz = along_x[2] + along_z[0]
    yz = along_y[2] + along_z[1]
    visc[x] = eddy((normal + normal) + (xy * xy + xz * xz + yz * yz))


def wind_plane(x, wind, above, below, visc, east, part):
    cells = east.shape[1]
    centre = [wind[c, x] for c in range(3)]
    nu = visc[x]
    lane = lax.broadcasted_iota(jnp.int32, (nu.shape[0], LANES), 1)
    ends = [jnp.where(lane < LANES // 2, u[:, :LANES], u[:, -LANES:]) for u in centre]
    beyond = eddy(2.0 * (ends[2] * ends[2]) + (ends[0] * ends[0] + ends[1] * ends[1]))
    sum_xn = nu + visc[x + 1]
    sum_xp = nu + visc[x - 1]
    sum_yn = nu + y_next(nu)
    sum_yp = nu + y_prev(nu)
    sum_zn = nu + z_next(nu, beyond)
    sum_zp = nu + z_prev(nu, beyond)
    whole = ((sum_xn + sum_xp) + (sum_yn + sum_yp)) + ((sum_zn + sum_zp) - 2.0 / TIME_STEP)
    coef = (
        sum_xn - centre[0],
        sum_xp + centre[0],
        sum_yn - centre[1],
        sum_yp + centre[1],
        sum_zn - centre[2],
        sum_zp + centre[2],
    )

    def one(c, rows):
        u = centre[c]
        total = coef[0][:rows] * wind[c, x + 1, :rows] + coef[1][:rows] * wind[c, x - 1, :rows]
        total += coef[2][:rows] * y_next(u)[:rows] + coef[3][:rows] * y_prev(u)[:rows]
        total += coef[4][:rows] * above[c, x, :rows] + coef[5][:rows] * below[c, x, :rows]
        return total - whole[:rows] * u[:rows]

    east[x] = one(0, cells)
    north = one(1, nu.shape[0])
    up = one(2, cells)
    edge = centre[2][:cells]
    top = sum_zn[:cells, -LANES:] * edge[:, -LANES:]
    bottom = sum_zp[:cells, :LANES] * edge[:, :LANES]
    part[x] = (y_next(north) - y_prev(north))[:cells] + (z_next(up, top) - z_prev(up, bottom))


def store_plane(c, x, plane, wind, above, below):
    none = jnp.zeros((plane.shape[0], LANES), F32)
    wind[c, x] = plane
    above[c, x] = z_next(plane, none)
    below[c, x] = z_prev(plane, none)


def by_parity(odd, body):
    pl.when(odd == 1)(lambda: body(True))
    pl.when(odd == 0)(lambda: body(False))


def each(first, last, body, jump=0, skip=0, unroll=1):
    def step(i, carry):
        body(i + jnp.where(i >= first + jump, skip, 0) if skip else i)
        return carry

    lax.fori_loop(first, last, step, 0, unroll=unroll)


def half_modes(first, source, east, part, basis_ref, modes, half):
    count, cells_y, levels = source.shape
    for i in range(count):
        x = (first + i) % (2 * count) + HALO
        source[i] = part[x] + (east[x + 1] - east[x - 1])
    width = count * cells_y
    flat = source[...].reshape(width, levels)
    result = dot(basis_ref[...], value_parts(flat, 1, DCT_PARTS), ((1,), (1,)))
    modes[:, half * width : (half + 1) * width] = result


def inner_kernel(place_ref, winds_ref, near_ref, far_ref, basis_ref, *refs):
    wind, above, below, visc, east, part, modes, source = refs
    cells_x, cells_y, levels = winds_ref.shape[1:]

    def load(odd):
        after_ref, before_ref = (far_ref, near_ref) if odd else (near_ref, far_ref)

        def plane(x):
            for c in range(3):
                pieces = [winds_ref[c, x], after_ref[c, x], before_ref[c, x]]
                own, after, before = [piece.astype(F32) for piece in pieces]
                whole = jnp.concatenate([own, after, before], axis=0)
                store_plane(c, x + HALO, whole, wind, above, below)

        each(0, cells_x, plane, unroll=4)

    by_parity(place_ref[0] % 2, load)
    first, last = HALO, HALO + cells_x
    each(first + 1, last - 1, lambda x: visc_plane(x, wind, above, below, visc), unroll=2)
    each(first + 2, last - 2, lambda x: wind_plane(x, wind, above, below, visc, east, part), unroll=2)
    half_modes(EARLY, source, east, part, basis_ref, modes, 0)


def outer_kernel(low_ref, high_ref, low_corner_ref, high_corner_ref, basis_ref, *refs):
    wind, above, below, visc, east, part, modes, source = refs[7:]
    levels = wind.shape[3]
    cells_x = skip = wind.shape[1] - 2 * HALO
    row = lax.broadcasted_iota(jnp.int32, (8, levels), 0)

    def load(c):
        for side, ref, corner_ref in ((0, low_ref, low_corner_ref), (1, high_ref, high_corner_ref)):
            nearest = corner_ref[c].astype(F32)
            second = jnp.where(row < 4, pltpu.roll(nearest, 6, 0), pltpu.roll(nearest, 2, 0))
            for i, rest in enumerate((nearest, second, jnp.zeros_like(nearest))):
                index = i if side else HALO - 1 - i
                plane = jnp.concatenate([ref[c, index].astype(F32), rest], axis=0)
                start = HALO + cells_x if side else 0
                store_plane(c, start + index, plane, wind, above, below)

    each(0, 3, load)
    each(1, 7, lambda x: visc_plane(x, wind, above, below, visc), 3, skip - 2, unroll=2)
    each(2, 8, lambda x: wind_plane(x, wind, above, below, visc, east, part), 3, skip - 4, unroll=2)

    half_modes(cells_x - EARLY, source, east, part, basis_ref, modes, 1)


def pack_kernel(place_ref, *refs):
    winds = refs[:3]
    winds_ref, inner_ref, outer_ref, down_ref, up_ref, sems = refs[3:]
    cells_x, cells_y, levels = winds[0].shape
    copies = [
        pltpu.make_async_copy(ref, winds_ref.at[c], sems.at[c]) for c, ref in enumerate(winds)
    ]
    for copy in copies:
        copy.start()
    for copy in copies:
        copy.wait()

    def pack(odd):
        leading_ref, last_ref = (inner_ref, outer_ref) if odd else (outer_ref, inner_ref)
        for c in range(3):
            for x in range(cells_x):
                own = winds_ref[c, x]
                leading_ref[c, x] = own[:ROWS]
                last_ref[c, x] = own[cells_y - ROWS :]

    by_parity(place_ref[0] % 2, pack)
    down_ref[...] = winds_ref[:, :HALO]
    up_ref[...] = winds_ref[:, cells_x - HALO :]


def pack_winds(winds, place):
    cells_x, cells_y, levels = winds[0].shape
    vmem = pl.BlockSpec(memory_space=pltpu.VMEM)
    edge = pltpu.VMEM((3, cells_x, ROWS, levels), BF16)
    side = pltpu.VMEM((3, HALO, cells_y, levels), BF16)
    return pl.pallas_call(
        pack_kernel,
        out_shape=[pltpu.VMEM((3, cells_x, cells_y, levels), BF16), edge, edge, side, side],
        in_specs=[pl.BlockSpec(memory_space=pltpu.SMEM)] + [pl.BlockSpec(memory_space=pl.ANY)] * 3,
        out_specs=[vmem] * 5,
        scratch_shapes=[pltpu.SemaphoreType.DMA((3,))],
        compiler_params=KERNEL_VMEM,
        name="pack_winds",
    )(place, *[pltpu.with_memory_space_constraint(wind, pltpu.HBM) for wind in winds])


def source_modes(winds, place, basis_rows):
    cells_x, cells_y, levels = winds[0].shape
    planes = cells_x + 2 * HALO
    rows = cells_y + 2 * ROWS
    odd_north = place % 2
    place = place.reshape(1)
    stacked, inner_rows, outer_rows, leading, last = pack_winds(winds, place)
    inner, outer = swaps("py")
    up, down = ring("px")
    outer_got = lax.ppermute(outer_rows, "py", outer)
    inner_got = lax.ppermute(inner_rows, "py", inner)
    low = lax.ppermute(last, "px", up)
    high = lax.ppermute(leading, "px", down)

    def corner(first, second):
        near, far = [[v[:, x] for x in (first, second)] for v in (inner_got, outer_got)]
        after = [jnp.where(odd_north == 1, f, n) for n, f in zip(near, far)]
        before = [jnp.where(odd_north == 1, n, f) for n, f in zip(near, far)]
        none = jnp.zeros((3, 2, levels), BF16)
        pieces = [after[0][:, :2], after[1][:, :1], none, before[1][:, 3:], before[0][:, 2:]]
        return jnp.concatenate(pieces, axis=1)

    low_corner = lax.ppermute(corner(cells_x - 1, cells_x - 2), "px", up)
    high_corner = lax.ppermute(corner(0, 1), "px", down)
    vmem = pl.BlockSpec(memory_space=pltpu.VMEM)
    smem = pl.BlockSpec(memory_space=pltpu.SMEM)
    shapes = [pltpu.VMEM((3, planes, rows, levels), F32)] * 3
    shapes += [pltpu.VMEM((planes, rows, levels), F32)]
    shapes += [pltpu.VMEM((planes, cells_y, levels), F32)] * 2
    shapes += [pltpu.VMEM((levels, cells_x * cells_y), F32)]
    scratch = [pltpu.VMEM((cells_x // 2, cells_y, levels), F32)]
    basis = on_chip(table_parts(basis_rows * np.float32(0.0625), 1, DCT_PARTS))
    state = pl.pallas_call(
        inner_kernel,
        out_shape=shapes,
        in_specs=[smem] + [vmem] * 4,
        out_specs=[vmem] * 7,
        scratch_shapes=scratch,
        cost_estimate=pl.CostEstimate(flops=40_000_000, bytes_accessed=6_000_000, transcendentals=0),
        compiler_params=KERNEL_VMEM,
        name="inner_planes",
    )(place, on_chip(stacked), on_chip(inner_got), on_chip(outer_got), basis)
    results = pl.pallas_call(
        outer_kernel,
        out_shape=shapes,
        in_specs=[vmem] * 12,
        out_specs=[vmem] * 7,
        input_output_aliases={5 + i: i for i in range(7)},
        scratch_shapes=scratch,
        compiler_params=KERNEL_VMEM,
        name="outer_planes",
    )(
        on_chip(low),
        on_chip(high),
        on_chip(low_corner),
        on_chip(high_corner),
        basis,
        *[on_chip(part) for part in state],
    )
    return results[6]


def block_transpose(values, width):
    count = len(values)
    values = list(values)
    lane = lax.broadcasted_iota(jnp.int32, values[0].shape, 1) // width
    step = 1
    while step < count:
        odd = (lane & step) != 0
        for i in range(count):
            if i & step:
                continue
            low, high = values[i], values[i + step]
            shift = width * step
            values[i] = jnp.where(odd, pltpu.roll(high, shift, 1), low)
            values[i + step] = jnp.where(odd, high, pltpu.roll(low, low.shape[1] - shift, 1))
        step *= 2
    return values


def solve_kernel(
    east_count, north_count, cells_x, cells_y,
    in_ref, qx_ref, qxt_ref, qy_ref, qyt_ref, ex_ref, ey_ref, em_ref, place_ref, out_ref, work,
):
    total_x = east_count * cells_x
    total_y = north_count * cells_y
    block = in_ref.shape[1]
    groups = cells_x // north_count
    chunk = total_x * block // CHUNKS
    for h in range(CHUNKS):
        pieces = []
        for a in range(h * east_count // CHUNKS, (h + 1) * east_count // CHUNKS):
            for g in range(groups):
                lanes = slice(g * total_y, (g + 1) * total_y)
                got = [in_ref[a * north_count + b, :, lanes] for b in range(north_count)]
                pieces += block_transpose(got, cells_y)
        lines = value_parts(jnp.concatenate(pieces, axis=0), 1, NORTH_PARTS)
        work[h * chunk : (h + 1) * chunk, :] = dot(lines, qy_ref[...], ((1,), (0,)))
    planes = [work[pl.ds(i, total_x, stride=block), :] for i in range(block)]
    waves = dot(qxt_ref[...], value_parts(jnp.concatenate(planes, axis=1), 0, EAST_PARTS), ((1,), (0,)))
    eigen = ex_ref[...] + ey_ref[0:1, :]
    first = place_ref[0] * block
    solved = []
    for i in range(block):
        value = eigen + em_ref[first + i]
        empty = value == 0.0
        factor = jnp.where(empty, 0.0, -1.0 / jnp.where(empty, 1.0, value))
        solved.append(waves[:, i * total_y : (i + 1) * total_y] * factor)
    back = dot(qx_ref[...], value_parts(jnp.concatenate(solved, axis=1), 0, INVERSE), ((1,), (0,)))
    for i in range(block):
        work[pl.ds(i, total_x, stride=block), :] = back[:, i * total_y : (i + 1) * total_y]
    for h in range(CHUNKS):
        lines = value_parts(work[h * chunk : (h + 1) * chunk, :], 1, INVERSE)
        lines = dot(lines, qyt_ref[...], ((1,), (0,)))
        row = 0
        for a in range(h * east_count // CHUNKS, (h + 1) * east_count // CHUNKS):
            for g in range(groups):
                lanes = slice(g * total_y, (g + 1) * total_y)
                pieces = [lines[row + i * block : row + (i + 1) * block] for i in range(north_count)]
                row += north_count * block
                for b, piece in enumerate(block_transpose(pieces, cells_y)):
                    out_ref[a * north_count + b, :, lanes] = piece


def solve_planes(blocks, place, east_count, north_count, cells_x, cells_y, levels):
    total_x = east_count * cells_x
    total_y = north_count * cells_y
    qx, ex = fourier_basis(total_x)
    qy, ey = fourier_basis(total_y)
    qx = np.roll(qx.reshape(east_count, cells_x, total_x), -EARLY, axis=1).reshape(total_x, total_x)
    tables = [
        table_parts(qx, 1, INVERSE),
        table_parts(qx.T, 1, EAST_PARTS),
        table_parts(qy, 0, NORTH_PARTS),
        table_parts(qy.T, 0, INVERSE),
    ]
    tables += [
        np.ascontiguousarray(np.broadcast_to(ex[:, None], (total_x, total_y))),
        np.ascontiguousarray(np.broadcast_to(ey[None, :], (8, total_y))),
    ]
    vmem = pl.BlockSpec(memory_space=pltpu.VMEM)
    smem = pl.BlockSpec(memory_space=pltpu.SMEM)
    return pl.pallas_call(
        functools.partial(solve_kernel, east_count, north_count, cells_x, cells_y),
        out_shape=pltpu.VMEM(blocks.shape, F32),
        in_specs=[vmem] * 7 + [smem] * 2,
        out_specs=vmem,
        scratch_shapes=[pltpu.VMEM((total_x * blocks.shape[1], total_y), F32)],
        compiler_params=KERNEL_VMEM,
        name="solve_planes",
    )(on_chip(blocks), *[on_chip(table) for table in tables], mode_eigen(levels), place.reshape(1))


def pressure_kernel(shift, modes_ref, basis_ref, out_ref, cells, sems):
    total = cells.shape[0]
    half = total // 2
    copies = []

    def send(first, count):
        target = out_ref.at[pl.ds((first + shift) % total, count)]
        copy = pltpu.make_async_copy(cells.at[pl.ds(first, count)], target, sems.at[len(copies)])
        copy.start()
        copies.append(copy)

    for first in (0, half):
        part = value_parts(modes_ref[:, first : first + half], 0, INVERSE)
        cells[first : first + half, :] = dot(part, basis_ref[...], ((0,), (0,)))
        if first:
            send(first, half - shift)
            send(total - shift, shift)
        else:
            send(first, half)
    for copy in copies:
        copy.wait()


def pressure_cells(modes, basis_rows, shift):
    shape = (modes.shape[1], basis_rows.shape[1])
    return pl.pallas_call(
        functools.partial(pressure_kernel, shift),
        out_shape=jax.ShapeDtypeStruct(shape, F32),
        in_specs=[pl.BlockSpec(memory_space=pltpu.VMEM)] * 2,
        out_specs=pl.BlockSpec(memory_space=pl.ANY),
        scratch_shapes=[pltpu.VMEM(shape, F32), pltpu.SemaphoreType.DMA((3,))],
        compiler_params=KERNEL_VMEM,
        name="pressure_cells",
    )(on_chip(modes), on_chip(table_parts(basis_rows, 0, INVERSE)))


def rotation(row_count, col_count, length, direction):
    product = (
        lax.broadcasted_iota(jnp.int32, (row_count, col_count), 0)
        * lax.broadcasted_iota(jnp.int32, (row_count, col_count), 1)
        % length
    )
    radians = 2.0 * math.pi / length * product.astype(jnp.float32)
    return (jnp.cos(radians), direction * jnp.sin(radians))


def matmul(table, operand):
    return jnp.dot(
        table, operand, precision=lax.Precision.HIGHEST, preferred_element_type=jnp.float32
    )


def contract(formula, table, operand):
    return jnp.einsum(
        formula, table, operand, precision=lax.Precision.HIGHEST, preferred_element_type=jnp.float32
    )


def transform_rows(real_part, imag_part, direction):
    length = real_part.shape[0]
    width = real_part.shape[1]
    factor_low = 1
    for candidate in range(1, math.isqrt(length) + 1):
        if length % candidate == 0:
            factor_low = candidate
    factor_high = length // factor_low
    cos_high, sin_high = rotation(factor_high, factor_high, factor_high, direction)
    grid_real = real_part.reshape(factor_high, factor_low * width)
    grid_imag = imag_part.reshape(factor_high, factor_low * width)
    section_real = (matmul(cos_high, grid_real) - matmul(sin_high, grid_imag)).reshape(
        factor_high, factor_low, width
    )
    section_imag = (matmul(cos_high, grid_imag) + matmul(sin_high, grid_real)).reshape(
        factor_high, factor_low, width
    )
    turn_cos, turn_sin = rotation(factor_high, factor_low, length, direction)
    turn_cos = turn_cos[:, :, None]
    turn_sin = turn_sin[:, :, None]
    turned_real = section_real * turn_cos - section_imag * turn_sin
    turned_imag = section_real * turn_sin + section_imag * turn_cos
    cos_low, sin_low = rotation(factor_low, factor_low, factor_low, direction)
    out_real = contract("ca,kar->ckr", cos_low, turned_real) - contract(
        "ca,kar->ckr", sin_low, turned_imag
    )
    out_imag = contract("ca,kar->ckr", cos_low, turned_imag) + contract(
        "ca,kar->ckr", sin_low, turned_real
    )
    return (out_real.reshape(length, width), out_imag.reshape(length, width))


def first_forward(flat, high_count, second_cells, level_count):
    total = flat.shape[0]
    width = flat.shape[1]
    low_length = total // high_count
    grid = flat.reshape(low_length, high_count * width)
    cos_low, sin_low = rotation(low_length, low_length, low_length, -1.0)
    section_real = matmul(cos_low, grid).reshape(low_length, high_count, second_cells, level_count)
    section_imag = matmul(sin_low, grid).reshape(low_length, high_count, second_cells, level_count)
    turn_cos, turn_sin = rotation(low_length, high_count, total, -1.0)
    turn_cos = turn_cos[:, :, None, None]
    turn_sin = turn_sin[:, :, None, None]
    turned_real = section_real * turn_cos - section_imag * turn_sin
    turned_imag = section_real * turn_sin + section_imag * turn_cos
    cos_high, sin_high = rotation(high_count, high_count, high_count, -1.0)
    out_real = contract("ca,kaym->cykm", cos_high, turned_real) - contract(
        "ca,kaym->cykm", sin_high, turned_imag
    )
    out_imag = contract("ca,kaym->cykm", cos_high, turned_imag) + contract(
        "ca,kaym->cykm", sin_high, turned_real
    )
    merged = low_length * level_count
    return (
        out_real.reshape(high_count, second_cells, merged),
        out_imag.reshape(high_count, second_cells, merged),
    )


def first_inverse(real_part, imag_part, level_count):
    high_count = real_part.shape[0]
    second_cells = real_part.shape[1]
    low_length = real_part.shape[2] // level_count
    total = high_count * low_length
    data_real = real_part.reshape(high_count, second_cells, low_length, level_count)
    data_imag = imag_part.reshape(high_count, second_cells, low_length, level_count)
    cos_high, sin_high = rotation(high_count, high_count, high_count, 1.0)
    section_real = contract("ac,cykm->kaym", cos_high, data_real) - contract(
        "ac,cykm->kaym", sin_high, data_imag
    )
    section_imag = contract("ac,cykm->kaym", cos_high, data_imag) + contract(
        "ac,cykm->kaym", sin_high, data_real
    )
    turn_cos, turn_sin = rotation(low_length, high_count, total, 1.0)
    turn_cos = turn_cos[:, :, None, None]
    turn_sin = turn_sin[:, :, None, None]
    turned_real = section_real * turn_cos - section_imag * turn_sin
    turned_imag = section_real * turn_sin + section_imag * turn_cos
    cos_low, sin_low = rotation(low_length, low_length, low_length, 1.0)
    flat = matmul(cos_low, turned_real.reshape(low_length, -1)) - matmul(
        sin_low, turned_imag.reshape(low_length, -1)
    )
    return flat.reshape(total, second_cells * level_count)


def solve_modes(
    real_part, imag_part, first_rank, second_rank, first_total, second_total, levels, level_count
):
    low_length = real_part.shape[1] // level_count
    shape_full = (second_total, low_length, level_count)
    wave_second = lax.broadcasted_iota(jnp.int32, shape_full, 0)
    wave_first = second_rank * low_length + lax.broadcasted_iota(jnp.int32, shape_full, 1)
    mode_index = first_rank * level_count + lax.broadcasted_iota(jnp.int32, shape_full, 2)
    eigen = 4.0 * jnp.sin(math.pi / first_total * wave_first.astype(jnp.float32)) ** 2
    eigen = eigen + 4.0 * jnp.sin(math.pi / second_total * wave_second.astype(jnp.float32)) ** 2
    eigen = eigen + 4.0 * jnp.sin(math.pi / (2.0 * levels) * mode_index.astype(jnp.float32)) ** 2
    empty = (wave_first == 0) & (wave_second == 0) & (mode_index == 0)
    factor = jnp.where(empty, 0.0, -1.0 / jnp.where(empty, 1.0, eigen)) / (
        first_total * second_total
    )
    factor = factor.reshape(second_total, low_length * level_count)
    return (real_part * factor, imag_part * factor)


def fold_half(real_part, imag_part, level_count):
    high_count = real_part.shape[0]
    second_cells = real_part.shape[1]
    low_length = real_part.shape[2] // level_count
    half_high = high_count // 2
    half_low = low_length // 2
    nyquist = real_part[half_high, :, :level_count]

    def halve(values):
        kept = values[:half_high].reshape(half_high, second_cells, 2, half_low * level_count)
        return kept.transpose(0, 2, 1, 3).reshape(high_count, second_cells, half_low * level_count)

    kept_real = halve(real_part)
    kept_imag = halve(imag_part).at[0, :, :level_count].set(nyquist)
    return (kept_real, kept_imag)


def solve_half(
    real_part, imag_part, first_rank, second_rank, first_total, second_total, levels, level_count
):
    packed_real = real_part[:, :level_count]
    packed_imag = imag_part[:, :level_count]
    mirror_real = jnp.roll(packed_real[::-1], 1, axis=0)
    mirror_imag = jnp.roll(packed_imag[::-1], 1, axis=0)
    zero_real = 0.5 * (packed_real + mirror_real)
    zero_imag = 0.5 * (packed_imag - mirror_imag)
    nyquist_real = 0.5 * (packed_imag + mirror_imag)
    nyquist_imag = -0.5 * (packed_real - mirror_real)
    first_block = second_rank == 0
    real_part = jnp.where(first_block, real_part.at[:, :level_count].set(zero_real), real_part)
    imag_part = jnp.where(first_block, imag_part.at[:, :level_count].set(zero_imag), imag_part)
    solved_real, solved_imag = solve_modes(
        real_part,
        imag_part,
        first_rank,
        second_rank,
        first_total,
        second_total,
        levels,
        level_count,
    )
    wave_second = lax.broadcasted_iota(jnp.int32, (second_total, level_count), 0)
    mode_index = first_rank * level_count + lax.broadcasted_iota(
        jnp.int32, (second_total, level_count), 1
    )
    eigen = 4.0 + 4.0 * jnp.sin(math.pi / second_total * wave_second.astype(jnp.float32)) ** 2
    eigen = eigen + 4.0 * jnp.sin(math.pi / (2.0 * levels) * mode_index.astype(jnp.float32)) ** 2
    nyquist_factor = -1.0 / eigen / (first_total * second_total)
    solved_nyquist_real = nyquist_real * nyquist_factor
    solved_nyquist_imag = nyquist_imag * nyquist_factor
    joined_real = solved_real[:, :level_count] - solved_nyquist_imag
    joined_imag = solved_imag[:, :level_count] + solved_nyquist_real
    solved_real = jnp.where(
        first_block, solved_real.at[:, :level_count].set(joined_real), solved_real
    )
    solved_imag = jnp.where(
        first_block, solved_imag.at[:, :level_count].set(joined_imag), solved_imag
    )
    return (solved_real, solved_imag)


def unfold_half(real_part, imag_part, level_count):
    high_count = real_part.shape[0]
    second_cells = real_part.shape[1]
    half_low = real_part.shape[2] // level_count
    half_high = high_count // 2
    low_length = 2 * half_low

    def unhalve(values):
        shaped = values.reshape(half_high, 2, second_cells, half_low * level_count)
        return shaped.transpose(0, 2, 1, 3).reshape(
            half_high, second_cells, low_length * level_count
        )

    lower_real = unhalve(real_part)
    lower_imag = unhalve(imag_part)
    zero_line = lower_real[0, :, :level_count]
    nyquist_line = lower_imag[0, :, :level_count]
    upper = jnp.zeros((high_count - half_high, second_cells, low_length * level_count), jnp.float32)
    full_real = jnp.concatenate([2.0 * lower_real, upper], axis=0)
    full_imag = jnp.concatenate([2.0 * lower_imag, upper], axis=0)
    full_real = (
        full_real.at[0, :, :level_count]
        .set(zero_line)
        .at[half_high, :, :level_count]
        .set(nyquist_line)
    )
    full_imag = full_imag.at[0, :, :level_count].set(0.0)
    return (full_real, full_imag)


def spectral(
    modes,
    first_rank,
    second_rank,
    second_count,
    levels,
    send_out,
    send_across,
    bring_back,
    bring_home,
):
    first_count = modes.shape[0]
    first_cells = modes.shape[1]
    merged = modes.shape[2]
    level_count = levels // first_count
    second_cells = merged // level_count
    first_total = first_count * first_cells
    second_total = second_count * second_cells
    pencil = send_out(modes).reshape(first_total, merged)
    line_real, line_imag = first_forward(pencil, second_count, second_cells, level_count)
    line_real, line_imag = fold_half(line_real, line_imag, level_count)
    across_real, across_imag = send_across(line_real, line_imag)
    across_real = across_real.reshape(second_total, -1)
    across_imag = across_imag.reshape(second_total, -1)
    wave_real, wave_imag = transform_rows(across_real, across_imag, -1.0)
    wave_real, wave_imag = solve_half(
        wave_real,
        wave_imag,
        first_rank,
        second_rank,
        first_total,
        second_total,
        levels,
        level_count,
    )
    back_real, back_imag = transform_rows(wave_real, wave_imag, 1.0)
    home_real, home_imag = bring_back(
        back_real.reshape(1, second_total, -1), back_imag.reshape(1, second_total, -1)
    )
    home_real, home_imag = unfold_half(home_real, home_imag, level_count)
    flat = first_inverse(home_real, home_imag, level_count)
    return bring_home(flat.reshape(1, first_total, merged))


def staged(modes, east_count, north_count, cells_x, cells_y):
    levels = modes.shape[0]
    level_count = levels // east_count

    def send_out(values):
        return lax.all_to_all(values, "px", split_axis=0, concat_axis=1, tiled=True)

    def send_across(real_part, imag_part):
        return (
            lax.all_to_all(real_part, "py", split_axis=0, concat_axis=1, tiled=True),
            lax.all_to_all(imag_part, "py", split_axis=0, concat_axis=1, tiled=True),
        )

    def bring_back(real_part, imag_part):
        return (
            lax.all_to_all(real_part, "py", split_axis=1, concat_axis=0, tiled=True),
            lax.all_to_all(imag_part, "py", split_axis=1, concat_axis=0, tiled=True),
        )

    def bring_home(values):
        return lax.all_to_all(values, "px", split_axis=1, concat_axis=0, tiled=True)

    shaped = modes.reshape(east_count, level_count, cells_x, cells_y).transpose(0, 2, 3, 1)
    shaped = jnp.roll(shaped, EARLY, axis=1)
    result = spectral(
        shaped.reshape(east_count, cells_x, cells_y * level_count),
        lax.axis_index("px"),
        lax.axis_index("py"),
        north_count,
        levels,
        send_out,
        send_across,
        bring_back,
        bring_home,
    )
    result = jnp.roll(result.reshape(east_count, cells_x, cells_y, level_count), -EARLY, axis=1)
    result = result.transpose(0, 3, 1, 2)
    return result.reshape(levels, cells_x * cells_y)


def shards(wind_east, wind_north, wind_up):
    cells_x, cells_y, levels = wind_east.shape
    east_count = lax.axis_size("px")
    north_count = lax.axis_size("py")
    devices = east_count * north_count
    basis_rows = np.ascontiguousarray(cosine_basis(levels).T)
    north_rank = lax.axis_index("py")
    place = lax.axis_index("px") * north_count + north_rank
    modes = source_modes((wind_east, wind_north, wind_up), place, basis_rows)
    if levels == 8 * devices and north_count * cells_y == 128 and cells_x % north_count == 0:
        blocks = modes.reshape(devices, levels // devices, cells_x * cells_y)
        blocks = lax.all_to_all(blocks, ("px", "py"), split_axis=0, concat_axis=0, tiled=True)
        blocks = solve_planes(blocks, place, east_count, north_count, cells_x, cells_y, levels)
        blocks = lax.all_to_all(blocks, ("px", "py"), split_axis=0, concat_axis=0, tiled=True)
        modes = blocks.reshape(levels, cells_x * cells_y)
    else:
        modes = staged(modes, east_count, north_count, cells_x, cells_y)
    return pressure_cells(modes, basis_rows, EARLY * cells_y).reshape(cells_x, cells_y, levels)


def solution(mesh):
    return jax.shard_map(
        shards,
        mesh=mesh,
        in_specs=(P("px", "py", None), P("px", "py", None), P("px", "py", None)),
        out_specs=P("px", "py", None),
        check_vma=False,
    )
```

```python
import functools
import math

import jax
import jax.numpy as jnp
import ml_dtypes
import numpy as np
from jax import lax
from jax.experimental import pallas as pl
from jax.experimental.pallas import tpu as pltpu
from jax.sharding import PartitionSpec as P

NU_BASE = 0.01
SMAGORINSKY = 0.16
STRAIN_FLOOR = 1.0
TIME_STEP = 0.25
HALO = 3
ROWS = 4
EARLY = 4
CHUNKS = 2
LANES = 128
F32 = jnp.float32
BF16 = jnp.bfloat16
DCT_PARTS = 3
NORTH_PARTS = 3
EAST_PARTS = 3
INVERSE = 2
KERNEL_VMEM = pltpu.CompilerParams(vmem_limit_bytes=24 * 2**20)


def cosine_basis(levels):
    level = np.arange(levels, dtype=np.int64)[:, None]
    mode = np.arange(levels, dtype=np.int64)[None, :]
    radians = math.pi / (2.0 * levels) * ((2 * level + 1) * mode % (4 * levels))
    weight = np.where(mode == 0, math.sqrt(1.0 / levels), math.sqrt(2.0 / levels))
    return (weight * np.cos(radians)).astype(np.float32)


def fourier_basis(length):
    cell = np.arange(length)
    half = length // 2
    columns = [np.full(length, math.sqrt(1.0 / length))]
    waves = [0]
    for wave in range(1, half):
        angle = 2.0 * math.pi * (cell * wave % length) / length
        columns += [math.sqrt(2.0 / length) * np.cos(angle), math.sqrt(2.0 / length) * np.sin(angle)]
        waves += [wave, wave]
    columns.append(math.sqrt(1.0 / length) * (1.0 - 2.0 * (cell % 2)))
    waves.append(half)
    eigen = 4.0 * np.sin(math.pi / length * np.array(waves)) ** 2
    return np.stack(columns, axis=1).astype(np.float32), eigen.astype(np.float32)


def mode_eigen(levels):
    return (4.0 * np.sin(math.pi / (2.0 * levels) * np.arange(levels)) ** 2).astype(np.float32)


PAIRS = {2: ((0, 0), (0, 1), (1, 0)), 3: ((0, 0), (0, 1), (1, 0), (1, 1), (0, 2), (2, 0))}


def parts_of(values, count, narrow):
    parts = []
    for _ in range(count):
        parts.append(values.astype(narrow))
        values = values - parts[-1].astype(values.dtype)
    return parts


def table_parts(table, axis, count):
    parts = parts_of(table, count, ml_dtypes.bfloat16)
    return np.ascontiguousarray(np.concatenate([parts[t] for t, _ in PAIRS[count]], axis=axis))


def value_parts(values, axis, count):
    parts = parts_of(values, count, BF16)
    return jnp.concatenate([parts[v] for _, v in PAIRS[count]], axis=axis)


def dot(left, right, contract):
    return lax.dot_general(left, right, (contract, ((), ())), preferred_element_type=F32)


def on_chip(values):
    return pltpu.with_memory_space_constraint(values, pltpu.VMEM)


def swaps(axis):
    size = lax.axis_size(axis)
    inner = [(i, i ^ 1) for i in range(size)]
    outer = [(i, (i - 1 if i % 2 == 0 else i + 1) % size) for i in range(size)]
    return inner, outer


def ring(axis):
    size = lax.axis_size(axis)
    up = [(i, (i + 1) % size) for i in range(size)]
    return up, [(j, i) for i, j in up]


def lane_blocks(values):
    return [values[:, i : i + LANES] for i in range(0, values.shape[1], LANES)]


def z_next(values, edge):
    lane = lax.broadcasted_iota(jnp.int32, (values.shape[0], LANES), 1)
    turned = [pltpu.roll(block, LANES - 1, 1) for block in lane_blocks(values)] + [edge]
    last = lane == LANES - 1
    pairs = zip(turned[1:], turned[:-1])
    return jnp.concatenate([jnp.where(last, after, here) for after, here in pairs], axis=1)


def z_prev(values, edge):
    lane = lax.broadcasted_iota(jnp.int32, (values.shape[0], LANES), 1)
    turned = [edge] + [pltpu.roll(block, 1, 1) for block in lane_blocks(values)]
    pairs = zip(turned[:-1], turned[1:])
    return jnp.concatenate([jnp.where(lane == 0, before, here) for before, here in pairs], axis=1)


def y_next(values):
    return pltpu.roll(values, values.shape[0] - 1, 0)


def y_prev(values):
    return pltpu.roll(values, 1, 0)


def eddy(total):
    root = total + 4.0 * STRAIN_FLOOR
    return NU_BASE + (0.5 * SMAGORINSKY) * (root * lax.rsqrt(root))


def visc_plane(x, wind, above, below, visc):
    along_x = [wind[c, x + 1] - wind[c, x - 1] for c in range(3)]
    along_y = [y_next(wind[c, x]) - y_prev(wind[c, x]) for c in range(3)]
    along_z = [above[c, x] - below[c, x] for c in range(3)]
    normal = along_x[0] * along_x[0] + along_y[1] * along_y[1] + along_z[2] * along_z[2]
    xy = along_x[1] + along_y[0]
    xz = along_x[2] + along_z[0]
    yz = along_y[2] + along_z[1]
    visc[x] = eddy((normal + normal) + (xy * xy + xz * xz + yz * yz))


def wind_plane(x, wind, above, below, visc, east, part):
    cells = east.shape[1]
    centre = [wind[c, x] for c in range(3)]
    nu = visc[x]
    lane = lax.broadcasted_iota(jnp.int32, (nu.shape[0], LANES), 1)
    ends = [jnp.where(lane < LANES // 2, u[:, :LANES], u[:, -LANES:]) for u in centre]
    beyond = eddy(2.0 * (ends[2] * ends[2]) + (ends[0] * ends[0] + ends[1] * ends[1]))
    sum_xn = nu + visc[x + 1]
    sum_xp = nu + visc[x - 1]
    sum_yn = nu + y_next(nu)
    sum_yp = nu + y_prev(nu)
    sum_zn = nu + z_next(nu, beyond)
    sum_zp = nu + z_prev(nu, beyond)
    whole = ((sum_xn + sum_xp) + (sum_yn + sum_yp)) + ((sum_zn + sum_zp) - 2.0 / TIME_STEP)
    coef = (
        sum_xn - centre[0],
        sum_xp + centre[0],
        sum_yn - centre[1],
        sum_yp + centre[1],
        sum_zn - centre[2],
        sum_zp + centre[2],
    )

    def one(c, rows):
        u = centre[c]
        total = coef[0][:rows] * wind[c, x + 1, :rows] + coef[1][:rows] * wind[c, x - 1, :rows]
        total += coef[2][:rows] * y_next(u)[:rows] + coef[3][:rows] * y_prev(u)[:rows]
        total += coef[4][:rows] * above[c, x, :rows] + coef[5][:rows] * below[c, x, :rows]
        return total - whole[:rows] * u[:rows]

    east[x] = one(0, cells)
    north = one(1, nu.shape[0])
    up = one(2, cells)
    edge = centre[2][:cells]
    top = sum_zn[:cells, -LANES:] * edge[:, -LANES:]
    bottom = sum_zp[:cells, :LANES] * edge[:, :LANES]
    part[x] = (y_next(north) - y_prev(north))[:cells] + (z_next(up, top) - z_prev(up, bottom))


def store_plane(c, x, plane, wind, above, below):
    none = jnp.zeros((plane.shape[0], LANES), F32)
    wind[c, x] = plane
    above[c, x] = z_next(plane, none)
    below[c, x] = z_prev(plane, none)


def by_parity(odd, body):
    pl.when(odd == 1)(lambda: body(True))
    pl.when(odd == 0)(lambda: body(False))


def each(first, last, body, jump=0, skip=0, unroll=1):
    def step(i, carry):
        body(i + jnp.where(i >= first + jump, skip, 0) if skip else i)
        return carry

    lax.fori_loop(first, last, step, 0, unroll=unroll)


def half_modes(first, source, east, part, basis_ref, modes, half):
    count, cells_y, levels = source.shape
    for i in range(count):
        x = (first + i) % (2 * count) + HALO
        source[i] = part[x] + (east[x + 1] - east[x - 1])
    width = count * cells_y
    flat = source[...].reshape(width, levels)
    result = dot(basis_ref[...], value_parts(flat, 1, DCT_PARTS), ((1,), (1,)))
    modes[:, half * width : (half + 1) * width] = result


def inner_kernel(place_ref, winds_ref, near_ref, far_ref, table_ref, *refs):
    wind, above, below, visc, east, part, modes, basis_ref, source, sem = refs
    fetch = pltpu.make_async_copy(table_ref, basis_ref, sem)
    fetch.start()
    cells_x, cells_y, levels = winds_ref.shape[1:]

    def load(odd):
        after_ref, before_ref = (far_ref, near_ref) if odd else (near_ref, far_ref)

        def plane(x):
            for c in range(3):
                pieces = [winds_ref[c, x], after_ref[c, x], before_ref[c, x]]
                own, after, before = [piece.astype(F32) for piece in pieces]
                whole = jnp.concatenate([own, after, before], axis=0)
                store_plane(c, x + HALO, whole, wind, above, below)

        each(0, cells_x, plane, unroll=4)

    by_parity(place_ref[0] // lax.axis_size("px") % 2, load)
    first, last = HALO, HALO + cells_x
    each(first + 1, last - 1, lambda x: visc_plane(x, wind, above, below, visc), unroll=2)
    each(first + 2, last - 2, lambda x: wind_plane(x, wind, above, below, visc, east, part), unroll=2)
    fetch.wait()
    half_modes(EARLY, source, east, part, basis_ref, modes, 0)


def outer_kernel(low_ref, high_ref, low_corner_ref, high_corner_ref, basis_ref, *refs):
    wind, above, below, visc, east, part, modes, source = refs[7:]
    levels = wind.shape[3]
    cells_x = skip = wind.shape[1] - 2 * HALO
    row = lax.broadcasted_iota(jnp.int32, (8, levels), 0)

    def load(c):
        for side, ref, corner_ref in ((0, low_ref, low_corner_ref), (1, high_ref, high_corner_ref)):
            nearest = corner_ref[c].astype(F32)
            second = jnp.where(row < 4, pltpu.roll(nearest, 6, 0), pltpu.roll(nearest, 2, 0))
            for i, rest in enumerate((nearest, second, jnp.zeros_like(nearest))):
                index = i if side else HALO - 1 - i
                plane = jnp.concatenate([ref[c, index].astype(F32), rest], axis=0)
                start = HALO + cells_x if side else 0
                store_plane(c, start + index, plane, wind, above, below)

    each(0, 3, load)
    each(1, 7, lambda x: visc_plane(x, wind, above, below, visc), 3, skip - 2, unroll=2)
    each(2, 8, lambda x: wind_plane(x, wind, above, below, visc, east, part), 3, skip - 4, unroll=2)

    half_modes(cells_x - EARLY, source, east, part, basis_ref, modes, 1)


def pack_kernel(place_ref, *refs):
    winds = refs[:3]
    winds_ref, inner_ref, outer_ref, down_ref, up_ref, sems = refs[3:]
    cells_x, cells_y, levels = winds[0].shape
    copies = [
        pltpu.make_async_copy(ref, winds_ref.at[c], sems.at[c]) for c, ref in enumerate(winds)
    ]
    for copy in copies:
        copy.start()
    for copy in copies:
        copy.wait()

    def pack(odd):
        leading_ref, last_ref = (inner_ref, outer_ref) if odd else (outer_ref, inner_ref)
        for c in range(3):
            for x in range(cells_x):
                own = winds_ref[c, x]
                leading_ref[c, x] = own[:ROWS]
                last_ref[c, x] = own[cells_y - ROWS :]

    by_parity(place_ref[0] // lax.axis_size("px") % 2, pack)
    down_ref[...] = winds_ref[:, :HALO]
    up_ref[...] = winds_ref[:, cells_x - HALO :]


def pack_winds(winds, place):
    cells_x, cells_y, levels = winds[0].shape
    vmem = pl.BlockSpec(memory_space=pltpu.VMEM)
    edge = pltpu.VMEM((3, cells_x, ROWS, levels), BF16)
    side = pltpu.VMEM((3, HALO, cells_y, levels), BF16)
    return pl.pallas_call(
        pack_kernel,
        out_shape=[pltpu.VMEM((3, cells_x, cells_y, levels), BF16), edge, edge, side, side],
        in_specs=[pl.BlockSpec(memory_space=pltpu.SMEM)] + [pl.BlockSpec(memory_space=pl.ANY)] * 3,
        out_specs=[vmem] * 5,
        scratch_shapes=[pltpu.SemaphoreType.DMA((3,))],
        compiler_params=KERNEL_VMEM,
        name="pack_winds",
    )(place, *[pltpu.with_memory_space_constraint(wind, pltpu.HBM) for wind in winds])


def source_modes(winds, place, basis_rows):
    cells_x, cells_y, levels = winds[0].shape
    planes = cells_x + 2 * HALO
    rows = cells_y + 2 * ROWS
    odd_north = place // lax.axis_size("px") % 2
    place = place.reshape(1)
    stacked, inner_rows, outer_rows, leading, last = pack_winds(winds, place)
    inner, outer = swaps("py")
    up, down = ring("px")
    outer_got = lax.ppermute(outer_rows, "py", outer)
    inner_got = lax.ppermute(inner_rows, "py", inner)
    low = lax.ppermute(last, "px", up)
    high = lax.ppermute(leading, "px", down)

    def corner(first, second):
        near, far = [[v[:, x] for x in (first, second)] for v in (inner_got, outer_got)]
        after = [jnp.where(odd_north == 1, f, n) for n, f in zip(near, far)]
        before = [jnp.where(odd_north == 1, n, f) for n, f in zip(near, far)]
        none = jnp.zeros((3, 2, levels), BF16)
        pieces = [after[0][:, :2], after[1][:, :1], none, before[1][:, 3:], before[0][:, 2:]]
        return jnp.concatenate(pieces, axis=1)

    low_corner = lax.ppermute(corner(cells_x - 1, cells_x - 2), "px", up)
    high_corner = lax.ppermute(corner(0, 1), "px", down)
    vmem = pl.BlockSpec(memory_space=pltpu.VMEM)
    smem = pl.BlockSpec(memory_space=pltpu.SMEM)
    shapes = [pltpu.VMEM((3, planes, rows, levels), F32)] * 3
    shapes += [pltpu.VMEM((planes, rows, levels), F32)]
    shapes += [pltpu.VMEM((planes, cells_y, levels), F32)] * 2
    shapes += [pltpu.VMEM((levels, cells_x * cells_y), F32)]
    scratch = [pltpu.VMEM((cells_x // 2, cells_y, levels), F32)]
    basis = table_parts(basis_rows * np.float32(0.0625), 1, DCT_PARTS)
    state = pl.pallas_call(
        inner_kernel,
        out_shape=shapes + [pltpu.VMEM(basis.shape, BF16)],
        in_specs=[smem] + [vmem] * 3 + [pl.BlockSpec(memory_space=pl.ANY)],
        out_specs=[vmem] * 8,
        scratch_shapes=scratch + [pltpu.SemaphoreType.DMA],
        cost_estimate=pl.CostEstimate(flops=40_000_000, bytes_accessed=6_000_000, transcendentals=0),
        compiler_params=KERNEL_VMEM,
        name="inner_planes",
    )(
        place,
        *[on_chip(got) for got in (stacked, inner_got, outer_got)],
        pltpu.with_memory_space_constraint(basis, pltpu.HBM),
    )
    results = pl.pallas_call(
        outer_kernel,
        out_shape=shapes,
        in_specs=[vmem] * 12,
        out_specs=[vmem] * 7,
        input_output_aliases={5 + i: i for i in range(7)},
        scratch_shapes=scratch,
        compiler_params=KERNEL_VMEM,
        name="outer_planes",
    )(
        on_chip(low),
        on_chip(high),
        on_chip(low_corner),
        on_chip(high_corner),
        on_chip(state[7]),
        *[on_chip(part) for part in state[:7]],
    )
    return results[6]


def block_transpose(values, width):
    count = len(values)
    values = list(values)
    lane = lax.broadcasted_iota(jnp.int32, values[0].shape, 1) // width
    step = 1
    while step < count:
        odd = (lane & step) != 0
        for i in range(count):
            if i & step:
                continue
            low, high = values[i], values[i + step]
            shift = width * step
            values[i] = jnp.where(odd, pltpu.roll(high, shift, 1), low)
            values[i + step] = jnp.where(odd, high, pltpu.roll(low, low.shape[1] - shift, 1))
        step *= 2
    return values


def solve_kernel(
    east_count, north_count, cells_x, cells_y,
    in_ref, qx_ref, qxt_ref, qy_ref, qyt_ref, ex_ref, ey_ref, em_ref, place_ref, out_ref, work,
):
    total_x = east_count * cells_x
    total_y = north_count * cells_y
    block = in_ref.shape[1]
    groups = cells_x // north_count
    chunk = total_x * block // CHUNKS
    for h in range(CHUNKS):
        pieces = []
        for a in range(h * east_count // CHUNKS, (h + 1) * east_count // CHUNKS):
            for g in range(groups):
                lanes = slice(g * total_y, (g + 1) * total_y)
                got = [in_ref[b * east_count + a, :, lanes] for b in range(north_count)]
                pieces += block_transpose(got, cells_y)
        lines = value_parts(jnp.concatenate(pieces, axis=0), 1, NORTH_PARTS)
        work[h * chunk : (h + 1) * chunk, :] = dot(lines, qy_ref[...], ((1,), (0,)))
    planes = [work[pl.ds(i, total_x, stride=block), :] for i in range(block)]
    waves = dot(qxt_ref[...], value_parts(jnp.concatenate(planes, axis=1), 0, EAST_PARTS), ((1,), (0,)))
    eigen = ex_ref[...] + ey_ref[0:1, :]
    first = place_ref[0] * block
    solved = []
    for i in range(block):
        value = eigen + em_ref[first + i]
        empty = value == 0.0
        factor = jnp.where(empty, 0.0, -1.0 / jnp.where(empty, 1.0, value))
        solved.append(waves[:, i * total_y : (i + 1) * total_y] * factor)
    back = dot(qx_ref[...], value_parts(jnp.concatenate(solved, axis=1), 0, INVERSE), ((1,), (0,)))
    for i in range(block):
        work[pl.ds(i, total_x, stride=block), :] = back[:, i * total_y : (i + 1) * total_y]
    for h in range(CHUNKS):
        lines = value_parts(work[h * chunk : (h + 1) * chunk, :], 1, INVERSE)
        lines = dot(lines, qyt_ref[...], ((1,), (0,)))
        row = 0
        for a in range(h * east_count // CHUNKS, (h + 1) * east_count // CHUNKS):
            for g in range(groups):
                lanes = slice(g * total_y, (g + 1) * total_y)
                pieces = [lines[row + i * block : row + (i + 1) * block] for i in range(north_count)]
                row += north_count * block
                for b, piece in enumerate(block_transpose(pieces, cells_y)):
                    out_ref[b * east_count + a, :, lanes] = piece


def solve_planes(blocks, place, east_count, north_count, cells_x, cells_y, levels):
    total_x = east_count * cells_x
    total_y = north_count * cells_y
    qx, ex = fourier_basis(total_x)
    qy, ey = fourier_basis(total_y)
    qx = np.roll(qx.reshape(east_count, cells_x, total_x), -EARLY, axis=1).reshape(total_x, total_x)
    tables = [
        table_parts(qx, 1, INVERSE),
        table_parts(qx.T, 1, EAST_PARTS),
        table_parts(qy, 0, NORTH_PARTS),
        table_parts(qy.T, 0, INVERSE),
    ]
    tables += [
        np.ascontiguousarray(np.broadcast_to(ex[:, None], (total_x, total_y))),
        np.ascontiguousarray(np.broadcast_to(ey[None, :], (8, total_y))),
    ]
    vmem = pl.BlockSpec(memory_space=pltpu.VMEM)
    smem = pl.BlockSpec(memory_space=pltpu.SMEM)
    return pl.pallas_call(
        functools.partial(solve_kernel, east_count, north_count, cells_x, cells_y),
        out_shape=pltpu.VMEM(blocks.shape, F32),
        in_specs=[vmem] * 7 + [smem] * 2,
        out_specs=vmem,
        scratch_shapes=[pltpu.VMEM((total_x * blocks.shape[1], total_y), F32)],
        compiler_params=KERNEL_VMEM,
        name="solve_planes",
    )(on_chip(blocks), *[on_chip(table) for table in tables], mode_eigen(levels), place.reshape(1))


def pressure_kernel(shift, modes_ref, basis_ref, out_ref, cells, sems):
    total = cells.shape[0]
    half = total // 2
    copies = []

    def send(first, count):
        target = out_ref.at[pl.ds((first + shift) % total, count)]
        copy = pltpu.make_async_copy(cells.at[pl.ds(first, count)], target, sems.at[len(copies)])
        copy.start()
        copies.append(copy)

    for first in (0, half):
        part = value_parts(modes_ref[:, first : first + half], 0, INVERSE)
        cells[first : first + half, :] = dot(part, basis_ref[...], ((0,), (0,)))
        if first:
            send(first, half - shift)
            send(total - shift, shift)
        else:
            send(first, half)
    for copy in copies:
        copy.wait()


def pressure_cells(modes, basis_rows, shift):
    shape = (modes.shape[1], basis_rows.shape[1])
    return pl.pallas_call(
        functools.partial(pressure_kernel, shift),
        out_shape=jax.ShapeDtypeStruct(shape, F32),
        in_specs=[pl.BlockSpec(memory_space=pltpu.VMEM)] * 2,
        out_specs=pl.BlockSpec(memory_space=pl.ANY),
        scratch_shapes=[pltpu.VMEM(shape, F32), pltpu.SemaphoreType.DMA((3,))],
        compiler_params=KERNEL_VMEM,
        name="pressure_cells",
    )(on_chip(modes), on_chip(table_parts(basis_rows, 0, INVERSE)))


def rotation(row_count, col_count, length, direction):
    product = (
        lax.broadcasted_iota(jnp.int32, (row_count, col_count), 0)
        * lax.broadcasted_iota(jnp.int32, (row_count, col_count), 1)
        % length
    )
    radians = 2.0 * math.pi / length * product.astype(jnp.float32)
    return (jnp.cos(radians), direction * jnp.sin(radians))


def matmul(table, operand):
    return jnp.dot(
        table, operand, precision=lax.Precision.HIGHEST, preferred_element_type=jnp.float32
    )


def contract(formula, table, operand):
    return jnp.einsum(
        formula, table, operand, precision=lax.Precision.HIGHEST, preferred_element_type=jnp.float32
    )


def transform_rows(real_part, imag_part, direction):
    length = real_part.shape[0]
    width = real_part.shape[1]
    factor_low = 1
    for candidate in range(1, math.isqrt(length) + 1):
        if length % candidate == 0:
            factor_low = candidate
    factor_high = length // factor_low
    cos_high, sin_high = rotation(factor_high, factor_high, factor_high, direction)
    grid_real = real_part.reshape(factor_high, factor_low * width)
    grid_imag = imag_part.reshape(factor_high, factor_low * width)
    section_real = (matmul(cos_high, grid_real) - matmul(sin_high, grid_imag)).reshape(
        factor_high, factor_low, width
    )
    section_imag = (matmul(cos_high, grid_imag) + matmul(sin_high, grid_real)).reshape(
        factor_high, factor_low, width
    )
    turn_cos, turn_sin = rotation(factor_high, factor_low, length, direction)
    turn_cos = turn_cos[:, :, None]
    turn_sin = turn_sin[:, :, None]
    turned_real = section_real * turn_cos - section_imag * turn_sin
    turned_imag = section_real * turn_sin + section_imag * turn_cos
    cos_low, sin_low = rotation(factor_low, factor_low, factor_low, direction)
    out_real = contract("ca,kar->ckr", cos_low, turned_real) - contract(
        "ca,kar->ckr", sin_low, turned_imag
    )
    out_imag = contract("ca,kar->ckr", cos_low, turned_imag) + contract(
        "ca,kar->ckr", sin_low, turned_real
    )
    return (out_real.reshape(length, width), out_imag.reshape(length, width))


def first_forward(flat, high_count, second_cells, level_count):
    total = flat.shape[0]
    width = flat.shape[1]
    low_length = total // high_count
    grid = flat.reshape(low_length, high_count * width)
    cos_low, sin_low = rotation(low_length, low_length, low_length, -1.0)
    section_real = matmul(cos_low, grid).reshape(low_length, high_count, second_cells, level_count)
    section_imag = matmul(sin_low, grid).reshape(low_length, high_count, second_cells, level_count)
    turn_cos, turn_sin = rotation(low_length, high_count, total, -1.0)
    turn_cos = turn_cos[:, :, None, None]
    turn_sin = turn_sin[:, :, None, None]
    turned_real = section_real * turn_cos - section_imag * turn_sin
    turned_imag = section_real * turn_sin + section_imag * turn_cos
    cos_high, sin_high = rotation(high_count, high_count, high_count, -1.0)
    out_real = contract("ca,kaym->cykm", cos_high, turned_real) - contract(
        "ca,kaym->cykm", sin_high, turned_imag
    )
    out_imag = contract("ca,kaym->cykm", cos_high, turned_imag) + contract(
        "ca,kaym->cykm", sin_high, turned_real
    )
    merged = low_length * level_count
    return (
        out_real.reshape(high_count, second_cells, merged),
        out_imag.reshape(high_count, second_cells, merged),
    )


def first_inverse(real_part, imag_part, level_count):
    high_count = real_part.shape[0]
    second_cells = real_part.shape[1]
    low_length = real_part.shape[2] // level_count
    total = high_count * low_length
    data_real = real_part.reshape(high_count, second_cells, low_length, level_count)
    data_imag = imag_part.reshape(high_count, second_cells, low_length, level_count)
    cos_high, sin_high = rotation(high_count, high_count, high_count, 1.0)
    section_real = contract("ac,cykm->kaym", cos_high, data_real) - contract(
        "ac,cykm->kaym", sin_high, data_imag
    )
    section_imag = contract("ac,cykm->kaym", cos_high, data_imag) + contract(
        "ac,cykm->kaym", sin_high, data_real
    )
    turn_cos, turn_sin = rotation(low_length, high_count, total, 1.0)
    turn_cos = turn_cos[:, :, None, None]
    turn_sin = turn_sin[:, :, None, None]
    turned_real = section_real * turn_cos - section_imag * turn_sin
    turned_imag = section_real * turn_sin + section_imag * turn_cos
    cos_low, sin_low = rotation(low_length, low_length, low_length, 1.0)
    flat = matmul(cos_low, turned_real.reshape(low_length, -1)) - matmul(
        sin_low, turned_imag.reshape(low_length, -1)
    )
    return flat.reshape(total, second_cells * level_count)


def solve_modes(
    real_part, imag_part, first_rank, second_rank, first_total, second_total, levels, level_count
):
    low_length = real_part.shape[1] // level_count
    shape_full = (second_total, low_length, level_count)
    wave_second = lax.broadcasted_iota(jnp.int32, shape_full, 0)
    wave_first = second_rank * low_length + lax.broadcasted_iota(jnp.int32, shape_full, 1)
    mode_index = first_rank * level_count + lax.broadcasted_iota(jnp.int32, shape_full, 2)
    eigen = 4.0 * jnp.sin(math.pi / first_total * wave_first.astype(jnp.float32)) ** 2
    eigen = eigen + 4.0 * jnp.sin(math.pi / second_total * wave_second.astype(jnp.float32)) ** 2
    eigen = eigen + 4.0 * jnp.sin(math.pi / (2.0 * levels) * mode_index.astype(jnp.float32)) ** 2
    empty = (wave_first == 0) & (wave_second == 0) & (mode_index == 0)
    factor = jnp.where(empty, 0.0, -1.0 / jnp.where(empty, 1.0, eigen)) / (
        first_total * second_total
    )
    factor = factor.reshape(second_total, low_length * level_count)
    return (real_part * factor, imag_part * factor)


def fold_half(real_part, imag_part, level_count):
    high_count = real_part.shape[0]
    second_cells = real_part.shape[1]
    low_length = real_part.shape[2] // level_count
    half_high = high_count // 2
    half_low = low_length // 2
    nyquist = real_part[half_high, :, :level_count]

    def halve(values):
        kept = values[:half_high].reshape(half_high, second_cells, 2, half_low * level_count)
        return kept.transpose(0, 2, 1, 3).reshape(high_count, second_cells, half_low * level_count)

    kept_real = halve(real_part)
    kept_imag = halve(imag_part).at[0, :, :level_count].set(nyquist)
    return (kept_real, kept_imag)


def solve_half(
    real_part, imag_part, first_rank, second_rank, first_total, second_total, levels, level_count
):
    packed_real = real_part[:, :level_count]
    packed_imag = imag_part[:, :level_count]
    mirror_real = jnp.roll(packed_real[::-1], 1, axis=0)
    mirror_imag = jnp.roll(packed_imag[::-1], 1, axis=0)
    zero_real = 0.5 * (packed_real + mirror_real)
    zero_imag = 0.5 * (packed_imag - mirror_imag)
    nyquist_real = 0.5 * (packed_imag + mirror_imag)
    nyquist_imag = -0.5 * (packed_real - mirror_real)
    first_block = second_rank == 0
    real_part = jnp.where(first_block, real_part.at[:, :level_count].set(zero_real), real_part)
    imag_part = jnp.where(first_block, imag_part.at[:, :level_count].set(zero_imag), imag_part)
    solved_real, solved_imag = solve_modes(
        real_part,
        imag_part,
        first_rank,
        second_rank,
        first_total,
        second_total,
        levels,
        level_count,
    )
    wave_second = lax.broadcasted_iota(jnp.int32, (second_total, level_count), 0)
    mode_index = first_rank * level_count + lax.broadcasted_iota(
        jnp.int32, (second_total, level_count), 1
    )
    eigen = 4.0 + 4.0 * jnp.sin(math.pi / second_total * wave_second.astype(jnp.float32)) ** 2
    eigen = eigen + 4.0 * jnp.sin(math.pi / (2.0 * levels) * mode_index.astype(jnp.float32)) ** 2
    nyquist_factor = -1.0 / eigen / (first_total * second_total)
    solved_nyquist_real = nyquist_real * nyquist_factor
    solved_nyquist_imag = nyquist_imag * nyquist_factor
    joined_real = solved_real[:, :level_count] - solved_nyquist_imag
    joined_imag = solved_imag[:, :level_count] + solved_nyquist_real
    solved_real = jnp.where(
        first_block, solved_real.at[:, :level_count].set(joined_real), solved_real
    )
    solved_imag = jnp.where(
        first_block, solved_imag.at[:, :level_count].set(joined_imag), solved_imag
    )
    return (solved_real, solved_imag)


def unfold_half(real_part, imag_part, level_count):
    high_count = real_part.shape[0]
    second_cells = real_part.shape[1]
    half_low = real_part.shape[2] // level_count
    half_high = high_count // 2
    low_length = 2 * half_low

    def unhalve(values):
        shaped = values.reshape(half_high, 2, second_cells, half_low * level_count)
        return shaped.transpose(0, 2, 1, 3).reshape(
            half_high, second_cells, low_length * level_count
        )

    lower_real = unhalve(real_part)
    lower_imag = unhalve(imag_part)
    zero_line = lower_real[0, :, :level_count]
    nyquist_line = lower_imag[0, :, :level_count]
    upper = jnp.zeros((high_count - half_high, second_cells, low_length * level_count), jnp.float32)
    full_real = jnp.concatenate([2.0 * lower_real, upper], axis=0)
    full_imag = jnp.concatenate([2.0 * lower_imag, upper], axis=0)
    full_real = (
        full_real.at[0, :, :level_count]
        .set(zero_line)
        .at[half_high, :, :level_count]
        .set(nyquist_line)
    )
    full_imag = full_imag.at[0, :, :level_count].set(0.0)
    return (full_real, full_imag)


def spectral(
    modes,
    first_rank,
    second_rank,
    second_count,
    levels,
    send_out,
    send_across,
    bring_back,
    bring_home,
):
    first_count = modes.shape[0]
    first_cells = modes.shape[1]
    merged = modes.shape[2]
    level_count = levels // first_count
    second_cells = merged // level_count
    first_total = first_count * first_cells
    second_total = second_count * second_cells
    pencil = send_out(modes).reshape(first_total, merged)
    line_real, line_imag = first_forward(pencil, second_count, second_cells, level_count)
    line_real, line_imag = fold_half(line_real, line_imag, level_count)
    across_real, across_imag = send_across(line_real, line_imag)
    across_real = across_real.reshape(second_total, -1)
    across_imag = across_imag.reshape(second_total, -1)
    wave_real, wave_imag = transform_rows(across_real, across_imag, -1.0)
    wave_real, wave_imag = solve_half(
        wave_real,
        wave_imag,
        first_rank,
        second_rank,
        first_total,
        second_total,
        levels,
        level_count,
    )
    back_real, back_imag = transform_rows(wave_real, wave_imag, 1.0)
    home_real, home_imag = bring_back(
        back_real.reshape(1, second_total, -1), back_imag.reshape(1, second_total, -1)
    )
    home_real, home_imag = unfold_half(home_real, home_imag, level_count)
    flat = first_inverse(home_real, home_imag, level_count)
    return bring_home(flat.reshape(1, first_total, merged))


def staged(modes, east_count, north_count, cells_x, cells_y):
    levels = modes.shape[0]
    level_count = levels // east_count

    def send_out(values):
        return lax.all_to_all(values, "px", split_axis=0, concat_axis=1, tiled=True)

    def send_across(real_part, imag_part):
        return (
            lax.all_to_all(real_part, "py", split_axis=0, concat_axis=1, tiled=True),
            lax.all_to_all(imag_part, "py", split_axis=0, concat_axis=1, tiled=True),
        )

    def bring_back(real_part, imag_part):
        return (
            lax.all_to_all(real_part, "py", split_axis=1, concat_axis=0, tiled=True),
            lax.all_to_all(imag_part, "py", split_axis=1, concat_axis=0, tiled=True),
        )

    def bring_home(values):
        return lax.all_to_all(values, "px", split_axis=1, concat_axis=0, tiled=True)

    shaped = modes.reshape(east_count, level_count, cells_x, cells_y).transpose(0, 2, 3, 1)
    shaped = jnp.roll(shaped, EARLY, axis=1)
    result = spectral(
        shaped.reshape(east_count, cells_x, cells_y * level_count),
        lax.axis_index("px"),
        lax.axis_index("py"),
        north_count,
        levels,
        send_out,
        send_across,
        bring_back,
        bring_home,
    )
    result = jnp.roll(result.reshape(east_count, cells_x, cells_y, level_count), -EARLY, axis=1)
    result = result.transpose(0, 3, 1, 2)
    return result.reshape(levels, cells_x * cells_y)


def shards(wind_east, wind_north, wind_up):
    cells_x, cells_y, levels = wind_east.shape
    east_count = lax.axis_size("px")
    north_count = lax.axis_size("py")
    devices = east_count * north_count
    basis_rows = np.ascontiguousarray(cosine_basis(levels).T)
    north_rank = lax.axis_index("py")
    place = north_rank * east_count + lax.axis_index("px")
    modes = source_modes((wind_east, wind_north, wind_up), place, basis_rows)
    if levels == 8 * devices and north_count * cells_y == 128 and cells_x % north_count == 0:
        blocks = modes.reshape(devices, levels // devices, cells_x * cells_y)
        blocks = lax.all_to_all(blocks, ("py", "px"), split_axis=0, concat_axis=0, tiled=True)
        blocks = solve_planes(blocks, place, east_count, north_count, cells_x, cells_y, levels)
        blocks = lax.all_to_all(blocks, ("py", "px"), split_axis=0, concat_axis=0, tiled=True)
        modes = blocks.reshape(levels, cells_x * cells_y)
    else:
        modes = staged(modes, east_count, north_count, cells_x, cells_y)
    return pressure_cells(modes, basis_rows, EARLY * cells_y).reshape(cells_x, cells_y, levels)


def solution(mesh):
    return jax.shard_map(
        shards,
        mesh=mesh,
        in_specs=(P("px", "py", None), P("px", "py", None), P("px", "py", None)),
        out_specs=P("px", "py", None),
        check_vma=False,
    )
```

```python
import functools
import math

import jax
import jax.numpy as jnp
import ml_dtypes
import numpy as np
from jax import lax
from jax.experimental import pallas as pl
from jax.experimental.pallas import tpu as pltpu
from jax.sharding import PartitionSpec as P

NU_BASE = 0.01
SMAGORINSKY = 0.16
STRAIN_FLOOR = 1.0
TIME_STEP = 0.25
HALO = 3
ROWS = 4
EARLY = 4
CHUNKS = 2
LANES = 128
F32 = jnp.float32
BF16 = jnp.bfloat16
DCT_PARTS = 3
NORTH_PARTS = 3
EAST_PARTS = 3
INVERSE = 2
KERNEL_VMEM = pltpu.CompilerParams(vmem_limit_bytes=24 * 2**20)


def cosine_basis(levels):
    level = np.arange(levels, dtype=np.int64)[:, None]
    mode = np.arange(levels, dtype=np.int64)[None, :]
    radians = math.pi / (2.0 * levels) * ((2 * level + 1) * mode % (4 * levels))
    weight = np.where(mode == 0, math.sqrt(1.0 / levels), math.sqrt(2.0 / levels))
    return (weight * np.cos(radians)).astype(np.float32)


def fourier_basis(length):
    cell = np.arange(length)
    half = length // 2
    columns = [np.full(length, math.sqrt(1.0 / length))]
    waves = [0]
    for wave in range(1, half):
        angle = 2.0 * math.pi * (cell * wave % length) / length
        columns += [math.sqrt(2.0 / length) * np.cos(angle), math.sqrt(2.0 / length) * np.sin(angle)]
        waves += [wave, wave]
    columns.append(math.sqrt(1.0 / length) * (1.0 - 2.0 * (cell % 2)))
    waves.append(half)
    eigen = 4.0 * np.sin(math.pi / length * np.array(waves)) ** 2
    return np.stack(columns, axis=1).astype(np.float32), eigen.astype(np.float32)


def mode_eigen(levels):
    return (4.0 * np.sin(math.pi / (2.0 * levels) * np.arange(levels)) ** 2).astype(np.float32)


PAIRS = {2: ((0, 0), (0, 1), (1, 0)), 3: ((0, 0), (0, 1), (1, 0), (1, 1), (0, 2), (2, 0))}


def parts_of(values, count, narrow):
    parts = []
    for _ in range(count):
        parts.append(values.astype(narrow))
        values = values - parts[-1].astype(values.dtype)
    return parts


def table_parts(table, axis, count):
    parts = parts_of(table, count, ml_dtypes.bfloat16)
    return np.ascontiguousarray(np.concatenate([parts[t] for t, _ in PAIRS[count]], axis=axis))


def value_parts(values, axis, count):
    parts = parts_of(values, count, BF16)
    return jnp.concatenate([parts[v] for _, v in PAIRS[count]], axis=axis)


def dot(left, right, contract):
    return lax.dot_general(left, right, (contract, ((), ())), preferred_element_type=F32)


def on_chip(values):
    return pltpu.with_memory_space_constraint(values, pltpu.VMEM)


def swaps(axis):
    size = lax.axis_size(axis)
    inner = [(i, i ^ 1) for i in range(size)]
    outer = [(i, (i - 1 if i % 2 == 0 else i + 1) % size) for i in range(size)]
    return inner, outer


def ring(axis):
    size = lax.axis_size(axis)
    up = [(i, (i + 1) % size) for i in range(size)]
    return up, [(j, i) for i, j in up]


def lane_blocks(values):
    return [values[:, i : i + LANES] for i in range(0, values.shape[1], LANES)]


def z_next(values, edge):
    lane = lax.broadcasted_iota(jnp.int32, (values.shape[0], LANES), 1)
    turned = [pltpu.roll(block, LANES - 1, 1) for block in lane_blocks(values)] + [edge]
    last = lane == LANES - 1
    pairs = zip(turned[1:], turned[:-1])
    return jnp.concatenate([jnp.where(last, after, here) for after, here in pairs], axis=1)


def z_prev(values, edge):
    lane = lax.broadcasted_iota(jnp.int32, (values.shape[0], LANES), 1)
    turned = [edge] + [pltpu.roll(block, 1, 1) for block in lane_blocks(values)]
    pairs = zip(turned[:-1], turned[1:])
    return jnp.concatenate([jnp.where(lane == 0, before, here) for before, here in pairs], axis=1)


def y_next(values):
    return pltpu.roll(values, values.shape[0] - 1, 0)


def y_prev(values):
    return pltpu.roll(values, 1, 0)


def eddy(total):
    root = total + 4.0 * STRAIN_FLOOR
    return NU_BASE + (0.5 * SMAGORINSKY) * (root * lax.rsqrt(root))


def visc_plane(x, wind, above, below, visc):
    along_x = [wind[c, x + 1] - wind[c, x - 1] for c in range(3)]
    along_y = [y_next(wind[c, x]) - y_prev(wind[c, x]) for c in range(3)]
    along_z = [above[c, x] - below[c, x] for c in range(3)]
    normal = along_x[0] * along_x[0] + along_y[1] * along_y[1] + along_z[2] * along_z[2]
    xy = along_x[1] + along_y[0]
    xz = along_x[2] + along_z[0]
    yz = along_y[2] + along_z[1]
    visc[x] = eddy((normal + normal) + (xy * xy + xz * xz + yz * yz))


def wind_plane(x, wind, above, below, visc, east, part):
    cells = east.shape[1]
    centre = [wind[c, x] for c in range(3)]
    nu = visc[x]
    lane = lax.broadcasted_iota(jnp.int32, (nu.shape[0], LANES), 1)
    ends = [jnp.where(lane < LANES // 2, u[:, :LANES], u[:, -LANES:]) for u in centre]
    beyond = eddy(2.0 * (ends[2] * ends[2]) + (ends[0] * ends[0] + ends[1] * ends[1]))
    sum_xn = nu + visc[x + 1]
    sum_xp = nu + visc[x - 1]
    sum_yn = nu + y_next(nu)
    sum_yp = nu + y_prev(nu)
    sum_zn = nu + z_next(nu, beyond)
    sum_zp = nu + z_prev(nu, beyond)
    whole = ((sum_xn + sum_xp) + (sum_yn + sum_yp)) + ((sum_zn + sum_zp) - 2.0 / TIME_STEP)
    coef = (
        sum_xn - centre[0],
        sum_xp + centre[0],
        sum_yn - centre[1],
        sum_yp + centre[1],
        sum_zn - centre[2],
        sum_zp + centre[2],
    )

    def one(c, rows):
        u = centre[c]
        total = coef[0][:rows] * wind[c, x + 1, :rows] + coef[1][:rows] * wind[c, x - 1, :rows]
        total += coef[2][:rows] * y_next(u)[:rows] + coef[3][:rows] * y_prev(u)[:rows]
        total += coef[4][:rows] * above[c, x, :rows] + coef[5][:rows] * below[c, x, :rows]
        return total - whole[:rows] * u[:rows]

    east[x] = one(0, cells)
    if part is None:
        return
    north = one(1, nu.shape[0])
    up = one(2, cells)
    edge = centre[2][:cells]
    top = sum_zn[:cells, -LANES:] * edge[:, -LANES:]
    bottom = sum_zp[:cells, :LANES] * edge[:, :LANES]
    part[x] = (y_next(north) - y_prev(north))[:cells] + (z_next(up, top) - z_prev(up, bottom))


def shift_table(levels):
    level = lax.broadcasted_iota(jnp.int32, (levels, levels), 0)
    moved = lax.broadcasted_iota(jnp.int32, (levels, levels), 1)
    tables = [jnp.where(level == moved + step, 1.0, 0.0) for step in (1, -1)]
    return jnp.concatenate(tables, axis=1).astype(BF16)


def store_planes(places, planes, table, wind, above, below):
    rows, levels = planes[0].shape
    stacked = jnp.concatenate(planes, axis=0).astype(BF16)
    moved = dot(stacked, table, ((1,), (0,)))
    for i, ((c, x), plane) in enumerate(zip(places, planes)):
        wind[c, x] = plane
        above[c, x] = moved[i * rows : (i + 1) * rows, :levels]
        below[c, x] = moved[i * rows : (i + 1) * rows, levels:]


def by_parity(odd, body):
    pl.when(odd == 1)(lambda: body(True))
    pl.when(odd == 0)(lambda: body(False))


def each(first, last, body, jump=0, skip=0, unroll=1):
    def step(i, carry):
        body(i + jnp.where(i >= first + jump, skip, 0) if skip else i)
        return carry

    lax.fori_loop(first, last, step, 0, unroll=unroll)


def half_modes(first, source, east, part, basis_ref, modes, half):
    count, cells_y, levels = source.shape
    for i in range(count):
        x = (first + i) % (2 * count) + HALO
        source[i] = part[x] + (east[x + 1] - east[x - 1])
    width = count * cells_y
    flat = source[...].reshape(width, levels)
    result = dot(basis_ref[...], value_parts(flat, 1, DCT_PARTS), ((1,), (1,)))
    modes[:, half * width : (half + 1) * width] = result


def inner_kernel(place_ref, winds_ref, near_ref, far_ref, table_ref, *refs):
    wind, above, below, visc, east, part, modes, basis_ref, table, source, sem = refs
    fetch = pltpu.make_async_copy(table_ref, basis_ref, sem)
    fetch.start()
    cells_x, cells_y, levels = winds_ref.shape[1:]

    table[...] = shift_table(levels)

    def load(odd):
        after_ref, before_ref = (far_ref, near_ref) if odd else (near_ref, far_ref)

        def plane(x):
            for c in range(3):
                pieces = [winds_ref[c, x], after_ref[c, x], before_ref[c, x]]
                whole = jnp.concatenate([piece.astype(F32) for piece in pieces], axis=0)
                none = jnp.zeros((whole.shape[0], LANES), F32)
                wind[c, x + HALO] = whole
                above[c, x + HALO] = z_next(whole, none)
                below[c, x + HALO] = z_prev(whole, none)

        each(0, cells_x, plane, unroll=4)

    by_parity(place_ref[0] // lax.axis_size("px") % 2, load)
    first, last = HALO, HALO + cells_x
    each(first + 1, last - 1, lambda x: visc_plane(x, wind, above, below, visc), unroll=2)
    each(first + 2, last - 2, lambda x: wind_plane(x, wind, above, below, visc, east, part), unroll=2)
    fetch.wait()
    half_modes(EARLY, source, east, part, basis_ref, modes, 0)


def side_kernel(side, planes_ref, corner_ref, table, *refs):
    if side:
        wind, above, below, visc, east, part, modes, source = refs[8:]
        basis_ref = refs[0]
    else:
        wind, above, below, visc, east, part = refs[6:]
    levels = wind.shape[3]
    cells_x = wind.shape[1] - 2 * HALO
    row = lax.broadcasted_iota(jnp.int32, (8, levels), 0)

    places, planes = [], []
    for c in range(3):
        nearest = corner_ref[c].astype(F32)
        second = jnp.where(row < 4, pltpu.roll(nearest, 6, 0), pltpu.roll(nearest, 2, 0))
        for i, rest in enumerate((nearest, second, jnp.zeros_like(nearest))):
            index = i if side else HALO - 1 - i
            planes.append(jnp.concatenate([planes_ref[c, index].astype(F32), rest], axis=0))
            places.append((c, index + (HALO + cells_x if side else 0)))
    store_planes(places, planes, table[...], wind, above, below)
    skip = cells_x + 1 if side else 0
    each(1 + skip, 4 + skip, lambda x: visc_plane(x, wind, above, below, visc), unroll=3)
    first = cells_x + 1 if side else HALO
    each(first, first + 2, lambda x: wind_plane(x, wind, above, below, visc, east, part), unroll=2)
    wind_plane(HALO + cells_x if side else 2, wind, above, below, visc, east, None)
    if side:
        half_modes(cells_x - EARLY, source, east, part, basis_ref, modes, 1)


def pack_kernel(place_ref, *refs):
    winds = refs[:3]
    winds_ref, inner_ref, outer_ref, down_ref, up_ref, sems = refs[3:]
    cells_x, cells_y, levels = winds[0].shape
    copies = [
        pltpu.make_async_copy(ref, winds_ref.at[c], sems.at[c]) for c, ref in enumerate(winds)
    ]
    for copy in copies:
        copy.start()
    for copy in copies:
        copy.wait()

    def pack(odd):
        leading_ref, last_ref = (inner_ref, outer_ref) if odd else (outer_ref, inner_ref)
        for c in range(3):
            for x in range(cells_x):
                own = winds_ref[c, x]
                leading_ref[c, x] = own[:ROWS]
                last_ref[c, x] = own[cells_y - ROWS :]

    by_parity(place_ref[0] // lax.axis_size("px") % 2, pack)
    down_ref[...] = winds_ref[:, :HALO]
    up_ref[...] = winds_ref[:, cells_x - HALO :]


def pack_winds(winds, place):
    cells_x, cells_y, levels = winds[0].shape
    vmem = pl.BlockSpec(memory_space=pltpu.VMEM)
    edge = pltpu.VMEM((3, cells_x, ROWS, levels), BF16)
    side = pltpu.VMEM((3, HALO, cells_y, levels), BF16)
    return pl.pallas_call(
        pack_kernel,
        out_shape=[pltpu.VMEM((3, cells_x, cells_y, levels), BF16), edge, edge, side, side],
        in_specs=[pl.BlockSpec(memory_space=pltpu.SMEM)] + [pl.BlockSpec(memory_space=pl.ANY)] * 3,
        out_specs=[vmem] * 5,
        scratch_shapes=[pltpu.SemaphoreType.DMA((3,))],
        compiler_params=KERNEL_VMEM,
        name="pack_winds",
    )(place, *[pltpu.with_memory_space_constraint(wind, pltpu.HBM) for wind in winds])


def source_modes(winds, place, basis_rows):
    cells_x, cells_y, levels = winds[0].shape
    planes = cells_x + 2 * HALO
    rows = cells_y + 2 * ROWS
    odd_north = place // lax.axis_size("px") % 2
    place = place.reshape(1)
    stacked, inner_rows, outer_rows, leading, last = pack_winds(winds, place)
    inner, outer = swaps("py")
    up, down = ring("px")
    outer_got = lax.ppermute(outer_rows, "py", outer)
    inner_got = lax.ppermute(inner_rows, "py", inner)
    low = lax.ppermute(last, "px", up)
    high = lax.ppermute(leading, "px", down)

    def corner(first, second):
        near, far = [[v[:, x] for x in (first, second)] for v in (inner_got, outer_got)]
        after = [jnp.where(odd_north == 1, f, n) for n, f in zip(near, far)]
        before = [jnp.where(odd_north == 1, n, f) for n, f in zip(near, far)]
        none = jnp.zeros((3, 2, levels), BF16)
        pieces = [after[0][:, :2], after[1][:, :1], none, before[1][:, 3:], before[0][:, 2:]]
        return jnp.concatenate(pieces, axis=1)

    low_corner = lax.ppermute(corner(cells_x - 1, cells_x - 2), "px", up)
    high_corner = lax.ppermute(corner(0, 1), "px", down)
    vmem = pl.BlockSpec(memory_space=pltpu.VMEM)
    smem = pl.BlockSpec(memory_space=pltpu.SMEM)
    shapes = [pltpu.VMEM((3, planes, rows, levels), F32)] * 3
    shapes += [pltpu.VMEM((planes, rows, levels), F32)]
    shapes += [pltpu.VMEM((planes, cells_y, levels), F32)] * 2
    shapes += [pltpu.VMEM((levels, cells_x * cells_y), F32)]
    scratch = [pltpu.VMEM((cells_x // 2, cells_y, levels), F32)]
    basis = table_parts(basis_rows * np.float32(0.0625), 1, DCT_PARTS)
    state = pl.pallas_call(
        inner_kernel,
        out_shape=shapes + [pltpu.VMEM(basis.shape, BF16), pltpu.VMEM((levels, 2 * levels), BF16)],
        in_specs=[smem] + [vmem] * 3 + [pl.BlockSpec(memory_space=pl.ANY)],
        out_specs=[vmem] * 9,
        scratch_shapes=scratch + [pltpu.SemaphoreType.DMA],
        cost_estimate=pl.CostEstimate(flops=40_000_000, bytes_accessed=6_000_000, transcendentals=0),
        compiler_params=KERNEL_VMEM,
        name="inner_planes",
    )(
        place,
        *[on_chip(got) for got in (stacked, inner_got, outer_got)],
        pltpu.with_memory_space_constraint(basis, pltpu.HBM),
    )
    low_state = pl.pallas_call(
        functools.partial(side_kernel, 0),
        out_shape=shapes[:6],
        in_specs=[vmem] * 9,
        out_specs=[vmem] * 6,
        input_output_aliases={3 + i: i for i in range(6)},
        cost_estimate=pl.CostEstimate(flops=8_000_000, bytes_accessed=2_000_000, transcendentals=0),
        compiler_params=KERNEL_VMEM,
        name="low_planes",
    )(*[on_chip(got) for got in (low, low_corner, state[8], *state[:6])])
    results = pl.pallas_call(
        functools.partial(side_kernel, 1),
        out_shape=shapes,
        in_specs=[vmem] * 11,
        out_specs=[vmem] * 7,
        input_output_aliases={4 + i: i for i in range(7)},
        scratch_shapes=scratch,
        compiler_params=KERNEL_VMEM,
        name="high_planes",
    )(*[on_chip(got) for got in (high, high_corner, state[8], state[7], *low_state, state[6])])
    return results[6]


def block_transpose(values, width):
    count = len(values)
    values = list(values)
    lane = lax.broadcasted_iota(jnp.int32, values[0].shape, 1) // width
    step = 1
    while step < count:
        odd = (lane & step) != 0
        for i in range(count):
            if i & step:
                continue
            low, high = values[i], values[i + step]
            shift = width * step
            values[i] = jnp.where(odd, pltpu.roll(high, shift, 1), low)
            values[i + step] = jnp.where(odd, high, pltpu.roll(low, low.shape[1] - shift, 1))
        step *= 2
    return values


def solve_kernel(
    east_count, north_count, cells_x, cells_y,
    in_ref, qx_ref, qxt_ref, qy_ref, qyt_ref, ex_ref, ey_ref, em_ref, place_ref, out_ref, work,
):
    total_x = east_count * cells_x
    total_y = north_count * cells_y
    block = in_ref.shape[1]
    groups = cells_x // north_count
    chunk = total_x * block // CHUNKS
    for h in range(CHUNKS):
        pieces = []
        for a in range(h * east_count // CHUNKS, (h + 1) * east_count // CHUNKS):
            for g in range(groups):
                lanes = slice(g * total_y, (g + 1) * total_y)
                got = [in_ref[b * east_count + a, :, lanes] for b in range(north_count)]
                pieces += block_transpose(got, cells_y)
        lines = value_parts(jnp.concatenate(pieces, axis=0), 1, NORTH_PARTS)
        work[h * chunk : (h + 1) * chunk, :] = dot(lines, qy_ref[...], ((1,), (0,)))
    planes = [work[pl.ds(i, total_x, stride=block), :] for i in range(block)]
    waves = dot(qxt_ref[...], value_parts(jnp.concatenate(planes, axis=1), 0, EAST_PARTS), ((1,), (0,)))
    eigen = ex_ref[...] + ey_ref[0:1, :]
    first = place_ref[0] * block
    solved = []
    for i in range(block):
        value = eigen + em_ref[first + i]
        empty = value == 0.0
        factor = jnp.where(empty, 0.0, -1.0 / jnp.where(empty, 1.0, value))
        solved.append(waves[:, i * total_y : (i + 1) * total_y] * factor)
    back = dot(qx_ref[...], value_parts(jnp.concatenate(solved, axis=1), 0, INVERSE), ((1,), (0,)))
    for i in range(block):
        work[pl.ds(i, total_x, stride=block), :] = back[:, i * total_y : (i + 1) * total_y]
    for h in range(CHUNKS):
        lines = value_parts(work[h * chunk : (h + 1) * chunk, :], 1, INVERSE)
        lines = dot(lines, qyt_ref[...], ((1,), (0,)))
        row = 0
        for a in range(h * east_count // CHUNKS, (h + 1) * east_count // CHUNKS):
            for g in range(groups):
                lanes = slice(g * total_y, (g + 1) * total_y)
                pieces = [lines[row + i * block : row + (i + 1) * block] for i in range(north_count)]
                row += north_count * block
                for b, piece in enumerate(block_transpose(pieces, cells_y)):
                    out_ref[b * east_count + a, :, lanes] = piece


def solve_planes(blocks, place, east_count, north_count, cells_x, cells_y, levels):
    total_x = east_count * cells_x
    total_y = north_count * cells_y
    qx, ex = fourier_basis(total_x)
    qy, ey = fourier_basis(total_y)
    qx = np.roll(qx.reshape(east_count, cells_x, total_x), -EARLY, axis=1).reshape(total_x, total_x)
    tables = [
        table_parts(qx, 1, INVERSE),
        table_parts(qx.T, 1, EAST_PARTS),
        table_parts(qy, 0, NORTH_PARTS),
        table_parts(qy.T, 0, INVERSE),
    ]
    tables += [
        np.ascontiguousarray(np.broadcast_to(ex[:, None], (total_x, total_y))),
        np.ascontiguousarray(np.broadcast_to(ey[None, :], (8, total_y))),
    ]
    vmem = pl.BlockSpec(memory_space=pltpu.VMEM)
    smem = pl.BlockSpec(memory_space=pltpu.SMEM)
    return pl.pallas_call(
        functools.partial(solve_kernel, east_count, north_count, cells_x, cells_y),
        out_shape=pltpu.VMEM(blocks.shape, F32),
        in_specs=[vmem] * 7 + [smem] * 2,
        out_specs=vmem,
        scratch_shapes=[pltpu.VMEM((total_x * blocks.shape[1], total_y), F32)],
        compiler_params=KERNEL_VMEM,
        name="solve_planes",
    )(on_chip(blocks), *[on_chip(table) for table in tables], mode_eigen(levels), place.reshape(1))


def pressure_kernel(shift, modes_ref, basis_ref, out_ref, cells, sems):
    total = cells.shape[0]
    half = total // 2
    copies = []

    def send(first, count):
        target = out_ref.at[pl.ds((first + shift) % total, count)]
        copy = pltpu.make_async_copy(cells.at[pl.ds(first, count)], target, sems.at[len(copies)])
        copy.start()
        copies.append(copy)

    for first in (0, half):
        part = value_parts(modes_ref[:, first : first + half], 0, INVERSE)
        cells[first : first + half, :] = dot(part, basis_ref[...], ((0,), (0,)))
        if first:
            send(first, half - shift)
            send(total - shift, shift)
        else:
            send(first, half)
    for copy in copies:
        copy.wait()


def pressure_cells(modes, basis_rows, shift):
    shape = (modes.shape[1], basis_rows.shape[1])
    return pl.pallas_call(
        functools.partial(pressure_kernel, shift),
        out_shape=jax.ShapeDtypeStruct(shape, F32),
        in_specs=[pl.BlockSpec(memory_space=pltpu.VMEM)] * 2,
        out_specs=pl.BlockSpec(memory_space=pl.ANY),
        scratch_shapes=[pltpu.VMEM(shape, F32), pltpu.SemaphoreType.DMA((3,))],
        compiler_params=KERNEL_VMEM,
        name="pressure_cells",
    )(on_chip(modes), on_chip(table_parts(basis_rows, 0, INVERSE)))


def rotation(row_count, col_count, length, direction):
    product = (
        lax.broadcasted_iota(jnp.int32, (row_count, col_count), 0)
        * lax.broadcasted_iota(jnp.int32, (row_count, col_count), 1)
        % length
    )
    radians = 2.0 * math.pi / length * product.astype(jnp.float32)
    return (jnp.cos(radians), direction * jnp.sin(radians))


def matmul(table, operand):
    return jnp.dot(
        table, operand, precision=lax.Precision.HIGHEST, preferred_element_type=jnp.float32
    )


def contract(formula, table, operand):
    return jnp.einsum(
        formula, table, operand, precision=lax.Precision.HIGHEST, preferred_element_type=jnp.float32
    )


def transform_rows(real_part, imag_part, direction):
    length = real_part.shape[0]
    width = real_part.shape[1]
    factor_low = 1
    for candidate in range(1, math.isqrt(length) + 1):
        if length % candidate == 0:
            factor_low = candidate
    factor_high = length // factor_low
    cos_high, sin_high = rotation(factor_high, factor_high, factor_high, direction)
    grid_real = real_part.reshape(factor_high, factor_low * width)
    grid_imag = imag_part.reshape(factor_high, factor_low * width)
    section_real = (matmul(cos_high, grid_real) - matmul(sin_high, grid_imag)).reshape(
        factor_high, factor_low, width
    )
    section_imag = (matmul(cos_high, grid_imag) + matmul(sin_high, grid_real)).reshape(
        factor_high, factor_low, width
    )
    turn_cos, turn_sin = rotation(factor_high, factor_low, length, direction)
    turn_cos = turn_cos[:, :, None]
    turn_sin = turn_sin[:, :, None]
    turned_real = section_real * turn_cos - section_imag * turn_sin
    turned_imag = section_real * turn_sin + section_imag * turn_cos
    cos_low, sin_low = rotation(factor_low, factor_low, factor_low, direction)
    out_real = contract("ca,kar->ckr", cos_low, turned_real) - contract(
        "ca,kar->ckr", sin_low, turned_imag
    )
    out_imag = contract("ca,kar->ckr", cos_low, turned_imag) + contract(
        "ca,kar->ckr", sin_low, turned_real
    )
    return (out_real.reshape(length, width), out_imag.reshape(length, width))


def first_forward(flat, high_count, second_cells, level_count):
    total = flat.shape[0]
    width = flat.shape[1]
    low_length = total // high_count
    grid = flat.reshape(low_length, high_count * width)
    cos_low, sin_low = rotation(low_length, low_length, low_length, -1.0)
    section_real = matmul(cos_low, grid).reshape(low_length, high_count, second_cells, level_count)
    section_imag = matmul(sin_low, grid).reshape(low_length, high_count, second_cells, level_count)
    turn_cos, turn_sin = rotation(low_length, high_count, total, -1.0)
    turn_cos = turn_cos[:, :, None, None]
    turn_sin = turn_sin[:, :, None, None]
    turned_real = section_real * turn_cos - section_imag * turn_sin
    turned_imag = section_real * turn_sin + section_imag * turn_cos
    cos_high, sin_high = rotation(high_count, high_count, high_count, -1.0)
    out_real = contract("ca,kaym->cykm", cos_high, turned_real) - contract(
        "ca,kaym->cykm", sin_high, turned_imag
    )
    out_imag = contract("ca,kaym->cykm", cos_high, turned_imag) + contract(
        "ca,kaym->cykm", sin_high, turned_real
    )
    merged = low_length * level_count
    return (
        out_real.reshape(high_count, second_cells, merged),
        out_imag.reshape(high_count, second_cells, merged),
    )


def first_inverse(real_part, imag_part, level_count):
    high_count = real_part.shape[0]
    second_cells = real_part.shape[1]
    low_length = real_part.shape[2] // level_count
    total = high_count * low_length
    data_real = real_part.reshape(high_count, second_cells, low_length, level_count)
    data_imag = imag_part.reshape(high_count, second_cells, low_length, level_count)
    cos_high, sin_high = rotation(high_count, high_count, high_count, 1.0)
    section_real = contract("ac,cykm->kaym", cos_high, data_real) - contract(
        "ac,cykm->kaym", sin_high, data_imag
    )
    section_imag = contract("ac,cykm->kaym", cos_high, data_imag) + contract(
        "ac,cykm->kaym", sin_high, data_real
    )
    turn_cos, turn_sin = rotation(low_length, high_count, total, 1.0)
    turn_cos = turn_cos[:, :, None, None]
    turn_sin = turn_sin[:, :, None, None]
    turned_real = section_real * turn_cos - section_imag * turn_sin
    turned_imag = section_real * turn_sin + section_imag * turn_cos
    cos_low, sin_low = rotation(low_length, low_length, low_length, 1.0)
    flat = matmul(cos_low, turned_real.reshape(low_length, -1)) - matmul(
        sin_low, turned_imag.reshape(low_length, -1)
    )
    return flat.reshape(total, second_cells * level_count)


def solve_modes(
    real_part, imag_part, first_rank, second_rank, first_total, second_total, levels, level_count
):
    low_length = real_part.shape[1] // level_count
    shape_full = (second_total, low_length, level_count)
    wave_second = lax.broadcasted_iota(jnp.int32, shape_full, 0)
    wave_first = second_rank * low_length + lax.broadcasted_iota(jnp.int32, shape_full, 1)
    mode_index = first_rank * level_count + lax.broadcasted_iota(jnp.int32, shape_full, 2)
    eigen = 4.0 * jnp.sin(math.pi / first_total * wave_first.astype(jnp.float32)) ** 2
    eigen = eigen + 4.0 * jnp.sin(math.pi / second_total * wave_second.astype(jnp.float32)) ** 2
    eigen = eigen + 4.0 * jnp.sin(math.pi / (2.0 * levels) * mode_index.astype(jnp.float32)) ** 2
    empty = (wave_first == 0) & (wave_second == 0) & (mode_index == 0)
    factor = jnp.where(empty, 0.0, -1.0 / jnp.where(empty, 1.0, eigen)) / (
        first_total * second_total
    )
    factor = factor.reshape(second_total, low_length * level_count)
    return (real_part * factor, imag_part * factor)


def fold_half(real_part, imag_part, level_count):
    high_count = real_part.shape[0]
    second_cells = real_part.shape[1]
    low_length = real_part.shape[2] // level_count
    half_high = high_count // 2
    half_low = low_length // 2
    nyquist = real_part[half_high, :, :level_count]

    def halve(values):
        kept = values[:half_high].reshape(half_high, second_cells, 2, half_low * level_count)
        return kept.transpose(0, 2, 1, 3).reshape(high_count, second_cells, half_low * level_count)

    kept_real = halve(real_part)
    kept_imag = halve(imag_part).at[0, :, :level_count].set(nyquist)
    return (kept_real, kept_imag)


def solve_half(
    real_part, imag_part, first_rank, second_rank, first_total, second_total, levels, level_count
):
    packed_real = real_part[:, :level_count]
    packed_imag = imag_part[:, :level_count]
    mirror_real = jnp.roll(packed_real[::-1], 1, axis=0)
    mirror_imag = jnp.roll(packed_imag[::-1], 1, axis=0)
    zero_real = 0.5 * (packed_real + mirror_real)
    zero_imag = 0.5 * (packed_imag - mirror_imag)
    nyquist_real = 0.5 * (packed_imag + mirror_imag)
    nyquist_imag = -0.5 * (packed_real - mirror_real)
    first_block = second_rank == 0
    real_part = jnp.where(first_block, real_part.at[:, :level_count].set(zero_real), real_part)
    imag_part = jnp.where(first_block, imag_part.at[:, :level_count].set(zero_imag), imag_part)
    solved_real, solved_imag = solve_modes(
        real_part,
        imag_part,
        first_rank,
        second_rank,
        first_total,
        second_total,
        levels,
        level_count,
    )
    wave_second = lax.broadcasted_iota(jnp.int32, (second_total, level_count), 0)
    mode_index = first_rank * level_count + lax.broadcasted_iota(
        jnp.int32, (second_total, level_count), 1
    )
    eigen = 4.0 + 4.0 * jnp.sin(math.pi / second_total * wave_second.astype(jnp.float32)) ** 2
    eigen = eigen + 4.0 * jnp.sin(math.pi / (2.0 * levels) * mode_index.astype(jnp.float32)) ** 2
    nyquist_factor = -1.0 / eigen / (first_total * second_total)
    solved_nyquist_real = nyquist_real * nyquist_factor
    solved_nyquist_imag = nyquist_imag * nyquist_factor
    joined_real = solved_real[:, :level_count] - solved_nyquist_imag
    joined_imag = solved_imag[:, :level_count] + solved_nyquist_real
    solved_real = jnp.where(
        first_block, solved_real.at[:, :level_count].set(joined_real), solved_real
    )
    solved_imag = jnp.where(
        first_block, solved_imag.at[:, :level_count].set(joined_imag), solved_imag
    )
    return (solved_real, solved_imag)


def unfold_half(real_part, imag_part, level_count):
    high_count = real_part.shape[0]
    second_cells = real_part.shape[1]
    half_low = real_part.shape[2] // level_count
    half_high = high_count // 2
    low_length = 2 * half_low

    def unhalve(values):
        shaped = values.reshape(half_high, 2, second_cells, half_low * level_count)
        return shaped.transpose(0, 2, 1, 3).reshape(
            half_high, second_cells, low_length * level_count
        )

    lower_real = unhalve(real_part)
    lower_imag = unhalve(imag_part)
    zero_line = lower_real[0, :, :level_count]
    nyquist_line = lower_imag[0, :, :level_count]
    upper = jnp.zeros((high_count - half_high, second_cells, low_length * level_count), jnp.float32)
    full_real = jnp.concatenate([2.0 * lower_real, upper], axis=0)
    full_imag = jnp.concatenate([2.0 * lower_imag, upper], axis=0)
    full_real = (
        full_real.at[0, :, :level_count]
        .set(zero_line)
        .at[half_high, :, :level_count]
        .set(nyquist_line)
    )
    full_imag = full_imag.at[0, :, :level_count].set(0.0)
    return (full_real, full_imag)


def spectral(
    modes,
    first_rank,
    second_rank,
    second_count,
    levels,
    send_out,
    send_across,
    bring_back,
    bring_home,
):
    first_count = modes.shape[0]
    first_cells = modes.shape[1]
    merged = modes.shape[2]
    level_count = levels // first_count
    second_cells = merged // level_count
    first_total = first_count * first_cells
    second_total = second_count * second_cells
    pencil = send_out(modes).reshape(first_total, merged)
    line_real, line_imag = first_forward(pencil, second_count, second_cells, level_count)
    line_real, line_imag = fold_half(line_real, line_imag, level_count)
    across_real, across_imag = send_across(line_real, line_imag)
    across_real = across_real.reshape(second_total, -1)
    across_imag = across_imag.reshape(second_total, -1)
    wave_real, wave_imag = transform_rows(across_real, across_imag, -1.0)
    wave_real, wave_imag = solve_half(
        wave_real,
        wave_imag,
        first_rank,
        second_rank,
        first_total,
        second_total,
        levels,
        level_count,
    )
    back_real, back_imag = transform_rows(wave_real, wave_imag, 1.0)
    home_real, home_imag = bring_back(
        back_real.reshape(1, second_total, -1), back_imag.reshape(1, second_total, -1)
    )
    home_real, home_imag = unfold_half(home_real, home_imag, level_count)
    flat = first_inverse(home_real, home_imag, level_count)
    return bring_home(flat.reshape(1, first_total, merged))


def staged(modes, east_count, north_count, cells_x, cells_y):
    levels = modes.shape[0]
    level_count = levels // east_count

    def send_out(values):
        return lax.all_to_all(values, "px", split_axis=0, concat_axis=1, tiled=True)

    def send_across(real_part, imag_part):
        return (
            lax.all_to_all(real_part, "py", split_axis=0, concat_axis=1, tiled=True),
            lax.all_to_all(imag_part, "py", split_axis=0, concat_axis=1, tiled=True),
        )

    def bring_back(real_part, imag_part):
        return (
            lax.all_to_all(real_part, "py", split_axis=1, concat_axis=0, tiled=True),
            lax.all_to_all(imag_part, "py", split_axis=1, concat_axis=0, tiled=True),
        )

    def bring_home(values):
        return lax.all_to_all(values, "px", split_axis=1, concat_axis=0, tiled=True)

    shaped = modes.reshape(east_count, level_count, cells_x, cells_y).transpose(0, 2, 3, 1)
    shaped = jnp.roll(shaped, EARLY, axis=1)
    result = spectral(
        shaped.reshape(east_count, cells_x, cells_y * level_count),
        lax.axis_index("px"),
        lax.axis_index("py"),
        north_count,
        levels,
        send_out,
        send_across,
        bring_back,
        bring_home,
    )
    result = jnp.roll(result.reshape(east_count, cells_x, cells_y, level_count), -EARLY, axis=1)
    result = result.transpose(0, 3, 1, 2)
    return result.reshape(levels, cells_x * cells_y)


def shards(wind_east, wind_north, wind_up):
    cells_x, cells_y, levels = wind_east.shape
    east_count = lax.axis_size("px")
    north_count = lax.axis_size("py")
    devices = east_count * north_count
    basis_rows = np.ascontiguousarray(cosine_basis(levels).T)
    north_rank = lax.axis_index("py")
    place = north_rank * east_count + lax.axis_index("px")
    modes = source_modes((wind_east, wind_north, wind_up), place, basis_rows)
    if levels == 8 * devices and north_count * cells_y == 128 and cells_x % north_count == 0:
        blocks = modes.reshape(devices, levels // devices, cells_x * cells_y)
        blocks = lax.all_to_all(blocks, ("py", "px"), split_axis=0, concat_axis=0, tiled=True)
        blocks = solve_planes(blocks, place, east_count, north_count, cells_x, cells_y, levels)
        blocks = lax.all_to_all(blocks, ("py", "px"), split_axis=0, concat_axis=0, tiled=True)
        modes = blocks.reshape(levels, cells_x * cells_y)
    else:
        modes = staged(modes, east_count, north_count, cells_x, cells_y)
    return pressure_cells(modes, basis_rows, EARLY * cells_y).reshape(cells_x, cells_y, levels)


def solution(mesh):
    return jax.shard_map(
        shards,
        mesh=mesh,
        in_specs=(P("px", "py", None), P("px", "py", None), P("px", "py", None)),
        out_specs=P("px", "py", None),
        check_vma=False,
    )
```

```python
import functools
import math

import jax
import jax.numpy as jnp
import ml_dtypes
import numpy as np
from jax import lax
from jax.experimental import pallas as pl
from jax.experimental.pallas import tpu as pltpu
from jax.sharding import PartitionSpec as P

NU_BASE = 0.01
SMAGORINSKY = 0.16
STRAIN_FLOOR = 1.0
TIME_STEP = 0.25
HALO = 3
ROWS = 4
EARLY = 4
CHUNKS = 2
LANES = 128
F32 = jnp.float32
BF16 = jnp.bfloat16
DCT_PARTS = 3
NORTH_PARTS = 3
EAST_PARTS = 3
INVERSE = 2
KERNEL_VMEM = pltpu.CompilerParams(vmem_limit_bytes=24 * 2**20)


def cosine_basis(levels):
    level = np.arange(levels, dtype=np.int64)[:, None]
    mode = np.arange(levels, dtype=np.int64)[None, :]
    radians = math.pi / (2.0 * levels) * ((2 * level + 1) * mode % (4 * levels))
    weight = np.where(mode == 0, math.sqrt(1.0 / levels), math.sqrt(2.0 / levels))
    return (weight * np.cos(radians)).astype(np.float32)


def fourier_basis(length):
    cell = np.arange(length)
    half = length // 2
    columns = [np.full(length, math.sqrt(1.0 / length))]
    waves = [0]
    for wave in range(1, half):
        angle = 2.0 * math.pi * (cell * wave % length) / length
        columns += [math.sqrt(2.0 / length) * np.cos(angle), math.sqrt(2.0 / length) * np.sin(angle)]
        waves += [wave, wave]
    columns.append(math.sqrt(1.0 / length) * (1.0 - 2.0 * (cell % 2)))
    waves.append(half)
    eigen = 4.0 * np.sin(math.pi / length * np.array(waves)) ** 2
    return np.stack(columns, axis=1).astype(np.float32), eigen.astype(np.float32)


def mode_eigen(levels):
    return (4.0 * np.sin(math.pi / (2.0 * levels) * np.arange(levels)) ** 2).astype(np.float32)


PAIRS = {2: ((0, 0), (0, 1), (1, 0)), 3: ((0, 0), (0, 1), (1, 0), (1, 1), (0, 2), (2, 0))}


def parts_of(values, count, narrow):
    parts = []
    for _ in range(count):
        parts.append(values.astype(narrow))
        values = values - parts[-1].astype(values.dtype)
    return parts


def table_parts(table, axis, count):
    parts = parts_of(table, count, ml_dtypes.bfloat16)
    return np.ascontiguousarray(np.concatenate([parts[t] for t, _ in PAIRS[count]], axis=axis))


def value_parts(values, axis, count):
    parts = parts_of(values, count, BF16)
    return jnp.concatenate([parts[v] for _, v in PAIRS[count]], axis=axis)


def dot(left, right, contract):
    return lax.dot_general(left, right, (contract, ((), ())), preferred_element_type=F32)


def on_chip(values):
    return pltpu.with_memory_space_constraint(values, pltpu.VMEM)


def swaps(axis):
    size = lax.axis_size(axis)
    inner = [(i, i ^ 1) for i in range(size)]
    outer = [(i, (i - 1 if i % 2 == 0 else i + 1) % size) for i in range(size)]
    return inner, outer


def ring(axis):
    size = lax.axis_size(axis)
    up = [(i, (i + 1) % size) for i in range(size)]
    return up, [(j, i) for i, j in up]


def lane_blocks(values):
    return [values[:, i : i + LANES] for i in range(0, values.shape[1], LANES)]


def z_next(values, edge):
    lane = lax.broadcasted_iota(jnp.int32, (values.shape[0], LANES), 1)
    turned = [pltpu.roll(block, LANES - 1, 1) for block in lane_blocks(values)] + [edge]
    last = lane == LANES - 1
    pairs = zip(turned[1:], turned[:-1])
    return jnp.concatenate([jnp.where(last, after, here) for after, here in pairs], axis=1)


def z_prev(values, edge):
    lane = lax.broadcasted_iota(jnp.int32, (values.shape[0], LANES), 1)
    turned = [edge] + [pltpu.roll(block, 1, 1) for block in lane_blocks(values)]
    pairs = zip(turned[:-1], turned[1:])
    return jnp.concatenate([jnp.where(lane == 0, before, here) for before, here in pairs], axis=1)


def y_next(values):
    return pltpu.roll(values, values.shape[0] - 1, 0)


def y_prev(values):
    return pltpu.roll(values, 1, 0)


def eddy(total):
    root = total + 4.0 * STRAIN_FLOOR
    return NU_BASE + (0.5 * SMAGORINSKY) * (root * lax.rsqrt(root))


def visc_plane(x, wind, above, below, visc):
    along_x = [wind[c, x + 1] - wind[c, x - 1] for c in range(3)]
    along_y = [y_next(wind[c, x]) - y_prev(wind[c, x]) for c in range(3)]
    along_z = [above[c, x] - below[c, x] for c in range(3)]
    normal = along_x[0] * along_x[0] + along_y[1] * along_y[1] + along_z[2] * along_z[2]
    xy = along_x[1] + along_y[0]
    xz = along_x[2] + along_z[0]
    yz = along_y[2] + along_z[1]
    visc[x] = eddy((normal + normal) + (xy * xy + xz * xz + yz * yz))


def wind_plane(x, wind, above, below, visc, east, part):
    cells = east.shape[1]
    centre = [wind[c, x] for c in range(3)]
    nu = visc[x]
    lane = lax.broadcasted_iota(jnp.int32, (nu.shape[0], LANES), 1)
    ends = [jnp.where(lane < LANES // 2, u[:, :LANES], u[:, -LANES:]) for u in centre]
    beyond = eddy(2.0 * (ends[2] * ends[2]) + (ends[0] * ends[0] + ends[1] * ends[1]))
    sum_xn = nu + visc[x + 1]
    sum_xp = nu + visc[x - 1]
    sum_yn = nu + y_next(nu)
    sum_yp = nu + y_prev(nu)
    sum_zn = nu + z_next(nu, beyond)
    sum_zp = nu + z_prev(nu, beyond)
    whole = ((sum_xn + sum_xp) + (sum_yn + sum_yp)) + ((sum_zn + sum_zp) - 2.0 / TIME_STEP)
    coef = (
        sum_xn - centre[0],
        sum_xp + centre[0],
        sum_yn - centre[1],
        sum_yp + centre[1],
        sum_zn - centre[2],
        sum_zp + centre[2],
    )

    def one(c, rows):
        u = centre[c]
        total = coef[0][:rows] * wind[c, x + 1, :rows] + coef[1][:rows] * wind[c, x - 1, :rows]
        total += coef[2][:rows] * y_next(u)[:rows] + coef[3][:rows] * y_prev(u)[:rows]
        total += coef[4][:rows] * above[c, x, :rows] + coef[5][:rows] * below[c, x, :rows]
        return total - whole[:rows] * u[:rows]

    east[x] = one(0, cells)
    if part is None:
        return
    north = one(1, nu.shape[0])
    up = one(2, cells)
    edge = centre[2][:cells]
    top = sum_zn[:cells, -LANES:] * edge[:, -LANES:]
    bottom = sum_zp[:cells, :LANES] * edge[:, :LANES]
    part[x] = (y_next(north) - y_prev(north))[:cells] + (z_next(up, top) - z_prev(up, bottom))


def shift_table(levels):
    level = lax.broadcasted_iota(jnp.int32, (levels, levels), 0)
    moved = lax.broadcasted_iota(jnp.int32, (levels, levels), 1)
    tables = [jnp.where(level == moved + step, 1.0, 0.0) for step in (1, -1)]
    return jnp.concatenate(tables, axis=1).astype(BF16)


def store_planes(places, planes, table, wind, above, below):
    rows, levels = planes[0].shape
    stacked = jnp.concatenate(planes, axis=0).astype(BF16)
    moved = dot(stacked, table, ((1,), (0,)))
    for i, ((c, x), plane) in enumerate(zip(places, planes)):
        wind[c, x] = plane
        above[c, x] = moved[i * rows : (i + 1) * rows, :levels]
        below[c, x] = moved[i * rows : (i + 1) * rows, levels:]


def by_parity(odd, body):
    pl.when(odd == 1)(lambda: body(True))
    pl.when(odd == 0)(lambda: body(False))


def each(first, last, body, jump=0, skip=0, unroll=1):
    def step(i, carry):
        body(i + jnp.where(i >= first + jump, skip, 0) if skip else i)
        return carry

    lax.fori_loop(first, last, step, 0, unroll=unroll)


def half_modes(first, source, east, part, basis_ref, modes, half):
    count, cells_y, levels = source.shape
    for i in range(count):
        x = (first + i) % (2 * count) + HALO
        source[i] = part[x] + (east[x + 1] - east[x - 1])
    width = count * cells_y
    flat = source[...].reshape(width, levels)
    result = dot(basis_ref[...], value_parts(flat, 1, DCT_PARTS), ((1,), (1,)))
    modes[:, half * width : (half + 1) * width] = result


def inner_kernel(place_ref, winds_ref, near_ref, far_ref, table_ref, *refs):
    wind, above, below, visc, east, part, modes, basis_ref, table, source, sem = refs
    fetch = pltpu.make_async_copy(table_ref, basis_ref, sem)
    fetch.start()
    cells_x, cells_y, levels = winds_ref.shape[1:]

    table[...] = shift_table(levels)

    def load(odd):
        after_ref, before_ref = (far_ref, near_ref) if odd else (near_ref, far_ref)

        def plane(x):
            for c in range(3):
                pieces = [winds_ref[c, x], after_ref[c, x], before_ref[c, x]]
                whole = jnp.concatenate([piece.astype(F32) for piece in pieces], axis=0)
                none = jnp.zeros((whole.shape[0], LANES), F32)
                wind[c, x + HALO] = whole
                above[c, x + HALO] = z_next(whole, none)
                below[c, x + HALO] = z_prev(whole, none)

        each(0, cells_x, plane, unroll=4)

    by_parity(place_ref[0] // lax.axis_size("px") % 2, load)
    first, last = HALO, HALO + cells_x
    each(first + 1, last - 1, lambda x: visc_plane(x, wind, above, below, visc), unroll=2)
    each(first + 2, last - 2, lambda x: wind_plane(x, wind, above, below, visc, east, part), unroll=2)
    fetch.wait()
    half_modes(EARLY, source, east, part, basis_ref, modes, 0)


def side_kernel(side, planes_ref, corner_ref, table, *refs):
    if side:
        wind, above, below, visc, east, part, modes, source = refs[8:]
        basis_ref = refs[0]
    else:
        wind, above, below, visc, east, part = refs[6:]
    levels = wind.shape[3]
    cells_x = wind.shape[1] - 2 * HALO
    row = lax.broadcasted_iota(jnp.int32, (8, levels), 0)

    places, planes = [], []
    for c in range(3):
        nearest = corner_ref[c].astype(F32)
        second = jnp.where(row < 4, pltpu.roll(nearest, 6, 0), pltpu.roll(nearest, 2, 0))
        for i, rest in enumerate((nearest, second, jnp.zeros_like(nearest))):
            index = i if side else HALO - 1 - i
            planes.append(jnp.concatenate([planes_ref[c, index].astype(F32), rest], axis=0))
            places.append((c, index + (HALO + cells_x if side else 0)))
    store_planes(places, planes, table[...], wind, above, below)
    skip = cells_x + 1 if side else 0
    each(1 + skip, 4 + skip, lambda x: visc_plane(x, wind, above, below, visc), unroll=3)
    first = cells_x + 1 if side else HALO
    each(first, first + 2, lambda x: wind_plane(x, wind, above, below, visc, east, part), unroll=2)
    wind_plane(HALO + cells_x if side else 2, wind, above, below, visc, east, None)
    if side:
        half_modes(cells_x - EARLY, source, east, part, basis_ref, modes, 1)


def pack_kernel(place_ref, *refs):
    winds = refs[:3]
    winds_ref, inner_ref, outer_ref, down_ref, up_ref, sems = refs[3:]
    cells_x, cells_y, levels = winds[0].shape
    copies = [
        pltpu.make_async_copy(ref, winds_ref.at[c], sems.at[c]) for c, ref in enumerate(winds)
    ]
    for copy in copies:
        copy.start()
    for copy in copies:
        copy.wait()

    def pack(odd):
        leading_ref, last_ref = (inner_ref, outer_ref) if odd else (outer_ref, inner_ref)
        for c in range(3):
            for x in range(cells_x):
                own = winds_ref[c, x]
                leading_ref[c, x] = own[:ROWS]
                last_ref[c, x] = own[cells_y - ROWS :]

    by_parity(place_ref[0] // lax.axis_size("px") % 2, pack)
    down_ref[...] = winds_ref[:, :HALO]
    up_ref[...] = winds_ref[:, cells_x - HALO :]


def pack_winds(winds, place):
    cells_x, cells_y, levels = winds[0].shape
    vmem = pl.BlockSpec(memory_space=pltpu.VMEM)
    edge = pltpu.VMEM((3, cells_x, ROWS, levels), BF16)
    side = pltpu.VMEM((3, HALO, cells_y, levels), BF16)
    return pl.pallas_call(
        pack_kernel,
        out_shape=[pltpu.VMEM((3, cells_x, cells_y, levels), BF16), edge, edge, side, side],
        in_specs=[pl.BlockSpec(memory_space=pltpu.SMEM)] + [pl.BlockSpec(memory_space=pl.ANY)] * 3,
        out_specs=[vmem] * 5,
        scratch_shapes=[pltpu.SemaphoreType.DMA((3,))],
        compiler_params=KERNEL_VMEM,
        name="pack_winds",
    )(place, *[pltpu.with_memory_space_constraint(wind, pltpu.HBM) for wind in winds])


def source_modes(winds, place, basis_rows):
    cells_x, cells_y, levels = winds[0].shape
    planes = cells_x + 2 * HALO
    rows = cells_y + 2 * ROWS
    odd_north = place // lax.axis_size("px") % 2
    place = place.reshape(1)
    stacked, inner_rows, outer_rows, leading, last = pack_winds(winds, place)
    inner, outer = swaps("py")
    up, down = ring("px")
    outer_got = lax.ppermute(outer_rows, "py", outer)
    inner_got = lax.ppermute(inner_rows, "py", inner)
    low = lax.ppermute(last, "px", up)
    high = lax.ppermute(leading, "px", down)

    def corner(first, second):
        near, far = [[v[:, x] for x in (first, second)] for v in (inner_got, outer_got)]
        after = [jnp.where(odd_north == 1, f, n) for n, f in zip(near, far)]
        before = [jnp.where(odd_north == 1, n, f) for n, f in zip(near, far)]
        none = jnp.zeros((3, 2, levels), BF16)
        pieces = [after[0][:, :2], after[1][:, :1], none, before[1][:, 3:], before[0][:, 2:]]
        return jnp.concatenate(pieces, axis=1)

    low_corner = lax.ppermute(corner(cells_x - 1, cells_x - 2), "px", up)
    high_corner = lax.ppermute(corner(0, 1), "px", down)
    vmem = pl.BlockSpec(memory_space=pltpu.VMEM)
    smem = pl.BlockSpec(memory_space=pltpu.SMEM)
    shapes = [pltpu.VMEM((3, planes, rows, levels), F32)] * 3
    shapes += [pltpu.VMEM((planes, rows, levels), F32)]
    shapes += [pltpu.VMEM((planes, cells_y, levels), F32)] * 2
    shapes += [pltpu.VMEM((levels, cells_x * cells_y), F32)]
    scratch = [pltpu.VMEM((cells_x // 2, cells_y, levels), F32)]
    basis = table_parts(basis_rows * np.float32(0.0625), 1, DCT_PARTS)
    state = pl.pallas_call(
        inner_kernel,
        out_shape=shapes + [pltpu.VMEM(basis.shape, BF16), pltpu.VMEM((levels, 2 * levels), BF16)],
        in_specs=[smem] + [vmem] * 3 + [pl.BlockSpec(memory_space=pl.ANY)],
        out_specs=[vmem] * 9,
        scratch_shapes=scratch + [pltpu.SemaphoreType.DMA],
        cost_estimate=pl.CostEstimate(flops=40_000_000, bytes_accessed=6_000_000, transcendentals=0),
        compiler_params=KERNEL_VMEM,
        name="inner_planes",
    )(
        place,
        *[on_chip(got) for got in (stacked, inner_got, outer_got)],
        pltpu.with_memory_space_constraint(basis, pltpu.HBM),
    )
    low_state = pl.pallas_call(
        functools.partial(side_kernel, 0),
        out_shape=shapes[:6],
        in_specs=[vmem] * 9,
        out_specs=[vmem] * 6,
        input_output_aliases={3 + i: i for i in range(6)},
        cost_estimate=pl.CostEstimate(flops=8_000_000, bytes_accessed=2_000_000, transcendentals=0),
        compiler_params=KERNEL_VMEM,
        name="low_planes",
    )(*[on_chip(got) for got in (low, low_corner, state[8], *state[:6])])
    results = pl.pallas_call(
        functools.partial(side_kernel, 1),
        out_shape=shapes,
        in_specs=[vmem] * 11,
        out_specs=[vmem] * 7,
        input_output_aliases={4 + i: i for i in range(7)},
        scratch_shapes=scratch,
        compiler_params=KERNEL_VMEM,
        name="high_planes",
    )(*[on_chip(got) for got in (high, high_corner, state[8], state[7], *low_state, state[6])])
    return results[6]


def block_transpose(values, width):
    count = len(values)
    values = list(values)
    lane = lax.broadcasted_iota(jnp.int32, values[0].shape, 1) // width
    step = 1
    while step < count:
        odd = (lane & step) != 0
        for i in range(count):
            if i & step:
                continue
            low, high = values[i], values[i + step]
            shift = width * step
            values[i] = jnp.where(odd, pltpu.roll(high, shift, 1), low)
            values[i + step] = jnp.where(odd, high, pltpu.roll(low, low.shape[1] - shift, 1))
        step *= 2
    return values


def solve_kernel(
    east_count, north_count, cells_x, cells_y,
    in_ref, qx_ref, qxt_ref, qy_ref, qyt_ref, ex_ref, ey_ref, em_ref, place_ref, out_ref, work,
):
    total_x = east_count * cells_x
    total_y = north_count * cells_y
    block = in_ref.shape[1]
    groups = cells_x // north_count
    chunk = total_x * block // CHUNKS
    for h in range(CHUNKS):
        pieces = []
        for a in range(h * east_count // CHUNKS, (h + 1) * east_count // CHUNKS):
            for g in range(groups):
                lanes = slice(g * total_y, (g + 1) * total_y)
                got = [in_ref[b * east_count + a, :, lanes] for b in range(north_count)]
                pieces += block_transpose(got, cells_y)
        lines = value_parts(jnp.concatenate(pieces, axis=0), 1, NORTH_PARTS)
        work[h * chunk : (h + 1) * chunk, :] = dot(lines, qy_ref[...], ((1,), (0,)))
    planes = [work[pl.ds(i, total_x, stride=block), :] for i in range(block)]
    waves = dot(qxt_ref[...], value_parts(jnp.concatenate(planes, axis=1), 0, EAST_PARTS), ((1,), (0,)))
    eigen = ex_ref[...] + ey_ref[0:1, :]
    first = place_ref[0] * block
    solved = []
    for i in range(block):
        value = eigen + em_ref[first + i]
        empty = value == 0.0
        factor = jnp.where(empty, 0.0, -1.0 / jnp.where(empty, 1.0, value))
        solved.append(waves[:, i * total_y : (i + 1) * total_y] * factor)
    back = dot(qx_ref[...], value_parts(jnp.concatenate(solved, axis=1), 0, INVERSE), ((1,), (0,)))
    for i in range(block):
        work[pl.ds(i, total_x, stride=block), :] = back[:, i * total_y : (i + 1) * total_y]
    for h in range(CHUNKS):
        lines = value_parts(work[h * chunk : (h + 1) * chunk, :], 1, INVERSE)
        lines = dot(lines, qyt_ref[...], ((1,), (0,)))
        row = 0
        for a in range(h * east_count // CHUNKS, (h + 1) * east_count // CHUNKS):
            for g in range(groups):
                lanes = slice(g * total_y, (g + 1) * total_y)
                pieces = [lines[row + i * block : row + (i + 1) * block] for i in range(north_count)]
                row += north_count * block
                for b, piece in enumerate(block_transpose(pieces, cells_y)):
                    out_ref[b * east_count + a, :, lanes] = piece


def solve_planes(blocks, place, east_count, north_count, cells_x, cells_y, levels):
    total_x = east_count * cells_x
    total_y = north_count * cells_y
    qx, ex = fourier_basis(total_x)
    qy, ey = fourier_basis(total_y)
    qx = np.roll(qx.reshape(east_count, cells_x, total_x), -EARLY, axis=1).reshape(total_x, total_x)
    tables = [
        table_parts(qx, 1, INVERSE),
        table_parts(qx.T, 1, EAST_PARTS),
        table_parts(qy, 0, NORTH_PARTS),
        table_parts(qy.T, 0, INVERSE),
    ]
    tables += [
        np.ascontiguousarray(np.broadcast_to(ex[:, None], (total_x, total_y))),
        np.ascontiguousarray(np.broadcast_to(ey[None, :], (8, total_y))),
    ]
    vmem = pl.BlockSpec(memory_space=pltpu.VMEM)
    smem = pl.BlockSpec(memory_space=pltpu.SMEM)
    return pl.pallas_call(
        functools.partial(solve_kernel, east_count, north_count, cells_x, cells_y),
        out_shape=pltpu.VMEM(blocks.shape, F32),
        in_specs=[vmem] * 7 + [smem] * 2,
        out_specs=vmem,
        scratch_shapes=[pltpu.VMEM((total_x * blocks.shape[1], total_y), F32)],
        compiler_params=pltpu.CompilerParams(vmem_limit_bytes=24 * 2**20),
        name="solve_planes",
    )(on_chip(blocks), *[on_chip(table) for table in tables], mode_eigen(levels), place.reshape(1))


def pressure_kernel(shift, modes_ref, basis_ref, out_ref, cells, sems):
    total = cells.shape[0]
    half = total // 2
    copies = []

    def send(first, count):
        target = out_ref.at[pl.ds((first + shift) % total, count)]
        copy = pltpu.make_async_copy(cells.at[pl.ds(first, count)], target, sems.at[len(copies)])
        copy.start()
        copies.append(copy)

    for first in (0, half):
        part = value_parts(modes_ref[:, first : first + half], 0, INVERSE)
        cells[first : first + half, :] = dot(part, basis_ref[...], ((0,), (0,)))
        if first:
            send(first, half - shift)
            send(total - shift, shift)
        else:
            send(first, half)
    for copy in copies:
        copy.wait()


def pressure_cells(modes, basis_rows, shift):
    shape = (modes.shape[1], basis_rows.shape[1])
    return pl.pallas_call(
        functools.partial(pressure_kernel, shift),
        out_shape=jax.ShapeDtypeStruct(shape, F32),
        in_specs=[pl.BlockSpec(memory_space=pltpu.VMEM)] * 2,
        out_specs=pl.BlockSpec(memory_space=pl.ANY),
        scratch_shapes=[pltpu.VMEM(shape, F32), pltpu.SemaphoreType.DMA((3,))],
        compiler_params=KERNEL_VMEM,
        name="pressure_cells",
    )(on_chip(modes), on_chip(table_parts(basis_rows, 0, INVERSE)))


def rotation(row_count, col_count, length, direction):
    product = (
        lax.broadcasted_iota(jnp.int32, (row_count, col_count), 0)
        * lax.broadcasted_iota(jnp.int32, (row_count, col_count), 1)
        % length
    )
    radians = 2.0 * math.pi / length * product.astype(jnp.float32)
    return (jnp.cos(radians), direction * jnp.sin(radians))


def matmul(table, operand):
    return jnp.dot(
        table, operand, precision=lax.Precision.HIGHEST, preferred_element_type=jnp.float32
    )


def contract(formula, table, operand):
    return jnp.einsum(
        formula, table, operand, precision=lax.Precision.HIGHEST, preferred_element_type=jnp.float32
    )


def transform_rows(real_part, imag_part, direction):
    length = real_part.shape[0]
    width = real_part.shape[1]
    factor_low = 1
    for candidate in range(1, math.isqrt(length) + 1):
        if length % candidate == 0:
            factor_low = candidate
    factor_high = length // factor_low
    cos_high, sin_high = rotation(factor_high, factor_high, factor_high, direction)
    grid_real = real_part.reshape(factor_high, factor_low * width)
    grid_imag = imag_part.reshape(factor_high, factor_low * width)
    section_real = (matmul(cos_high, grid_real) - matmul(sin_high, grid_imag)).reshape(
        factor_high, factor_low, width
    )
    section_imag = (matmul(cos_high, grid_imag) + matmul(sin_high, grid_real)).reshape(
        factor_high, factor_low, width
    )
    turn_cos, turn_sin = rotation(factor_high, factor_low, length, direction)
    turn_cos = turn_cos[:, :, None]
    turn_sin = turn_sin[:, :, None]
    turned_real = section_real * turn_cos - section_imag * turn_sin
    turned_imag = section_real * turn_sin + section_imag * turn_cos
    cos_low, sin_low = rotation(factor_low, factor_low, factor_low, direction)
    out_real = contract("ca,kar->ckr", cos_low, turned_real) - contract(
        "ca,kar->ckr", sin_low, turned_imag
    )
    out_imag = contract("ca,kar->ckr", cos_low, turned_imag) + contract(
        "ca,kar->ckr", sin_low, turned_real
    )
    return (out_real.reshape(length, width), out_imag.reshape(length, width))


def first_forward(flat, high_count, second_cells, level_count):
    total = flat.shape[0]
    width = flat.shape[1]
    low_length = total // high_count
    grid = flat.reshape(low_length, high_count * width)
    cos_low, sin_low = rotation(low_length, low_length, low_length, -1.0)
    section_real = matmul(cos_low, grid).reshape(low_length, high_count, second_cells, level_count)
    section_imag = matmul(sin_low, grid).reshape(low_length, high_count, second_cells, level_count)
    turn_cos, turn_sin = rotation(low_length, high_count, total, -1.0)
    turn_cos = turn_cos[:, :, None, None]
    turn_sin = turn_sin[:, :, None, None]
    turned_real = section_real * turn_cos - section_imag * turn_sin
    turned_imag = section_real * turn_sin + section_imag * turn_cos
    cos_high, sin_high = rotation(high_count, high_count, high_count, -1.0)
    out_real = contract("ca,kaym->cykm", cos_high, turned_real) - contract(
        "ca,kaym->cykm", sin_high, turned_imag
    )
    out_imag = contract("ca,kaym->cykm", cos_high, turned_imag) + contract(
        "ca,kaym->cykm", sin_high, turned_real
    )
    merged = low_length * level_count
    return (
        out_real.reshape(high_count, second_cells, merged),
        out_imag.reshape(high_count, second_cells, merged),
    )


def first_inverse(real_part, imag_part, level_count):
    high_count = real_part.shape[0]
    second_cells = real_part.shape[1]
    low_length = real_part.shape[2] // level_count
    total = high_count * low_length
    data_real = real_part.reshape(high_count, second_cells, low_length, level_count)
    data_imag = imag_part.reshape(high_count, second_cells, low_length, level_count)
    cos_high, sin_high = rotation(high_count, high_count, high_count, 1.0)
    section_real = contract("ac,cykm->kaym", cos_high, data_real) - contract(
        "ac,cykm->kaym", sin_high, data_imag
    )
    section_imag = contract("ac,cykm->kaym", cos_high, data_imag) + contract(
        "ac,cykm->kaym", sin_high, data_real
    )
    turn_cos, turn_sin = rotation(low_length, high_count, total, 1.0)
    turn_cos = turn_cos[:, :, None, None]
    turn_sin = turn_sin[:, :, None, None]
    turned_real = section_real * turn_cos - section_imag * turn_sin
    turned_imag = section_real * turn_sin + section_imag * turn_cos
    cos_low, sin_low = rotation(low_length, low_length, low_length, 1.0)
    flat = matmul(cos_low, turned_real.reshape(low_length, -1)) - matmul(
        sin_low, turned_imag.reshape(low_length, -1)
    )
    return flat.reshape(total, second_cells * level_count)


def solve_modes(
    real_part, imag_part, first_rank, second_rank, first_total, second_total, levels, level_count
):
    low_length = real_part.shape[1] // level_count
    shape_full = (second_total, low_length, level_count)
    wave_second = lax.broadcasted_iota(jnp.int32, shape_full, 0)
    wave_first = second_rank * low_length + lax.broadcasted_iota(jnp.int32, shape_full, 1)
    mode_index = first_rank * level_count + lax.broadcasted_iota(jnp.int32, shape_full, 2)
    eigen = 4.0 * jnp.sin(math.pi / first_total * wave_first.astype(jnp.float32)) ** 2
    eigen = eigen + 4.0 * jnp.sin(math.pi / second_total * wave_second.astype(jnp.float32)) ** 2
    eigen = eigen + 4.0 * jnp.sin(math.pi / (2.0 * levels) * mode_index.astype(jnp.float32)) ** 2
    empty = (wave_first == 0) & (wave_second == 0) & (mode_index == 0)
    factor = jnp.where(empty, 0.0, -1.0 / jnp.where(empty, 1.0, eigen)) / (
        first_total * second_total
    )
    factor = factor.reshape(second_total, low_length * level_count)
    return (real_part * factor, imag_part * factor)


def fold_half(real_part, imag_part, level_count):
    high_count = real_part.shape[0]
    second_cells = real_part.shape[1]
    low_length = real_part.shape[2] // level_count
    half_high = high_count // 2
    half_low = low_length // 2
    nyquist = real_part[half_high, :, :level_count]

    def halve(values):
        kept = values[:half_high].reshape(half_high, second_cells, 2, half_low * level_count)
        return kept.transpose(0, 2, 1, 3).reshape(high_count, second_cells, half_low * level_count)

    kept_real = halve(real_part)
    kept_imag = halve(imag_part).at[0, :, :level_count].set(nyquist)
    return (kept_real, kept_imag)


def solve_half(
    real_part, imag_part, first_rank, second_rank, first_total, second_total, levels, level_count
):
    packed_real = real_part[:, :level_count]
    packed_imag = imag_part[:, :level_count]
    mirror_real = jnp.roll(packed_real[::-1], 1, axis=0)
    mirror_imag = jnp.roll(packed_imag[::-1], 1, axis=0)
    zero_real = 0.5 * (packed_real + mirror_real)
    zero_imag = 0.5 * (packed_imag - mirror_imag)
    nyquist_real = 0.5 * (packed_imag + mirror_imag)
    nyquist_imag = -0.5 * (packed_real - mirror_real)
    first_block = second_rank == 0
    real_part = jnp.where(first_block, real_part.at[:, :level_count].set(zero_real), real_part)
    imag_part = jnp.where(first_block, imag_part.at[:, :level_count].set(zero_imag), imag_part)
    solved_real, solved_imag = solve_modes(
        real_part,
        imag_part,
        first_rank,
        second_rank,
        first_total,
        second_total,
        levels,
        level_count,
    )
    wave_second = lax.broadcasted_iota(jnp.int32, (second_total, level_count), 0)
    mode_index = first_rank * level_count + lax.broadcasted_iota(
        jnp.int32, (second_total, level_count), 1
    )
    eigen = 4.0 + 4.0 * jnp.sin(math.pi / second_total * wave_second.astype(jnp.float32)) ** 2
    eigen = eigen + 4.0 * jnp.sin(math.pi / (2.0 * levels) * mode_index.astype(jnp.float32)) ** 2
    nyquist_factor = -1.0 / eigen / (first_total * second_total)
    solved_nyquist_real = nyquist_real * nyquist_factor
    solved_nyquist_imag = nyquist_imag * nyquist_factor
    joined_real = solved_real[:, :level_count] - solved_nyquist_imag
    joined_imag = solved_imag[:, :level_count] + solved_nyquist_real
    solved_real = jnp.where(
        first_block, solved_real.at[:, :level_count].set(joined_real), solved_real
    )
    solved_imag = jnp.where(
        first_block, solved_imag.at[:, :level_count].set(joined_imag), solved_imag
    )
    return (solved_real, solved_imag)


def unfold_half(real_part, imag_part, level_count):
    high_count = real_part.shape[0]
    second_cells = real_part.shape[1]
    half_low = real_part.shape[2] // level_count
    half_high = high_count // 2
    low_length = 2 * half_low

    def unhalve(values):
        shaped = values.reshape(half_high, 2, second_cells, half_low * level_count)
        return shaped.transpose(0, 2, 1, 3).reshape(
            half_high, second_cells, low_length * level_count
        )

    lower_real = unhalve(real_part)
    lower_imag = unhalve(imag_part)
    zero_line = lower_real[0, :, :level_count]
    nyquist_line = lower_imag[0, :, :level_count]
    upper = jnp.zeros((high_count - half_high, second_cells, low_length * level_count), jnp.float32)
    full_real = jnp.concatenate([2.0 * lower_real, upper], axis=0)
    full_imag = jnp.concatenate([2.0 * lower_imag, upper], axis=0)
    full_real = (
        full_real.at[0, :, :level_count]
        .set(zero_line)
        .at[half_high, :, :level_count]
        .set(nyquist_line)
    )
    full_imag = full_imag.at[0, :, :level_count].set(0.0)
    return (full_real, full_imag)


def spectral(
    modes,
    first_rank,
    second_rank,
    second_count,
    levels,
    send_out,
    send_across,
    bring_back,
    bring_home,
):
    first_count = modes.shape[0]
    first_cells = modes.shape[1]
    merged = modes.shape[2]
    level_count = levels // first_count
    second_cells = merged // level_count
    first_total = first_count * first_cells
    second_total = second_count * second_cells
    pencil = send_out(modes).reshape(first_total, merged)
    line_real, line_imag = first_forward(pencil, second_count, second_cells, level_count)
    line_real, line_imag = fold_half(line_real, line_imag, level_count)
    across_real, across_imag = send_across(line_real, line_imag)
    across_real = across_real.reshape(second_total, -1)
    across_imag = across_imag.reshape(second_total, -1)
    wave_real, wave_imag = transform_rows(across_real, across_imag, -1.0)
    wave_real, wave_imag = solve_half(
        wave_real,
        wave_imag,
        first_rank,
        second_rank,
        first_total,
        second_total,
        levels,
        level_count,
    )
    back_real, back_imag = transform_rows(wave_real, wave_imag, 1.0)
    home_real, home_imag = bring_back(
        back_real.reshape(1, second_total, -1), back_imag.reshape(1, second_total, -1)
    )
    home_real, home_imag = unfold_half(home_real, home_imag, level_count)
    flat = first_inverse(home_real, home_imag, level_count)
    return bring_home(flat.reshape(1, first_total, merged))


def staged(modes, east_count, north_count, cells_x, cells_y):
    levels = modes.shape[0]
    level_count = levels // east_count

    def send_out(values):
        return lax.all_to_all(values, "px", split_axis=0, concat_axis=1, tiled=True)

    def send_across(real_part, imag_part):
        return (
            lax.all_to_all(real_part, "py", split_axis=0, concat_axis=1, tiled=True),
            lax.all_to_all(imag_part, "py", split_axis=0, concat_axis=1, tiled=True),
        )

    def bring_back(real_part, imag_part):
        return (
            lax.all_to_all(real_part, "py", split_axis=1, concat_axis=0, tiled=True),
            lax.all_to_all(imag_part, "py", split_axis=1, concat_axis=0, tiled=True),
        )

    def bring_home(values):
        return lax.all_to_all(values, "px", split_axis=1, concat_axis=0, tiled=True)

    shaped = modes.reshape(east_count, level_count, cells_x, cells_y).transpose(0, 2, 3, 1)
    shaped = jnp.roll(shaped, EARLY, axis=1)
    result = spectral(
        shaped.reshape(east_count, cells_x, cells_y * level_count),
        lax.axis_index("px"),
        lax.axis_index("py"),
        north_count,
        levels,
        send_out,
        send_across,
        bring_back,
        bring_home,
    )
    result = jnp.roll(result.reshape(east_count, cells_x, cells_y, level_count), -EARLY, axis=1)
    result = result.transpose(0, 3, 1, 2)
    return result.reshape(levels, cells_x * cells_y)


def shards(wind_east, wind_north, wind_up):
    cells_x, cells_y, levels = wind_east.shape
    east_count = lax.axis_size("px")
    north_count = lax.axis_size("py")
    devices = east_count * north_count
    basis_rows = np.ascontiguousarray(cosine_basis(levels).T)
    north_rank = lax.axis_index("py")
    place = north_rank * east_count + lax.axis_index("px")
    modes = source_modes((wind_east, wind_north, wind_up), place, basis_rows)
    if levels == 8 * devices and north_count * cells_y == 128 and cells_x % north_count == 0:
        blocks = modes.reshape(devices, levels // devices, cells_x * cells_y)
        blocks = lax.all_to_all(blocks, ("py", "px"), split_axis=0, concat_axis=0, tiled=True)
        blocks = solve_planes(blocks, place, east_count, north_count, cells_x, cells_y, levels)
        blocks = lax.all_to_all(blocks, ("py", "px"), split_axis=0, concat_axis=0, tiled=True)
        modes = blocks.reshape(levels, cells_x * cells_y)
    else:
        modes = staged(modes, east_count, north_count, cells_x, cells_y)
    return pressure_cells(modes, basis_rows, EARLY * cells_y).reshape(cells_x, cells_y, levels)


def solution(mesh):
    return jax.shard_map(
        shards,
        mesh=mesh,
        in_specs=(P("px", "py", None), P("px", "py", None), P("px", "py", None)),
        out_specs=P("px", "py", None),
        check_vma=False,
    )
```

```python
import functools
import math

import jax
import jax.numpy as jnp
import ml_dtypes
import numpy as np
from jax import lax
from jax.experimental import pallas as pl
from jax.experimental.pallas import tpu as pltpu
from jax.sharding import PartitionSpec as P

NU_BASE = 0.01
SMAGORINSKY = 0.16
STRAIN_FLOOR = 1.0
TIME_STEP = 0.25
HALO = 3
ROWS = 4
EARLY = 4
GROUP = 16
CHUNKS = 2
LANES = 128
F32 = jnp.float32
BF16 = jnp.bfloat16
DCT_PARTS = 3
NORTH_PARTS = 3
EAST_PARTS = 3
INVERSE = 2
KERNEL_VMEM = pltpu.CompilerParams(vmem_limit_bytes=24 * 2**20)


def cosine_basis(levels):
    level = np.arange(levels, dtype=np.int64)[:, None]
    mode = np.arange(levels, dtype=np.int64)[None, :]
    radians = math.pi / (2.0 * levels) * ((2 * level + 1) * mode % (4 * levels))
    weight = np.where(mode == 0, math.sqrt(1.0 / levels), math.sqrt(2.0 / levels))
    return (weight * np.cos(radians)).astype(np.float32)


def fourier_basis(length):
    cell = np.arange(length)
    half = length // 2
    columns = [np.full(length, math.sqrt(1.0 / length))]
    waves = [0]
    for wave in range(1, half):
        angle = 2.0 * math.pi * (cell * wave % length) / length
        columns += [math.sqrt(2.0 / length) * np.cos(angle), math.sqrt(2.0 / length) * np.sin(angle)]
        waves += [wave, wave]
    columns.append(math.sqrt(1.0 / length) * (1.0 - 2.0 * (cell % 2)))
    waves.append(half)
    eigen = 4.0 * np.sin(math.pi / length * np.array(waves)) ** 2
    return np.stack(columns, axis=1).astype(np.float32), eigen.astype(np.float32)


def mode_eigen(levels):
    return (4.0 * np.sin(math.pi / (2.0 * levels) * np.arange(levels)) ** 2).astype(np.float32)


PAIRS = {2: ((0, 0), (0, 1), (1, 0)), 3: ((0, 0), (0, 1), (1, 0), (1, 1), (0, 2), (2, 0))}


def parts_of(values, count, narrow):
    parts = []
    for _ in range(count):
        parts.append(values.astype(narrow))
        values = values - parts[-1].astype(values.dtype)
    return parts


def table_parts(table, axis, count):
    parts = parts_of(table, count, ml_dtypes.bfloat16)
    return np.ascontiguousarray(np.concatenate([parts[t] for t, _ in PAIRS[count]], axis=axis))


def value_parts(values, axis, count):
    parts = parts_of(values, count, BF16)
    return jnp.concatenate([parts[v] for _, v in PAIRS[count]], axis=axis)


def dot(left, right, contract):
    return lax.dot_general(left, right, (contract, ((), ())), preferred_element_type=F32)


def on_chip(values):
    return pltpu.with_memory_space_constraint(values, pltpu.VMEM)


def swaps(axis):
    size = lax.axis_size(axis)
    inner = [(i, i ^ 1) for i in range(size)]
    outer = [(i, (i - 1 if i % 2 == 0 else i + 1) % size) for i in range(size)]
    return inner, outer


def ring(axis):
    size = lax.axis_size(axis)
    up = [(i, (i + 1) % size) for i in range(size)]
    return up, [(j, i) for i, j in up]


def lane_blocks(values):
    return [values[:, i : i + LANES] for i in range(0, values.shape[1], LANES)]


def z_next(values, edge):
    lane = lax.broadcasted_iota(jnp.int32, (values.shape[0], LANES), 1)
    turned = [pltpu.roll(block, LANES - 1, 1) for block in lane_blocks(values)] + [edge]
    last = lane == LANES - 1
    pairs = zip(turned[1:], turned[:-1])
    return jnp.concatenate([jnp.where(last, after, here) for after, here in pairs], axis=1)


def z_prev(values, edge):
    lane = lax.broadcasted_iota(jnp.int32, (values.shape[0], LANES), 1)
    turned = [edge] + [pltpu.roll(block, 1, 1) for block in lane_blocks(values)]
    pairs = zip(turned[:-1], turned[1:])
    return jnp.concatenate([jnp.where(lane == 0, before, here) for before, here in pairs], axis=1)


def y_next(values):
    return pltpu.roll(values, values.shape[0] - 1, 0)


def y_prev(values):
    return pltpu.roll(values, 1, 0)


def eddy(total):
    root = total + 4.0 * STRAIN_FLOOR
    return NU_BASE + (0.5 * SMAGORINSKY) * (root * lax.rsqrt(root))


def visc_plane(x, wind, above, below, visc):
    along_x = [wind[c, x + 1] - wind[c, x - 1] for c in range(3)]
    along_y = [y_next(wind[c, x]) - y_prev(wind[c, x]) for c in range(3)]
    along_z = [above[c, x] - below[c, x] for c in range(3)]
    normal = along_x[0] * along_x[0] + along_y[1] * along_y[1] + along_z[2] * along_z[2]
    xy = along_x[1] + along_y[0]
    xz = along_x[2] + along_z[0]
    yz = along_y[2] + along_z[1]
    visc[x] = eddy((normal + normal) + (xy * xy + xz * xz + yz * yz))


def wind_plane(x, wind, above, below, visc, east, part):
    cells = east.shape[1]
    centre = [wind[c, x] for c in range(3)]
    nu = visc[x]
    lane = lax.broadcasted_iota(jnp.int32, (nu.shape[0], LANES), 1)
    ends = [jnp.where(lane < LANES // 2, u[:, :LANES], u[:, -LANES:]) for u in centre]
    beyond = eddy(2.0 * (ends[2] * ends[2]) + (ends[0] * ends[0] + ends[1] * ends[1]))
    sum_xn = nu + visc[x + 1]
    sum_xp = nu + visc[x - 1]
    sum_yn = nu + y_next(nu)
    sum_yp = nu + y_prev(nu)
    sum_zn = nu + z_next(nu, beyond)
    sum_zp = nu + z_prev(nu, beyond)
    whole = ((sum_xn + sum_xp) + (sum_yn + sum_yp)) + ((sum_zn + sum_zp) - 2.0 / TIME_STEP)
    coef = (
        sum_xn - centre[0],
        sum_xp + centre[0],
        sum_yn - centre[1],
        sum_yp + centre[1],
        sum_zn - centre[2],
        sum_zp + centre[2],
    )

    def one(c, rows):
        u = centre[c]
        total = coef[0][:rows] * wind[c, x + 1, :rows] + coef[1][:rows] * wind[c, x - 1, :rows]
        total += coef[2][:rows] * y_next(u)[:rows] + coef[3][:rows] * y_prev(u)[:rows]
        total += coef[4][:rows] * above[c, x, :rows] + coef[5][:rows] * below[c, x, :rows]
        return total - whole[:rows] * u[:rows]

    east[x] = one(0, cells)
    if part is None:
        return
    north = one(1, nu.shape[0])
    up = one(2, cells)
    edge = centre[2][:cells]
    top = sum_zn[:cells, -LANES:] * edge[:, -LANES:]
    bottom = sum_zp[:cells, :LANES] * edge[:, :LANES]
    part[x] = (y_next(north) - y_prev(north))[:cells] + (z_next(up, top) - z_prev(up, bottom))


def shift_table(levels):
    level = lax.broadcasted_iota(jnp.int32, (levels, levels), 0)
    moved = lax.broadcasted_iota(jnp.int32, (levels, levels), 1)
    tables = [jnp.where(level == moved + step, 1.0, 0.0) for step in (1, -1)]
    return jnp.concatenate(tables, axis=1).astype(BF16)


def store_planes(places, planes, table, wind, above, below):
    rows, levels = planes[0].shape
    stacked = jnp.concatenate(planes, axis=0).astype(BF16)
    moved = dot(stacked, table, ((1,), (0,)))
    for i, ((c, x), plane) in enumerate(zip(places, planes)):
        wind[c, x] = plane
        above[c, x] = moved[i * rows : (i + 1) * rows, :levels]
        below[c, x] = moved[i * rows : (i + 1) * rows, levels:]


def by_parity(odd, body):
    pl.when(odd == 1)(lambda: body(True))
    pl.when(odd == 0)(lambda: body(False))


def each(first, last, body, jump=0, skip=0, unroll=1):
    def step(i, carry):
        body(i + jnp.where(i >= first + jump, skip, 0) if skip else i)
        return carry

    lax.fori_loop(first, last, step, 0, unroll=unroll)


def half_modes(first, source, east, part, basis_ref, modes, half):
    count, cells_y, levels = source.shape
    for i in range(count):
        x = (first + i) % (2 * count) + HALO
        source[i] = part[x] + (east[x + 1] - east[x - 1])
    width = count * cells_y
    flat = source[...].reshape(width, levels)
    result = dot(basis_ref[...], value_parts(flat, 1, DCT_PARTS), ((1,), (1,)))
    modes[:, half * width : (half + 1) * width] = result


def inner_kernel(place_ref, winds_ref, near_ref, far_ref, table_ref, *refs):
    wind, above, below, visc, east, part, modes, basis_ref, table, source, sem = refs
    fetch = pltpu.make_async_copy(table_ref, basis_ref, sem)
    fetch.start()
    cells_x, cells_y, levels = winds_ref.shape[1:]

    table[...] = shift_table(levels)

    def load(odd):
        after_ref, before_ref = (far_ref, near_ref) if odd else (near_ref, far_ref)

        def group(i):
            places, planes = [], []
            for j in range(GROUP):
                for c in range(3):
                    x = i * GROUP + j
                    pieces = [winds_ref[c, x], after_ref[c, x], before_ref[c, x]]
                    planes.append(jnp.concatenate([piece.astype(F32) for piece in pieces], axis=0))
                    places.append((c, x + HALO))
            store_planes(places, planes, table[...], wind, above, below)

        each(0, cells_x // GROUP, group)

    by_parity(place_ref[0] // lax.axis_size("px") % 2, load)
    first, last = HALO, HALO + cells_x
    each(first + 1, last - 1, lambda x: visc_plane(x, wind, above, below, visc), unroll=2)
    each(first + 2, last - 2, lambda x: wind_plane(x, wind, above, below, visc, east, part), unroll=2)
    fetch.wait()
    half_modes(EARLY, source, east, part, basis_ref, modes, 0)


def side_kernel(side, planes_ref, corner_ref, table, *refs):
    if side:
        wind, above, below, visc, east, part, modes, source = refs[8:]
        basis_ref = refs[0]
    else:
        wind, above, below, visc, east, part = refs[6:]
    levels = wind.shape[3]
    cells_x = wind.shape[1] - 2 * HALO
    row = lax.broadcasted_iota(jnp.int32, (8, levels), 0)

    places, planes = [], []
    for c in range(3):
        nearest = corner_ref[c].astype(F32)
        second = jnp.where(row < 4, pltpu.roll(nearest, 6, 0), pltpu.roll(nearest, 2, 0))
        for i, rest in enumerate((nearest, second, jnp.zeros_like(nearest))):
            index = i if side else HALO - 1 - i
            planes.append(jnp.concatenate([planes_ref[c, index].astype(F32), rest], axis=0))
            places.append((c, index + (HALO + cells_x if side else 0)))
    store_planes(places, planes, table[...], wind, above, below)
    skip = cells_x + 1 if side else 0
    each(1 + skip, 4 + skip, lambda x: visc_plane(x, wind, above, below, visc), unroll=3)
    first = cells_x + 1 if side else HALO
    each(first, first + 2, lambda x: wind_plane(x, wind, above, below, visc, east, part), unroll=2)
    wind_plane(HALO + cells_x if side else 2, wind, above, below, visc, east, None)
    if side:
        half_modes(cells_x - EARLY, source, east, part, basis_ref, modes, 1)


def pack_kernel(place_ref, *refs):
    winds = refs[:3]
    winds_ref, inner_ref, outer_ref, down_ref, up_ref, sems = refs[3:]
    cells_x, cells_y, levels = winds[0].shape
    copies = [
        pltpu.make_async_copy(ref, winds_ref.at[c], sems.at[c]) for c, ref in enumerate(winds)
    ]
    for copy in copies:
        copy.start()
    for copy in copies:
        copy.wait()

    def pack(odd):
        leading_ref, last_ref = (inner_ref, outer_ref) if odd else (outer_ref, inner_ref)
        for c in range(3):
            for x in range(cells_x):
                own = winds_ref[c, x]
                leading_ref[c, x] = own[:ROWS]
                last_ref[c, x] = own[cells_y - ROWS :]

    by_parity(place_ref[0] // lax.axis_size("px") % 2, pack)
    down_ref[...] = winds_ref[:, :HALO]
    up_ref[...] = winds_ref[:, cells_x - HALO :]


def pack_winds(winds, place):
    cells_x, cells_y, levels = winds[0].shape
    vmem = pl.BlockSpec(memory_space=pltpu.VMEM)
    edge = pltpu.VMEM((3, cells_x, ROWS, levels), BF16)
    side = pltpu.VMEM((3, HALO, cells_y, levels), BF16)
    return pl.pallas_call(
        pack_kernel,
        out_shape=[pltpu.VMEM((3, cells_x, cells_y, levels), BF16), edge, edge, side, side],
        in_specs=[pl.BlockSpec(memory_space=pltpu.SMEM)] + [pl.BlockSpec(memory_space=pl.ANY)] * 3,
        out_specs=[vmem] * 5,
        scratch_shapes=[pltpu.SemaphoreType.DMA((3,))],
        compiler_params=KERNEL_VMEM,
        name="pack_winds",
    )(place, *[pltpu.with_memory_space_constraint(wind, pltpu.HBM) for wind in winds])


def source_modes(winds, place, basis_rows):
    cells_x, cells_y, levels = winds[0].shape
    planes = cells_x + 2 * HALO
    rows = cells_y + 2 * ROWS
    odd_north = place // lax.axis_size("px") % 2
    place = place.reshape(1)
    stacked, inner_rows, outer_rows, leading, last = pack_winds(winds, place)
    inner, outer = swaps("py")
    up, down = ring("px")
    outer_got = lax.ppermute(outer_rows, "py", outer)
    inner_got = lax.ppermute(inner_rows, "py", inner)
    low = lax.ppermute(last, "px", up)
    high = lax.ppermute(leading, "px", down)

    def corner(first, second):
        near, far = [[v[:, x] for x in (first, second)] for v in (inner_got, outer_got)]
        after = [jnp.where(odd_north == 1, f, n) for n, f in zip(near, far)]
        before = [jnp.where(odd_north == 1, n, f) for n, f in zip(near, far)]
        none = jnp.zeros((3, 2, levels), BF16)
        pieces = [after[0][:, :2], after[1][:, :1], none, before[1][:, 3:], before[0][:, 2:]]
        return jnp.concatenate(pieces, axis=1)

    low_corner = lax.ppermute(corner(cells_x - 1, cells_x - 2), "px", up)
    high_corner = lax.ppermute(corner(0, 1), "px", down)
    vmem = pl.BlockSpec(memory_space=pltpu.VMEM)
    smem = pl.BlockSpec(memory_space=pltpu.SMEM)
    shapes = [pltpu.VMEM((3, planes, rows, levels), F32)] * 3
    shapes += [pltpu.VMEM((planes, rows, levels), F32)]
    shapes += [pltpu.VMEM((planes, cells_y, levels), F32)] * 2
    shapes += [pltpu.VMEM((levels, cells_x * cells_y), F32)]
    scratch = [pltpu.VMEM((cells_x // 2, cells_y, levels), F32)]
    basis = table_parts(basis_rows * np.float32(0.0625), 1, DCT_PARTS)
    state = pl.pallas_call(
        inner_kernel,
        out_shape=shapes + [pltpu.VMEM(basis.shape, BF16), pltpu.VMEM((levels, 2 * levels), BF16)],
        in_specs=[smem] + [vmem] * 3 + [pl.BlockSpec(memory_space=pl.ANY)],
        out_specs=[vmem] * 9,
        scratch_shapes=scratch + [pltpu.SemaphoreType.DMA],
        cost_estimate=pl.CostEstimate(flops=40_000_000, bytes_accessed=6_000_000, transcendentals=0),
        compiler_params=KERNEL_VMEM,
        name="inner_planes",
    )(
        place,
        *[on_chip(got) for got in (stacked, inner_got, outer_got)],
        pltpu.with_memory_space_constraint(basis, pltpu.HBM),
    )
    low_state = pl.pallas_call(
        functools.partial(side_kernel, 0),
        out_shape=shapes[:6],
        in_specs=[vmem] * 9,
        out_specs=[vmem] * 6,
        input_output_aliases={3 + i: i for i in range(6)},
        cost_estimate=pl.CostEstimate(flops=8_000_000, bytes_accessed=2_000_000, transcendentals=0),
        compiler_params=KERNEL_VMEM,
        name="low_planes",
    )(*[on_chip(got) for got in (low, low_corner, state[8], *state[:6])])
    results = pl.pallas_call(
        functools.partial(side_kernel, 1),
        out_shape=shapes,
        in_specs=[vmem] * 11,
        out_specs=[vmem] * 7,
        input_output_aliases={4 + i: i for i in range(7)},
        scratch_shapes=scratch,
        compiler_params=KERNEL_VMEM,
        name="high_planes",
    )(*[on_chip(got) for got in (high, high_corner, state[8], state[7], *low_state, state[6])])
    return results[6]


def block_transpose(values, width):
    count = len(values)
    values = list(values)
    lane = lax.broadcasted_iota(jnp.int32, values[0].shape, 1) // width
    step = 1
    while step < count:
        odd = (lane & step) != 0
        for i in range(count):
            if i & step:
                continue
            low, high = values[i], values[i + step]
            shift = width * step
            values[i] = jnp.where(odd, pltpu.roll(high, shift, 1), low)
            values[i + step] = jnp.where(odd, high, pltpu.roll(low, low.shape[1] - shift, 1))
        step *= 2
    return values


def solve_kernel(
    east_count, north_count, cells_x, cells_y,
    in_ref, qx_ref, qxt_ref, qy_ref, qyt_ref, ex_ref, ey_ref, em_ref, place_ref, out_ref, work,
):
    total_x = east_count * cells_x
    total_y = north_count * cells_y
    block = in_ref.shape[1]
    groups = cells_x // north_count
    chunk = total_x * block // CHUNKS
    for h in range(CHUNKS):
        pieces = []
        for a in range(h * east_count // CHUNKS, (h + 1) * east_count // CHUNKS):
            for g in range(groups):
                lanes = slice(g * total_y, (g + 1) * total_y)
                got = [in_ref[b * east_count + a, :, lanes] for b in range(north_count)]
                pieces += block_transpose(got, cells_y)
        lines = value_parts(jnp.concatenate(pieces, axis=0), 1, NORTH_PARTS)
        work[h * chunk : (h + 1) * chunk, :] = dot(lines, qy_ref[...], ((1,), (0,)))
    planes = [work[pl.ds(i, total_x, stride=block), :] for i in range(block)]
    waves = dot(qxt_ref[...], value_parts(jnp.concatenate(planes, axis=1), 0, EAST_PARTS), ((1,), (0,)))
    eigen = ex_ref[...] + ey_ref[0:1, :]
    first = place_ref[0] * block
    solved = []
    for i in range(block):
        value = eigen + em_ref[first + i]
        empty = value == 0.0
        factor = jnp.where(empty, 0.0, -1.0 / jnp.where(empty, 1.0, value))
        solved.append(waves[:, i * total_y : (i + 1) * total_y] * factor)
    back = dot(qx_ref[...], value_parts(jnp.concatenate(solved, axis=1), 0, INVERSE), ((1,), (0,)))
    for i in range(block):
        work[pl.ds(i, total_x, stride=block), :] = back[:, i * total_y : (i + 1) * total_y]
    for h in range(CHUNKS):
        lines = value_parts(work[h * chunk : (h + 1) * chunk, :], 1, INVERSE)
        lines = dot(lines, qyt_ref[...], ((1,), (0,)))
        row = 0
        for a in range(h * east_count // CHUNKS, (h + 1) * east_count // CHUNKS):
            for g in range(groups):
                lanes = slice(g * total_y, (g + 1) * total_y)
                pieces = [lines[row + i * block : row + (i + 1) * block] for i in range(north_count)]
                row += north_count * block
                for b, piece in enumerate(block_transpose(pieces, cells_y)):
                    out_ref[b * east_count + a, :, lanes] = piece


def solve_planes(blocks, place, east_count, north_count, cells_x, cells_y, levels):
    total_x = east_count * cells_x
    total_y = north_count * cells_y
    qx, ex = fourier_basis(total_x)
    qy, ey = fourier_basis(total_y)
    qx = np.roll(qx.reshape(east_count, cells_x, total_x), -EARLY, axis=1).reshape(total_x, total_x)
    tables = [
        table_parts(qx, 1, INVERSE),
        table_parts(qx.T, 1, EAST_PARTS),
        table_parts(qy, 0, NORTH_PARTS),
        table_parts(qy.T, 0, INVERSE),
    ]
    tables += [
        np.ascontiguousarray(np.broadcast_to(ex[:, None], (total_x, total_y))),
        np.ascontiguousarray(np.broadcast_to(ey[None, :], (8, total_y))),
    ]
    vmem = pl.BlockSpec(memory_space=pltpu.VMEM)
    smem = pl.BlockSpec(memory_space=pltpu.SMEM)
    return pl.pallas_call(
        functools.partial(solve_kernel, east_count, north_count, cells_x, cells_y),
        out_shape=pltpu.VMEM(blocks.shape, F32),
        in_specs=[vmem] * 7 + [smem] * 2,
        out_specs=vmem,
        scratch_shapes=[pltpu.VMEM((total_x * blocks.shape[1], total_y), F32)],
        compiler_params=pltpu.CompilerParams(vmem_limit_bytes=24 * 2**20),
        name="solve_planes",
    )(on_chip(blocks), *[on_chip(table) for table in tables], mode_eigen(levels), place.reshape(1))


def pressure_kernel(shift, modes_ref, basis_ref, out_ref, cells, sems):
    total = cells.shape[0]
    half = total // 2
    copies = []

    def send(first, count):
        target = out_ref.at[pl.ds((first + shift) % total, count)]
        copy = pltpu.make_async_copy(cells.at[pl.ds(first, count)], target, sems.at[len(copies)])
        copy.start()
        copies.append(copy)

    for first in (0, half):
        part = value_parts(modes_ref[:, first : first + half], 0, INVERSE)
        cells[first : first + half, :] = dot(part, basis_ref[...], ((0,), (0,)))
        if first:
            send(first, half - shift)
            send(total - shift, shift)
        else:
            send(first, half)
    for copy in copies:
        copy.wait()


def pressure_cells(modes, basis_rows, shift):
    shape = (modes.shape[1], basis_rows.shape[1])
    return pl.pallas_call(
        functools.partial(pressure_kernel, shift),
        out_shape=jax.ShapeDtypeStruct(shape, F32),
        in_specs=[pl.BlockSpec(memory_space=pltpu.VMEM)] * 2,
        out_specs=pl.BlockSpec(memory_space=pl.ANY),
        scratch_shapes=[pltpu.VMEM(shape, F32), pltpu.SemaphoreType.DMA((3,))],
        compiler_params=KERNEL_VMEM,
        name="pressure_cells",
    )(on_chip(modes), on_chip(table_parts(basis_rows, 0, INVERSE)))


def rotation(row_count, col_count, length, direction):
    product = (
        lax.broadcasted_iota(jnp.int32, (row_count, col_count), 0)
        * lax.broadcasted_iota(jnp.int32, (row_count, col_count), 1)
        % length
    )
    radians = 2.0 * math.pi / length * product.astype(jnp.float32)
    return (jnp.cos(radians), direction * jnp.sin(radians))


def matmul(table, operand):
    return jnp.dot(
        table, operand, precision=lax.Precision.HIGHEST, preferred_element_type=jnp.float32
    )


def contract(formula, table, operand):
    return jnp.einsum(
        formula, table, operand, precision=lax.Precision.HIGHEST, preferred_element_type=jnp.float32
    )


def transform_rows(real_part, imag_part, direction):
    length = real_part.shape[0]
    width = real_part.shape[1]
    factor_low = 1
    for candidate in range(1, math.isqrt(length) + 1):
        if length % candidate == 0:
            factor_low = candidate
    factor_high = length // factor_low
    cos_high, sin_high = rotation(factor_high, factor_high, factor_high, direction)
    grid_real = real_part.reshape(factor_high, factor_low * width)
    grid_imag = imag_part.reshape(factor_high, factor_low * width)
    section_real = (matmul(cos_high, grid_real) - matmul(sin_high, grid_imag)).reshape(
        factor_high, factor_low, width
    )
    section_imag = (matmul(cos_high, grid_imag) + matmul(sin_high, grid_real)).reshape(
        factor_high, factor_low, width
    )
    turn_cos, turn_sin = rotation(factor_high, factor_low, length, direction)
    turn_cos = turn_cos[:, :, None]
    turn_sin = turn_sin[:, :, None]
    turned_real = section_real * turn_cos - section_imag * turn_sin
    turned_imag = section_real * turn_sin + section_imag * turn_cos
    cos_low, sin_low = rotation(factor_low, factor_low, factor_low, direction)
    out_real = contract("ca,kar->ckr", cos_low, turned_real) - contract(
        "ca,kar->ckr", sin_low, turned_imag
    )
    out_imag = contract("ca,kar->ckr", cos_low, turned_imag) + contract(
        "ca,kar->ckr", sin_low, turned_real
    )
    return (out_real.reshape(length, width), out_imag.reshape(length, width))


def first_forward(flat, high_count, second_cells, level_count):
    total = flat.shape[0]
    width = flat.shape[1]
    low_length = total // high_count
    grid = flat.reshape(low_length, high_count * width)
    cos_low, sin_low = rotation(low_length, low_length, low_length, -1.0)
    section_real = matmul(cos_low, grid).reshape(low_length, high_count, second_cells, level_count)
    section_imag = matmul(sin_low, grid).reshape(low_length, high_count, second_cells, level_count)
    turn_cos, turn_sin = rotation(low_length, high_count, total, -1.0)
    turn_cos = turn_cos[:, :, None, None]
    turn_sin = turn_sin[:, :, None, None]
    turned_real = section_real * turn_cos - section_imag * turn_sin
    turned_imag = section_real * turn_sin + section_imag * turn_cos
    cos_high, sin_high = rotation(high_count, high_count, high_count, -1.0)
    out_real = contract("ca,kaym->cykm", cos_high, turned_real) - contract(
        "ca,kaym->cykm", sin_high, turned_imag
    )
    out_imag = contract("ca,kaym->cykm", cos_high, turned_imag) + contract(
        "ca,kaym->cykm", sin_high, turned_real
    )
    merged = low_length * level_count
    return (
        out_real.reshape(high_count, second_cells, merged),
        out_imag.reshape(high_count, second_cells, merged),
    )


def first_inverse(real_part, imag_part, level_count):
    high_count = real_part.shape[0]
    second_cells = real_part.shape[1]
    low_length = real_part.shape[2] // level_count
    total = high_count * low_length
    data_real = real_part.reshape(high_count, second_cells, low_length, level_count)
    data_imag = imag_part.reshape(high_count, second_cells, low_length, level_count)
    cos_high, sin_high = rotation(high_count, high_count, high_count, 1.0)
    section_real = contract("ac,cykm->kaym", cos_high, data_real) - contract(
        "ac,cykm->kaym", sin_high, data_imag
    )
    section_imag = contract("ac,cykm->kaym", cos_high, data_imag) + contract(
        "ac,cykm->kaym", sin_high, data_real
    )
    turn_cos, turn_sin = rotation(low_length, high_count, total, 1.0)
    turn_cos = turn_cos[:, :, None, None]
    turn_sin = turn_sin[:, :, None, None]
    turned_real = section_real * turn_cos - section_imag * turn_sin
    turned_imag = section_real * turn_sin + section_imag * turn_cos
    cos_low, sin_low = rotation(low_length, low_length, low_length, 1.0)
    flat = matmul(cos_low, turned_real.reshape(low_length, -1)) - matmul(
        sin_low, turned_imag.reshape(low_length, -1)
    )
    return flat.reshape(total, second_cells * level_count)


def solve_modes(
    real_part, imag_part, first_rank, second_rank, first_total, second_total, levels, level_count
):
    low_length = real_part.shape[1] // level_count
    shape_full = (second_total, low_length, level_count)
    wave_second = lax.broadcasted_iota(jnp.int32, shape_full, 0)
    wave_first = second_rank * low_length + lax.broadcasted_iota(jnp.int32, shape_full, 1)
    mode_index = first_rank * level_count + lax.broadcasted_iota(jnp.int32, shape_full, 2)
    eigen = 4.0 * jnp.sin(math.pi / first_total * wave_first.astype(jnp.float32)) ** 2
    eigen = eigen + 4.0 * jnp.sin(math.pi / second_total * wave_second.astype(jnp.float32)) ** 2
    eigen = eigen + 4.0 * jnp.sin(math.pi / (2.0 * levels) * mode_index.astype(jnp.float32)) ** 2
    empty = (wave_first == 0) & (wave_second == 0) & (mode_index == 0)
    factor = jnp.where(empty, 0.0, -1.0 / jnp.where(empty, 1.0, eigen)) / (
        first_total * second_total
    )
    factor = factor.reshape(second_total, low_length * level_count)
    return (real_part * factor, imag_part * factor)


def fold_half(real_part, imag_part, level_count):
    high_count = real_part.shape[0]
    second_cells = real_part.shape[1]
    low_length = real_part.shape[2] // level_count
    half_high = high_count // 2
    half_low = low_length // 2
    nyquist = real_part[half_high, :, :level_count]

    def halve(values):
        kept = values[:half_high].reshape(half_high, second_cells, 2, half_low * level_count)
        return kept.transpose(0, 2, 1, 3).reshape(high_count, second_cells, half_low * level_count)

    kept_real = halve(real_part)
    kept_imag = halve(imag_part).at[0, :, :level_count].set(nyquist)
    return (kept_real, kept_imag)


def solve_half(
    real_part, imag_part, first_rank, second_rank, first_total, second_total, levels, level_count
):
    packed_real = real_part[:, :level_count]
    packed_imag = imag_part[:, :level_count]
    mirror_real = jnp.roll(packed_real[::-1], 1, axis=0)
    mirror_imag = jnp.roll(packed_imag[::-1], 1, axis=0)
    zero_real = 0.5 * (packed_real + mirror_real)
    zero_imag = 0.5 * (packed_imag - mirror_imag)
    nyquist_real = 0.5 * (packed_imag + mirror_imag)
    nyquist_imag = -0.5 * (packed_real - mirror_real)
    first_block = second_rank == 0
    real_part = jnp.where(first_block, real_part.at[:, :level_count].set(zero_real), real_part)
    imag_part = jnp.where(first_block, imag_part.at[:, :level_count].set(zero_imag), imag_part)
    solved_real, solved_imag = solve_modes(
        real_part,
        imag_part,
        first_rank,
        second_rank,
        first_total,
        second_total,
        levels,
        level_count,
    )
    wave_second = lax.broadcasted_iota(jnp.int32, (second_total, level_count), 0)
    mode_index = first_rank * level_count + lax.broadcasted_iota(
        jnp.int32, (second_total, level_count), 1
    )
    eigen = 4.0 + 4.0 * jnp.sin(math.pi / second_total * wave_second.astype(jnp.float32)) ** 2
    eigen = eigen + 4.0 * jnp.sin(math.pi / (2.0 * levels) * mode_index.astype(jnp.float32)) ** 2
    nyquist_factor = -1.0 / eigen / (first_total * second_total)
    solved_nyquist_real = nyquist_real * nyquist_factor
    solved_nyquist_imag = nyquist_imag * nyquist_factor
    joined_real = solved_real[:, :level_count] - solved_nyquist_imag
    joined_imag = solved_imag[:, :level_count] + solved_nyquist_real
    solved_real = jnp.where(
        first_block, solved_real.at[:, :level_count].set(joined_real), solved_real
    )
    solved_imag = jnp.where(
        first_block, solved_imag.at[:, :level_count].set(joined_imag), solved_imag
    )
    return (solved_real, solved_imag)


def unfold_half(real_part, imag_part, level_count):
    high_count = real_part.shape[0]
    second_cells = real_part.shape[1]
    half_low = real_part.shape[2] // level_count
    half_high = high_count // 2
    low_length = 2 * half_low

    def unhalve(values):
        shaped = values.reshape(half_high, 2, second_cells, half_low * level_count)
        return shaped.transpose(0, 2, 1, 3).reshape(
            half_high, second_cells, low_length * level_count
        )

    lower_real = unhalve(real_part)
    lower_imag = unhalve(imag_part)
    zero_line = lower_real[0, :, :level_count]
    nyquist_line = lower_imag[0, :, :level_count]
    upper = jnp.zeros((high_count - half_high, second_cells, low_length * level_count), jnp.float32)
    full_real = jnp.concatenate([2.0 * lower_real, upper], axis=0)
    full_imag = jnp.concatenate([2.0 * lower_imag, upper], axis=0)
    full_real = (
        full_real.at[0, :, :level_count]
        .set(zero_line)
        .at[half_high, :, :level_count]
        .set(nyquist_line)
    )
    full_imag = full_imag.at[0, :, :level_count].set(0.0)
    return (full_real, full_imag)


def spectral(
    modes,
    first_rank,
    second_rank,
    second_count,
    levels,
    send_out,
    send_across,
    bring_back,
    bring_home,
):
    first_count = modes.shape[0]
    first_cells = modes.shape[1]
    merged = modes.shape[2]
    level_count = levels // first_count
    second_cells = merged // level_count
    first_total = first_count * first_cells
    second_total = second_count * second_cells
    pencil = send_out(modes).reshape(first_total, merged)
    line_real, line_imag = first_forward(pencil, second_count, second_cells, level_count)
    line_real, line_imag = fold_half(line_real, line_imag, level_count)
    across_real, across_imag = send_across(line_real, line_imag)
    across_real = across_real.reshape(second_total, -1)
    across_imag = across_imag.reshape(second_total, -1)
    wave_real, wave_imag = transform_rows(across_real, across_imag, -1.0)
    wave_real, wave_imag = solve_half(
        wave_real,
        wave_imag,
        first_rank,
        second_rank,
        first_total,
        second_total,
        levels,
        level_count,
    )
    back_real, back_imag = transform_rows(wave_real, wave_imag, 1.0)
    home_real, home_imag = bring_back(
        back_real.reshape(1, second_total, -1), back_imag.reshape(1, second_total, -1)
    )
    home_real, home_imag = unfold_half(home_real, home_imag, level_count)
    flat = first_inverse(home_real, home_imag, level_count)
    return bring_home(flat.reshape(1, first_total, merged))


def staged(modes, east_count, north_count, cells_x, cells_y):
    levels = modes.shape[0]
    level_count = levels // east_count

    def send_out(values):
        return lax.all_to_all(values, "px", split_axis=0, concat_axis=1, tiled=True)

    def send_across(real_part, imag_part):
        return (
            lax.all_to_all(real_part, "py", split_axis=0, concat_axis=1, tiled=True),
            lax.all_to_all(imag_part, "py", split_axis=0, concat_axis=1, tiled=True),
        )

    def bring_back(real_part, imag_part):
        return (
            lax.all_to_all(real_part, "py", split_axis=1, concat_axis=0, tiled=True),
            lax.all_to_all(imag_part, "py", split_axis=1, concat_axis=0, tiled=True),
        )

    def bring_home(values):
        return lax.all_to_all(values, "px", split_axis=1, concat_axis=0, tiled=True)

    shaped = modes.reshape(east_count, level_count, cells_x, cells_y).transpose(0, 2, 3, 1)
    shaped = jnp.roll(shaped, EARLY, axis=1)
    result = spectral(
        shaped.reshape(east_count, cells_x, cells_y * level_count),
        lax.axis_index("px"),
        lax.axis_index("py"),
        north_count,
        levels,
        send_out,
        send_across,
        bring_back,
        bring_home,
    )
    result = jnp.roll(result.reshape(east_count, cells_x, cells_y, level_count), -EARLY, axis=1)
    result = result.transpose(0, 3, 1, 2)
    return result.reshape(levels, cells_x * cells_y)


def shards(wind_east, wind_north, wind_up):
    cells_x, cells_y, levels = wind_east.shape
    east_count = lax.axis_size("px")
    north_count = lax.axis_size("py")
    devices = east_count * north_count
    basis_rows = np.ascontiguousarray(cosine_basis(levels).T)
    north_rank = lax.axis_index("py")
    place = north_rank * east_count + lax.axis_index("px")
    modes = source_modes((wind_east, wind_north, wind_up), place, basis_rows)
    if levels == 8 * devices and north_count * cells_y == 128 and cells_x % north_count == 0:
        blocks = modes.reshape(devices, levels // devices, cells_x * cells_y)
        blocks = lax.all_to_all(blocks, ("py", "px"), split_axis=0, concat_axis=0, tiled=True)
        blocks = solve_planes(blocks, place, east_count, north_count, cells_x, cells_y, levels)
        blocks = lax.all_to_all(blocks, ("py", "px"), split_axis=0, concat_axis=0, tiled=True)
        modes = blocks.reshape(levels, cells_x * cells_y)
    else:
        modes = staged(modes, east_count, north_count, cells_x, cells_y)
    return pressure_cells(modes, basis_rows, EARLY * cells_y).reshape(cells_x, cells_y, levels)


def solution(mesh):
    return jax.shard_map(
        shards,
        mesh=mesh,
        in_specs=(P("px", "py", None), P("px", "py", None), P("px", "py", None)),
        out_specs=P("px", "py", None),
        check_vma=False,
    )
```
